512 devices in a mesh: rve: 32 (over z, core), slab: 16 (over y, x).
Axes of the slice: x: 4, y: 4, z: 16, core: 2. Of those that a mesh axis runs over, the one named last changes fastest.
Arguments:
- phase_ids: int32 [64, 4096], P('slab'), may hold values from 0 to 1, as said below
- yield_flags: int32 [32, 3, 64, 4096], P('rve', None, 'slab'), may hold values from 0 to 1
- plastic_strain: float32 [32, 6, 64, 4096], P('rve', None, 'slab'), may hold values from -0.03 to 0.03
- displacements: float32 [20, 3], replicated, may hold values from -0.06 to 0.06
- connectivity: int32 [4, 8], replicated, may hold values from 0 to 19, as said below
Outputs:
- gauss_stress: float32 [32, 6], P('rve')
- gauss_tangent: float32 [32, 6, 6], P('rve')
- nodal_forces: float32 [20, 3], replicated
- stiffness: float32 [60, 60], replicated
The draws below stay inside these ranges and needn't reach their ends.
Inputs may be any that keep to these rules, and one draw needn't show every extreme that they name: `phase_ids`: 0 marks ferrite, 1 martensite. `connectivity`: element e is the cube [e, e+1] x [0,1] x [0,1]; entry c of its row is the id of its corner (e + c % 2, c // 2 % 2, c // 4); each point of the mesh has one id, distinct points distinct ids.
All inputs are finite; a program needn't handle non-finite values.
Results may differ from the reference program's by a relative error of at most 0.0001.
Values sent between devices are 32-bit elements; how exact they have to be, the bound alone decides.
No kernel may reach another device: no remote copies, remote signals or barrier semaphores. Data moves between devices by JAX's collectives and lax.ppermute only.
A program may use at most 64 MiB of HBM per device.

```python
import math
import jax
import jax.numpy as jnp
import numpy as np
from jax import lax

GRID = 64
ITERS = 2
POINTS = 32
ELEMENTS = 4
NODES = 20


def phase_field(key):
    start_share = jax.random.randint(jax.random.fold_in(key, 11), (), 0, 500)
    finish_share = jax.random.randint(jax.random.fold_in(key, 13), (), 500, 1000)
    planes = lax.broadcasted_iota(jnp.int32, (GRID, GRID * GRID), 0)
    yield_limit = start_share + (finish_share - start_share) * planes // (GRID - 1)
    scores = jax.random.randint(jax.random.fold_in(key, 17), (GRID, GRID * GRID), 0, 1000)
    return (scores < yield_limit).astype(jnp.int32)


def draw_phase_ids(key, part):
    return phase_field(key)


def draw_yield_flags(key, part):
    phases = phase_field(key)
    soft_share = jax.random.randint(jax.random.fold_in(key, 31), (POINTS, ITERS + 1, 1, 1), 400, 1000)
    hard_share = jax.random.randint(jax.random.fold_in(key, 37), (POINTS, ITERS + 1, 1, 1), 0, 400)
    scores = jax.random.randint(jax.random.fold_in(key, 43), (POINTS, ITERS + 1, GRID, GRID * GRID), 0, 1000)
    yield_limit = jnp.where(phases[None, None] == 1, hard_share, soft_share)
    return (scores < yield_limit).astype(jnp.int32)


def draw_plastic_strain(key, part):
    offsets = jnp.clip(0.005 * jax.random.normal(jax.random.fold_in(key, 53), (POINTS, 6, 1, 1), jnp.float32), -0.015, 0.015)
    rough_part = jnp.clip(0.003 * jax.random.normal(jax.random.fold_in(key, 61), (POINTS, 6, GRID, GRID * GRID), jnp.float32), -0.012, 0.012)
    return (offsets + rough_part).astype(jnp.float32)


def draw_connectivity(key, part):
    ordering = jax.random.permutation(jax.random.fold_in(key, 71), NODES).astype(jnp.int32)
    element_index = lax.broadcasted_iota(jnp.int32, (ELEMENTS, 8), 0)
    corner_index = lax.broadcasted_iota(jnp.int32, (ELEMENTS, 8), 1)
    structured = (element_index + corner_index % 2) * 4 + corner_index // 2 % 2 * 2 + corner_index // 4
    return ordering[structured].astype(jnp.int32)


def noise(stream_key, dims, spread, limit, kind=jnp.bfloat16):
    values = jax.random.normal(stream_key, dims, jnp.float32) * spread
    return jnp.minimum(jnp.maximum(values, -limit), limit).astype(kind)


def setup_inputs(seed: int = 0) -> dict:
    keys = jax.random.split(jax.random.key(seed), 6)
    return {
        "phase_ids": draw_phase_ids(jax.random.fold_in(keys[5], 71), 0),
        "yield_flags": draw_yield_flags(jax.random.fold_in(keys[5], 71), 0),
        "plastic_strain": draw_plastic_strain(jax.random.fold_in(keys[5], 71), 0),
        "displacements": noise(keys[3], (NODES, 3), 0.01, 0.06, jnp.float32),
        "connectivity": draw_connectivity(jax.random.fold_in(keys[5], 71), 0),
    }


SHEAR_MODULUS = 80.0
BULK_MODULUS = 160.0
REFERENCE_SHEAR = 80.0
REFERENCE_LAME = 160.0 - 160.0 / 3.0
TANGENT_UNIT = 100.0
QUADRATURE_WEIGHT = 0.125
DIAGONAL_PART = (1.0, 1.0, 1.0, 0.0, 0.0, 0.0)
PAIR_WEIGHTS = (1.0, 1.0, 1.0, 2.0, 2.0, 2.0)
TENSOR_PAIRS = ((0, 0), (1, 1), (2, 2), (1, 2), (0, 2), (0, 1))
TENSOR_ROWS = ((0, 5, 4), (5, 1, 3), (4, 3, 2))

def gradient_table():
    inverse_root = 1.0 / math.sqrt(3.0)
    table_rows = np.zeros((8, 6, 24))
    for gauss_corner in range(8):
        position = [0.5 + (2 * (gauss_corner >> axis_number & 1) - 1) * 0.5 * inverse_root for axis_number in range(3)]
        for corner in range(8):
            corner_bits = [corner >> axis_number & 1 for axis_number in range(3)]
            factors = [position[axis_number] * corner_bits[axis_number] + (1.0 - position[axis_number]) * (1 - corner_bits[axis_number]) for axis_number in range(3)]
            slopes = []
            for axis_number in range(3):
                slope_value = 2.0 * corner_bits[axis_number] - 1.0
                for other_axis in range(3):
                    if other_axis != axis_number:
                        slope_value = slope_value * factors[other_axis]
                slopes.append(slope_value)
            column = 3 * corner
            table_rows[gauss_corner, 0, column] += slopes[0]
            table_rows[gauss_corner, 1, column + 1] += slopes[1]
            table_rows[gauss_corner, 2, column + 2] += slopes[2]
            table_rows[gauss_corner, 3, column + 1] += 0.5 * slopes[2]
            table_rows[gauss_corner, 3, column + 2] += 0.5 * slopes[1]
            table_rows[gauss_corner, 4, column] += 0.5 * slopes[2]
            table_rows[gauss_corner, 4, column + 2] += 0.5 * slopes[0]
            table_rows[gauss_corner, 5, column] += 0.5 * slopes[1]
            table_rows[gauss_corner, 5, column + 1] += 0.5 * slopes[0]
    return table_rows

def point_geometry(points, connectivity, corner_lookup, node_count):
    element_count = connectivity.shape[0]
    point_count = points.shape[0]
    corner_selector = (points[:, None] % 8 == jnp.arange(8, dtype=jnp.int32)[None, :]).astype(jnp.float32)
    strain_row_values = jnp.einsum('zu,utf->ztf', corner_selector, corner_lookup, precision=lax.Precision.HIGHEST)
    element_onehot = points[:, None] // 8 == jnp.arange(element_count, dtype=jnp.int32)[None, :]
    corner_nodes = lax.optimization_barrier(jnp.sum(jnp.where(element_onehot[:, :, None], connectivity[None, :, :], 0), axis=1)).astype(jnp.int32)
    degrees = 3 * corner_nodes[:, :, None] + jnp.arange(3, dtype=jnp.int32)[None, None, :]
    degrees = degrees.reshape(point_count, 24)
    placing = (degrees[:, :, None] == jnp.arange(3 * node_count, dtype=jnp.int32)[None, None, :]).astype(jnp.float32)
    return (strain_row_values, placing)

def macro_strains(strain_row_values, placing, displacements):
    nodal_quantities = jnp.einsum('gpn,n->gp', placing, displacements.reshape(-1), precision=lax.Precision.HIGHEST)
    return jnp.einsum('vxw,vw->vx', strain_row_values, nodal_quantities, precision=lax.Precision.HIGHEST)

def material_response(strain, plastic, phase_ids, flag_values):
    diagonal = jnp.asarray(DIAGONAL_PART, jnp.float32)[:, None]
    weights = jnp.asarray(PAIR_WEIGHTS, jnp.float32)[:, None]
    martensite = phase_ids == 1
    yield_stress = jnp.where(martensite, 1.2, 0.3).astype(jnp.float32)
    hardening = jnp.where(martensite, 10.0, 2.0).astype(jnp.float32)
    elastic = strain - plastic
    volume = elastic[0] + elastic[1] + elastic[2]
    trial_dev = 2.0 * SHEAR_MODULUS * (elastic - diagonal * (volume / 3.0))
    equivalent = jnp.sqrt(1.5 * lax.optimization_barrier(jnp.sum(weights * trial_dev * trial_dev, axis=0)))
    bounded = jnp.maximum(equivalent, yield_stress)
    return_ratio = 3.0 * SHEAR_MODULUS / (3.0 * SHEAR_MODULUS + hardening)
    active = flag_values.astype(jnp.float32)
    plastic_flow = active * (equivalent - yield_stress) / bounded
    softening = 1.0 - return_ratio * plastic_flow
    stress = trial_dev * softening + diagonal * (BULK_MODULUS * volume)
    shear_term = 2.0 * SHEAR_MODULUS * softening
    tangent_weight = 3.0 * SHEAR_MODULUS * return_ratio * active * yield_stress / (bounded * bounded * bounded)
    return (stress, trial_dev, shear_term, tangent_weight)

def wave_terms(index_x, index_y, index_z):
    middle = GRID // 2
    signed = []
    for indices in (index_x, index_y, index_z):
        wrapped = jnp.where(indices < middle, indices, indices - GRID)
        signed.append(jnp.where(indices == middle, 0, wrapped))
    nyquist_free = (index_x != middle) & (index_y != middle) & (index_z != middle)
    length = signed[0] * signed[0] + signed[1] * signed[1] + signed[2] * signed[2]
    keep_mask = (nyquist_free & (length > 0)).astype(jnp.float32)
    inverse_length = 1.0 / jnp.sqrt(jnp.maximum(length, 1).astype(jnp.float32))
    normals = [signed_entry.astype(jnp.float32) * inverse_length for signed_entry in signed]
    return (normals, keep_mask)

def project_green(components, normals, keep_mask):
    traction = [components[tensor_row[0]] * normals[0] + components[tensor_row[1]] * normals[1] + components[tensor_row[2]] * normals[2] for tensor_row in TENSOR_ROWS]
    normal_load = normals[0] * traction[0] + normals[1] * traction[1] + normals[2] * traction[2]
    coupling = (REFERENCE_LAME + REFERENCE_SHEAR) / (REFERENCE_SHEAR * (REFERENCE_LAME + 2.0 * REFERENCE_SHEAR))
    result_list = []
    for left_axis, right_axis in TENSOR_PAIRS:
        entry_value = (normals[left_axis] * traction[right_axis] + normals[right_axis] * traction[left_axis]) / (2.0 * REFERENCE_SHEAR)
        entry_value = entry_value - coupling * normals[left_axis] * normals[right_axis] * normal_load
        result_list.append(entry_value * keep_mask)
    return jnp.stack(result_list)

def tangent_matrix(mean_shear, outer_sum):
    diagonal = jnp.asarray(DIAGONAL_PART, jnp.float32)
    volumetric = diagonal[:, None] * diagonal[None, :]
    weights = jnp.asarray(PAIR_WEIGHTS, jnp.float32)
    identity = jnp.eye(6, dtype=jnp.float32)
    whole = BULK_MODULUS * volumetric + mean_shear * (identity - volumetric / 3.0) - outer_sum * weights[None, :]
    return whole / TANGENT_UNIT

def assemble(stress_values, tangent_moduli, strain_row_values, placing):
    weights = jnp.asarray(PAIR_WEIGHTS, jnp.float32)
    force_row_values = strain_row_values * weights[None, :, None]
    element_force_vector = QUADRATURE_WEIGHT * jnp.einsum('mbh,mb->mh', force_row_values, stress_values, precision=lax.Precision.HIGHEST)
    element_stiffness_matrix = QUADRATURE_WEIGHT * jnp.einsum('xoh,xon,xnv->xhv', force_row_values, tangent_moduli, strain_row_values, precision=lax.Precision.HIGHEST)
    forces = jnp.einsum('gp,gpn->n', element_force_vector, placing, precision=lax.Precision.HIGHEST)
    stiffness = jnp.einsum('gpq,gpm,gqn->mn', element_stiffness_matrix, placing, placing, precision=lax.Precision.HIGHEST)
    return (forces.reshape(-1, 3), stiffness)

def reference(phase_ids, yield_flags, plastic_strain, displacements, connectivity):
    corner_lookup = jnp.asarray(gradient_table(), jnp.float32)
    points = jnp.arange(POINTS, dtype=jnp.int32)
    strain_row_values, placing = point_geometry(points, connectivity, corner_lookup, displacements.shape[0])
    macro_all = macro_strains(strain_row_values, placing, displacements)
    index_x = lax.broadcasted_iota(jnp.int32, (GRID, 1, 1), 0)
    index_y = lax.broadcasted_iota(jnp.int32, (1, GRID, 1), 1)
    index_z = lax.broadcasted_iota(jnp.int32, (1, 1, GRID), 2)
    normals, keep_mask = wave_terms(index_x, index_y, index_z)
    phases = phase_ids.reshape(-1)
    voxel_count = float(GRID ** 3)

    def one_point(inputs):
        macro_strain, plastic_cell, point_flags = inputs
        plastic = plastic_cell.reshape(6, -1)
        strain = jnp.broadcast_to(macro_strain[:, None], plastic.shape)
        for iteration in range(ITERS):
            stress = material_response(strain, plastic, phases, point_flags[iteration].reshape(-1))[0]
            spectrum = jnp.fft.fftn(stress.reshape(6, GRID, GRID, GRID), axes=(1, 2, 3))
            corrected = project_green([spectrum[component] for component in range(6)], normals, keep_mask)
            strain = strain - jnp.real(jnp.fft.ifftn(corrected, axes=(1, 2, 3))).reshape(6, -1)
        stress, trial_dev, shear_term, tangent_weight = material_response(strain, plastic, phases, point_flags[ITERS].reshape(-1))
        mean_stress = lax.optimization_barrier(jnp.sum(stress, axis=1)) / voxel_count
        mean_shear = jnp.sum(shear_term) / voxel_count
        outer_sum = jnp.dot(trial_dev * tangent_weight[None, :], trial_dev.T, precision=lax.Precision.HIGHEST) / voxel_count
        return (mean_stress, tangent_matrix(mean_shear, outer_sum))
    stress_values, tangent_moduli = lax.map(one_point, (macro_all, plastic_strain, yield_flags))
    forces, stiffness = assemble(stress_values, tangent_moduli, strain_row_values, placing)
    return (stress_values, tangent_moduli, forces, stiffness)
```

```python
import functools
import math

import jax
import jax.numpy as jnp
import ml_dtypes
import numpy as np
from jax import lax
from jax.experimental import pallas as pl
from jax.experimental.pallas import tpu as pltpu
from jax.sharding import PartitionSpec as P

GRID = 64
ITERS = 2
SLABS = 16
PLANES = GRID // SLABS
KEPT = GRID // 2

SHEAR_MODULUS = 80.0
BULK_MODULUS = 160.0
REFERENCE_SHEAR = 80.0
REFERENCE_LAME = 160.0 - 160.0 / 3.0
TANGENT_UNIT = 100.0
QUADRATURE_WEIGHT = 0.125
PAIR_WEIGHTS = (1.0, 1.0, 1.0, 2.0, 2.0, 2.0)
TENSOR_PAIRS = ((0, 0), (1, 1), (2, 2), (1, 2), (0, 2), (0, 1))
TENSOR_ROWS = ((0, 5, 4), (5, 1, 3), (4, 3, 2))
VOXELS = float(GRID**3)
GAUSS_LOW = 0.5 - 0.5 / math.sqrt(3.0)
GAUSS_HIGH = 0.5 + 0.5 / math.sqrt(3.0)
OUTER_AT = 8


def halves(table):
    high = table.astype(np.float32).astype(ml_dtypes.bfloat16)
    low = (table - high.astype(np.float64)).astype(np.float32).astype(ml_dtypes.bfloat16)
    return high, low


def depth_tables():
    z = np.arange(GRID)
    k = np.arange(KEPT)
    theta = 2.0 * np.pi * np.outer(z, k) / GRID
    forward = np.stack([np.cos(theta), -np.sin(theta)], axis=0)
    weight = np.where(k == 0, 1.0, 2.0) / VOXELS
    inverse = forward * weight[None, None, :]
    planes = np.eye(PLANES)
    pair = np.eye(2)
    there = np.einsum("lL,rR,pzk->lrzRpLk", planes, pair, forward)
    back = np.einsum("lL,rR,pzk->RpLklrz", planes, pair, inverse)
    return there.reshape(512, 512), back.reshape(512, 512)


def row_tables():
    y = 2 * np.arange(32)[None, :] + np.arange(2)[:, None]
    ky = 4 * np.arange(16)[:, None] + np.arange(4)[None, :]
    theta = 2.0 * np.pi * np.einsum("de,rm->derm", ky, y) / GRID
    c, s = np.cos(theta), np.sin(theta)
    there = np.zeros((16, 2, 4, 2, 2, 32))
    there[:, 0, :, :, 0, :] = c
    there[:, 0, :, :, 1, :] = s
    there[:, 1, :, :, 0, :] = -s
    there[:, 1, :, :, 1, :] = c
    back = np.zeros((2, 2, 32, 16, 2, 4))
    ct, st = np.einsum("derm->rmde", c), np.einsum("derm->rmde", s)
    back[:, 0, :, :, 0, :] = ct
    back[:, 0, :, :, 1, :] = -st
    back[:, 1, :, :, 0, :] = st
    back[:, 1, :, :, 1, :] = ct
    return there.reshape(128, 128), back.reshape(128, 128)


def column_tables():
    d = np.arange(16)
    theta = 2.0 * np.pi * np.outer(d, d) / 16.0
    c, s = np.cos(theta), np.sin(theta)
    same = np.eye(4)
    there = np.zeros((2, 16, 4, 16, 2, 4))
    there[0, :, :, :, 0, :] = np.einsum("bd,ef->bedf", c, same)
    there[0, :, :, :, 1, :] = np.einsum("bd,ef->bedf", s, same)
    there[1, :, :, :, 0, :] = np.einsum("bd,ef->bedf", -s, same)
    there[1, :, :, :, 1, :] = np.einsum("bd,ef->bedf", c, same)
    there = there.reshape(128, 128)
    phi = 2.0 * np.pi * np.outer(np.arange(16), np.arange(4)) / GRID
    twist = np.stack([np.cos(phi), np.sin(phi)])[:, :, None, :, None]
    twist = np.broadcast_to(twist, (2, 16, 4, 4, KEPT)).reshape(2, 64, 128)
    quarter = 2.0 * np.pi * np.outer(np.arange(4), np.arange(4)) / 4.0
    cq, sq = np.rint(np.cos(quarter)), np.rint(np.sin(quarter))
    kept = np.eye(KEPT)
    four = np.zeros((2, 4, KEPT, 2, 4, KEPT))
    four[0, :, :, 0] = np.einsum("la,kK->lkaK", cq, kept)
    four[1, :, :, 0] = np.einsum("la,kK->lkaK", sq, kept)
    four[0, :, :, 1] = np.einsum("la,kK->lkaK", -sq, kept)
    four[1, :, :, 1] = np.einsum("la,kK->lkaK", cq, kept)
    four = four.reshape(256, 256)
    return there, there.T.copy(), twist.astype(np.float32), four, four.T.copy()


def split(x):
    high = x.astype(jnp.bfloat16)
    low = (x - high.astype(jnp.float32)).astype(jnp.bfloat16)
    return high, low


def mm(a, b):
    return jnp.dot(a, b, preferred_element_type=jnp.float32)


def data_by_table(high, low, table_high, table_low):
    return mm(high, table_high) + (mm(low, table_high) + mm(high, table_low))


def table_by_data(table_high, table_low, high, low):
    return mm(table_high, high) + (mm(table_low, high) + mm(table_high, low))


def slopes_of(bits, low, high):
    at = [jnp.where(bit == 1, high, low) for bit in bits]
    far = [jnp.where(bit == 1, low, high) for bit in bits]

    def slope(corner, axis):
        value = None
        for other in range(3):
            if other != axis:
                factor = at[other] if corner >> other & 1 else far[other]
                value = factor if value is None else value * factor
        return value if corner >> axis & 1 else -value

    return slope


def macro_strain(point, conn_ref, disp_ref):
    low, high = jnp.float32(GAUSS_LOW), jnp.float32(GAUSS_HIGH)
    bits = [lax.bitwise_and(lax.shift_right_logical(point, d), 1) for d in range(3)]
    slope = slopes_of(bits, low, high)
    element = lax.shift_right_logical(point, 3)
    grad = [[jnp.float32(0.0)] * 3 for _ in range(3)]
    for corner in range(8):
        node = conn_ref[element, corner]
        for k in range(3):
            u = disp_ref[node, k]
            for d in range(3):
                grad[k][d] = grad[k][d] + slope(corner, d) * u
    strain = []
    for i, j in TENSOR_PAIRS:
        strain.append(grad[i][i] if i == j else 0.5 * (grad[i][j] + grad[j][i]))
    return strain


def material(elastic, phases, flags):
    hard = phases == 1
    limit = jnp.where(hard, 1.2, 0.3)
    ratio = jnp.where(
        hard,
        3.0 * SHEAR_MODULUS / (3.0 * SHEAR_MODULUS + 10.0),
        3.0 * SHEAR_MODULUS / (3.0 * SHEAR_MODULUS + 2.0),
    )
    active = flags.astype(jnp.float32)
    volume = elastic[0] + elastic[1] + elastic[2]
    third = volume * (1.0 / 3.0)
    trial = [2.0 * SHEAR_MODULUS * (elastic[a] - third) for a in range(3)]
    trial += [2.0 * SHEAR_MODULUS * elastic[a] for a in range(3, 6)]
    normal = trial[0] * trial[0] + trial[1] * trial[1] + trial[2] * trial[2]
    shear = trial[3] * trial[3] + trial[4] * trial[4] + trial[5] * trial[5]
    equivalent = jnp.sqrt(1.5 * (normal + 2.0 * shear))
    bounded = jnp.maximum(equivalent, limit)
    inverse = 1.0 / bounded
    scaled = ratio * active
    softening = 1.0 - scaled * (equivalent - limit) * inverse
    pressure = BULK_MODULUS * volume
    stress = [trial[a] * softening + pressure for a in range(3)]
    stress += [trial[a] * softening for a in range(3, 6)]
    weight = 3.0 * SHEAR_MODULUS * scaled * limit * (inverse * inverse * inverse)
    return stress, trial, softening, weight


def every_fourth(ref, start, plane):
    return ref[pl.ds(start + plane, 32, stride=4), :]


def put_split(high_ref, low_ref, rows, cols, value):
    high, low = split(value)
    high_ref[rows, cols] = high
    low_ref[rows, cols] = low


def forward_planes(xh, xl, bh, bl, wh, wl, th, tl, out_ref):
    turned = data_by_table(xh[...], xl[...], wh[...], wl[...])
    for c in range(6):
        for s in range(4):
            block = turned[c * 32 : (c + 1) * 32, s * 128 : (s + 1) * 128]
            put_split(bh, bl, pl.ds(s * 32, 32), pl.ds(c * 128, 128), block)
    spectrum = table_by_data(th[...], tl[...], bh[...], bl[...])
    for c in range(6):
        out_ref[:, c * 8 : (c + 1) * 8, :] = spectrum[:, c * 128 : (c + 1) * 128].reshape(
            16, 8, 128
        )


def load_columns(in_ref, bh, bl):
    for c in range(6):
        block = in_ref[:, c * 8 : (c + 1) * 8, :].reshape(128, 128)
        put_split(bh, bl, slice(None), pl.ds(c * 128, 128), block)


def backward_planes(in_ref, xh, xl, bh, bl, wh, wl, th, tl):
    load_columns(in_ref, bh, bl)
    rows = table_by_data(th[...], tl[...], bh[...], bl[...])
    for c in range(6):
        for s in range(4):
            block = rows[s * 32 : (s + 1) * 32, c * 128 : (c + 1) * 128]
            put_split(xh, xl, pl.ds(c * 32, 32), pl.ds(s * 128, 128), block)
    return data_by_table(xh[...], xl[...], wh[...], wl[...])


def first_kernel(
    point_ref, conn_ref, disp_ref, phase_ref, flag_ref, plastic_ref,
    wh, wl, th, tl, out_ref, xh, xl, bh, bl,
):
    macro = macro_strain(point_ref[0], conn_ref, disp_ref)
    for plane in range(PLANES):
        elastic = [macro[c] - every_fourth(plastic_ref, c * 128, plane) for c in range(6)]
        phases = every_fourth(phase_ref, 0, plane)
        flags = every_fourth(flag_ref, 0, plane)
        stress = material(elastic, phases, flags)[0]
        for c in range(6):
            put_split(xh, xl, pl.ds(c * 32, 32), pl.ds(plane * 128, 128), stress[c])
    forward_planes(xh, xl, bh, bl, wh, wl, th, tl, out_ref)


def middle_kernel(
    point_ref, conn_ref, disp_ref, phase_ref, flag_ref, plastic_ref, in_ref,
    vh, vl, uh, ul, wh, wl, th, tl, out_ref, elastic_ref, xh, xl, bh, bl,
):
    macro = macro_strain(point_ref[0], conn_ref, disp_ref)
    correction = backward_planes(in_ref, xh, xl, bh, bl, vh, vl, uh, ul)
    for plane in range(PLANES):
        lanes = slice(plane * 128, (plane + 1) * 128)
        elastic = []
        for c in range(6):
            before = macro[c] - every_fourth(plastic_ref, c * 128, plane)
            after = before - correction[c * 32 : (c + 1) * 32, lanes]
            elastic_ref[c * 32 : (c + 1) * 32, lanes] = after
            elastic.append(after)
        phases = every_fourth(phase_ref, 0, plane)
        flags = every_fourth(flag_ref, 0, plane)
        stress = material(elastic, phases, flags)[0]
        for c in range(6):
            put_split(xh, xl, pl.ds(c * 32, 32), pl.ds(plane * 128, 128), stress[c])
    forward_planes(xh, xl, bh, bl, wh, wl, th, tl, out_ref)


def last_kernel(
    phase_ref, flag_ref, elastic_ref, in_ref, vh, vl, uh, ul, out_ref, xh, xl, bh, bl
):
    correction = backward_planes(in_ref, xh, xl, bh, bl, vh, vl, uh, ul)
    sums = [None] * 28

    def collect(at, value):
        part = value.reshape(4, 8, 128)
        part = (part[0] + part[1]) + (part[2] + part[3])
        sums[at] = part if sums[at] is None else sums[at] + part

    for plane in range(PLANES):
        lanes = slice(plane * 128, (plane + 1) * 128)
        elastic = [
            elastic_ref[c * 32 : (c + 1) * 32, lanes] - correction[c * 32 : (c + 1) * 32, lanes]
            for c in range(6)
        ]
        phases = every_fourth(phase_ref, 0, plane)
        flags = every_fourth(flag_ref, 0, plane)
        stress, trial, softening, weight = material(elastic, phases, flags)
        for c in range(6):
            collect(c, stress[c])
        collect(6, softening)
        at = 7
        for a in range(6):
            scaled = weight * trial[a]
            for b in range(a, 6):
                collect(at, scaled * trial[b])
                at += 1
    row = lax.broadcasted_iota(jnp.int32, (128, 128), 0)
    lines = jnp.zeros((128, 128), jnp.float32)

    def place(at, value):
        return jnp.where(row == at, jnp.broadcast_to(value, (128, 128)), lines)

    totals = [jnp.sum(value, axis=0, keepdims=True) for value in sums]
    for c in range(7):
        lines = place(c, totals[c])
    at = 7
    for a in range(6):
        for b in range(a, 6):
            lines = place(OUTER_AT + 6 * a + b, totals[at])
            if a != b:
                lines = place(OUTER_AT + 6 * b + a, totals[at])
            at += 1
    ones = jnp.ones((8, 128), jnp.float32)
    line = lax.dot_general(
        ones, lines, (((1,), (1,)), ((), ())),
        precision=lax.Precision.HIGHEST, preferred_element_type=jnp.float32,
    )
    out_ref[...] = jnp.broadcast_to(line[None], out_ref.shape)


def column_kernel(slab_ref, in_ref, th, tl, bh_table, bl_table, twist_ref, four, fourback, out_ref, bh, bl, yh, yl):
    load_columns(in_ref, bh, bl)
    mixed = table_by_data(th[...], tl[...], bh[...], bl[...])
    cosine, sine = twist_ref[0], twist_ref[1]
    for c in range(6):
        lanes = slice(c * 128, (c + 1) * 128)
        real, imag = mixed[:64, lanes], mixed[64:, lanes]
        rows = pl.ds(c * 64, 64)
        put_split(yh, yl, rows, pl.ds(0, 128), real * cosine + imag * sine)
        put_split(yh, yl, rows, pl.ds(128, 128), imag * cosine - real * sine)
    spectrum = mm(yh[...], four[...]) + mm(yl[...], four[...])
    tau = [spectrum[c * 64 : (c + 1) * 64] for c in range(6)]

    shape = (64, 256)
    row = lax.broadcasted_iota(jnp.int32, shape, 0)
    lane = lax.broadcasted_iota(jnp.int32, shape, 1)
    lane = lax.bitwise_and(lane, 127)
    kx = 16 * lax.shift_right_logical(lane, 5) + lax.shift_right_logical(row, 2)
    ky = 4 * slab_ref[0] + lax.bitwise_and(row, 3)
    kz = lax.bitwise_and(lane, 31)
    half = GRID // 2
    keep = (kx != half) & (ky != half) & (kx + ky + kz > 0)
    xi = [
        jnp.where(kx < half, kx, kx - GRID).astype(jnp.float32),
        jnp.where(ky < half, ky, ky - GRID).astype(jnp.float32),
        kz.astype(jnp.float32),
    ]
    length = xi[0] * xi[0] + xi[1] * xi[1] + xi[2] * xi[2]
    inverse = jnp.where(keep, 1.0 / jnp.maximum(length, 1.0), 0.0)
    coupling = (REFERENCE_LAME + REFERENCE_SHEAR) / (
        REFERENCE_SHEAR * (REFERENCE_LAME + 2.0 * REFERENCE_SHEAR)
    )
    scaled = inverse * (1.0 / (2.0 * REFERENCE_SHEAR))
    traction = [
        tau[r[0]] * xi[0] + tau[r[1]] * xi[1] + tau[r[2]] * xi[2] for r in TENSOR_ROWS
    ]
    load = xi[0] * traction[0] + xi[1] * traction[1] + xi[2] * traction[2]
    load = load * (inverse * (REFERENCE_SHEAR * coupling))
    field = [scaled * (traction[i] - xi[i] * load) for i in range(3)]
    for c, (i, k) in enumerate(TENSOR_PAIRS):
        entry = xi[i] * field[k] + xi[k] * field[i]
        put_split(yh, yl, pl.ds(c * 64, 64), slice(None), entry)
    turned = mm(yh[...], fourback[...]) + mm(yl[...], fourback[...])
    for c in range(6):
        real, imag = turned[c * 64 : (c + 1) * 64, :128], turned[c * 64 : (c + 1) * 64, 128:]
        cols = pl.ds(c * 128, 128)
        put_split(bh, bl, pl.ds(0, 64), cols, real * cosine - imag * sine)
        put_split(bh, bl, pl.ds(64, 64), cols, real * sine + imag * cosine)
    result = table_by_data(bh_table[...], bl_table[...], bh[...], bl[...])
    for c in range(6):
        out_ref[:, c * 8 : (c + 1) * 8, :] = result[:, c * 128 : (c + 1) * 128].reshape(16, 8, 128)


def assembly_kernel(points, conn_ref, in_ref, stiffness_ref, forces_ref):
    sums = in_ref[pl.ds(0, points, stride=8), :] * (1.0 / VOXELS)
    shape = (points, 128)
    lane = lax.broadcasted_iota(jnp.int32, shape, 1)
    point = lax.broadcasted_iota(jnp.int32, shape, 0)
    element = lax.shift_right_logical(point, 3)
    bits = [lax.bitwise_and(lax.shift_right_logical(point, d), 1) for d in range(3)]
    slope = slopes_of(bits, GAUSS_LOW, GAUSS_HIGH)
    node = lane // 3
    part = lane - 3 * node
    elements = conn_ref.shape[0]
    grad = [jnp.zeros(shape, jnp.float32) for _ in range(3)]
    for corner in range(8):
        owner = jnp.full(shape, conn_ref[0, corner], jnp.int32)
        for e in range(1, elements):
            owner = jnp.where(element == e, conn_ref[e, corner], owner)
        here = (owner == node) & (lane < 60)
        for d in range(3):
            grad[d] = grad[d] + jnp.where(here, slope(corner, d), 0.0)
    basis = []
    for i, k in TENSOR_PAIRS:
        if i == k:
            basis.append(jnp.where(part == i, grad[i], 0.0))
        else:
            value = jnp.where(part == i, 0.5 * grad[k], 0.0)
            basis.append(value + jnp.where(part == k, 0.5 * grad[i], 0.0))
    mean_shear = 2.0 * SHEAR_MODULUS * sums[:, 6:7]

    def column(at):
        return jnp.broadcast_to(sums[:, at : at + 1], shape)

    mean_shear = jnp.broadcast_to(mean_shear, shape)
    on_diagonal = BULK_MODULUS + mean_shear * (2.0 / 3.0)
    off_diagonal = BULK_MODULUS - mean_shear * (1.0 / 3.0)
    answers = []
    force = jnp.zeros(shape, jnp.float32)
    scale = QUADRATURE_WEIGHT / TANGENT_UNIT
    for a in range(6):
        total = jnp.zeros(shape, jnp.float32)
        for b in range(6):
            low, high = min(a, b), max(a, b)
            entry = -PAIR_WEIGHTS[b] * column(OUTER_AT + 6 * low + high)
            if a == b:
                entry = entry + (on_diagonal if a < 3 else mean_shear)
            elif a < 3 and b < 3:
                entry = entry + off_diagonal
            total = total + entry * basis[b]
        answers.append(total * (PAIR_WEIGHTS[a] * scale))
        force = force + basis[a] * (column(a) * (PAIR_WEIGHTS[a] * QUADRATURE_WEIGHT))
    left = jnp.concatenate(basis, axis=0)
    right = jnp.concatenate(answers, axis=0)
    whole = lax.dot_general(
        left, right, (((0,), (0,)), ((), ())),
        precision=lax.Precision.HIGHEST, preferred_element_type=jnp.float32,
    )
    stiffness_ref[...] = whole[:60, :60]
    line = jnp.sum(force, axis=0, keepdims=True)
    row24 = lax.broadcasted_iota(jnp.int32, (24, 128), 0)
    lane24 = lax.broadcasted_iota(jnp.int32, (24, 128), 1)
    spread = jnp.where(lane24 // 3 == row24, jnp.broadcast_to(line, (24, 128)), 0.0)
    pick_row = lax.broadcasted_iota(jnp.int32, (128, 128), 0)
    pick_col = lax.broadcasted_iota(jnp.int32, (128, 128), 1)
    pick = (pick_row % 3 == pick_col).astype(jnp.float32)
    forces = jnp.dot(
        spread, pick, precision=lax.Precision.HIGHEST, preferred_element_type=jnp.float32
    )
    forces_ref[...] = forces[:20, :3]


SMEM = pl.BlockSpec(memory_space=pltpu.SMEM)
VMEM = pl.BlockSpec(memory_space=pltpu.VMEM)
BF16 = jnp.bfloat16
F32 = jnp.float32
LIMIT = 16 * 1024 * 1024


def params():
    return pltpu.CompilerParams(vmem_limit_bytes=LIMIT)


def cost(flops, size):
    return pl.CostEstimate(flops=flops, bytes_accessed=size, transcendentals=0)


def plane_scratch():
    return [
        pltpu.VMEM((192, 512), BF16),
        pltpu.VMEM((192, 512), BF16),
        pltpu.VMEM((128, 768), BF16),
        pltpu.VMEM((128, 768), BF16),
    ]


def exchange(array):
    return lax.all_to_all(array, "slab", split_axis=0, concat_axis=0, tiled=True)


def on_device(phase_ids, yield_flags, plastic_strain, displacements, connectivity):
    points = lax.axis_size("rve")
    point = lax.axis_index("rve").astype(jnp.int32).reshape(1)
    slab = lax.axis_index("slab").astype(jnp.int32).reshape(1)

    def rows(array):
        lead = math.prod(array.shape[:-2])
        array = array.reshape(lead, PLANES, 32, 128)
        return jnp.transpose(array, (0, 2, 1, 3)).reshape(lead * 128, 128)

    phases = rows(phase_ids)
    flags = rows(yield_flags)
    plastic = rows(plastic_strain)

    there, back = depth_tables()
    wh, wl = (jnp.asarray(t) for t in halves(there))
    vh, vl = (jnp.asarray(t) for t in halves(back))
    there, back = row_tables()
    th, tl = (jnp.asarray(t) for t in halves(there))
    uh, ul = (jnp.asarray(t) for t in halves(back))
    there, back, twist, four, fourback = column_tables()
    ch, cl = (jnp.asarray(t) for t in halves(there))
    dh, dl = (jnp.asarray(t) for t in halves(back))
    twist = jnp.asarray(twist)
    four = jnp.asarray(four.astype(ml_dtypes.bfloat16))
    fourback = jnp.asarray(fourback.astype(ml_dtypes.bfloat16))

    block = jax.ShapeDtypeStruct((16, 48, 128), F32)

    def flag_block(evaluation):
        return flags[evaluation * 128 : (evaluation + 1) * 128]

    first = pl.pallas_call(
        first_kernel, out_shape=block,
        in_specs=[SMEM] * 3 + [VMEM] * 7, out_specs=VMEM,
        scratch_shapes=plane_scratch(), compiler_params=params(),
        cost_estimate=cost(400_000_000, 2_000_000), name="first",
    )
    columns = pl.pallas_call(
        column_kernel, out_shape=block,
        in_specs=[SMEM] + [VMEM] * 8, out_specs=VMEM,
        scratch_shapes=[
            pltpu.VMEM((128, 768), BF16), pltpu.VMEM((128, 768), BF16),
            pltpu.VMEM((384, 256), BF16), pltpu.VMEM((384, 256), BF16),
        ],
        compiler_params=params(), cost_estimate=cost(400_000_000, 2_000_000), name="columns",
    )
    middle = pl.pallas_call(
        middle_kernel, out_shape=(block, jax.ShapeDtypeStruct((192, 512), F32)),
        in_specs=[SMEM] * 3 + [VMEM] * 12, out_specs=(VMEM, VMEM),
        scratch_shapes=plane_scratch(), compiler_params=params(),
        cost_estimate=cost(800_000_000, 4_000_000), name="middle",
    )
    last = pl.pallas_call(
        last_kernel, out_shape=jax.ShapeDtypeStruct((16, 8, 128), F32),
        in_specs=[VMEM] * 8, out_specs=VMEM,
        scratch_shapes=plane_scratch(), compiler_params=params(),
        cost_estimate=cost(400_000_000, 2_000_000), name="last",
    )
    assembly = pl.pallas_call(
        functools.partial(assembly_kernel, points),
        out_shape=(jax.ShapeDtypeStruct((60, 60), F32), jax.ShapeDtypeStruct((20, 3), F32)),
        in_specs=[SMEM, VMEM], out_specs=(VMEM, VMEM), compiler_params=params(),
        cost_estimate=cost(10_000_000, 200_000), name="assembly",
    )

    def apply_columns(array):
        received = exchange(array)
        return exchange(columns(slab, received, ch, cl, dh, dl, twist, four, fourback))

    spectrum = first(
        point, connectivity, displacements, phases, flag_block(0), plastic, wh, wl, th, tl
    )
    planes = apply_columns(spectrum)
    spectrum, elastic = middle(
        point, connectivity, displacements, phases, flag_block(1), plastic, planes,
        vh, vl, uh, ul, wh, wl, th, tl,
    )
    planes = apply_columns(spectrum)
    partial = last(phases, flag_block(2), elastic, planes, vh, vl, uh, ul)
    sums = jnp.sum(exchange(partial), axis=0)
    everyone = lax.all_to_all(
        jnp.broadcast_to(sums[None], (points, 8, 128)), "rve", 0, 0, tiled=True
    )
    stiffness, forces = assembly(connectivity, everyone.reshape(points * 8, 128))

    own = sums[0] * (1.0 / VOXELS)
    mean_stress = own[:6].reshape(1, 6)
    outer = own[OUTER_AT : OUTER_AT + 36].reshape(6, 6)
    diagonal = np.array([1.0, 1.0, 1.0, 0.0, 0.0, 0.0])
    volumetric = diagonal[:, None] * diagonal[None, :]
    fixed = jnp.asarray(BULK_MODULUS * volumetric / TANGENT_UNIT, F32)
    turning = (np.eye(6) - volumetric / 3.0) * (2.0 * SHEAR_MODULUS / TANGENT_UNIT)
    weights = np.asarray(PAIR_WEIGHTS)[None, :] / TANGENT_UNIT
    tangent = (
        fixed + own[6] * jnp.asarray(turning, F32) - outer * jnp.asarray(weights, F32)
    )
    return (mean_stress, tangent[None], forces, stiffness)


def solution(mesh):
    return jax.shard_map(
        on_device,
        mesh=mesh,
        in_specs=(
            P("slab", None),
            P("rve", None, "slab", None),
            P("rve", None, "slab", None),
            P(),
            P(),
        ),
        out_specs=(P("rve", None), P("rve", None, None), P(), P()),
        check_vma=False,
    )
```

```python
import functools
import math

import jax
import jax.numpy as jnp
import ml_dtypes
import numpy as np
from jax import lax
from jax.experimental import pallas as pl
from jax.experimental.pallas import tpu as pltpu
from jax.sharding import PartitionSpec as P

GRID = 64
ITERS = 2
SLABS = 16
PLANES = GRID // SLABS
KEPT = GRID // 2

SHEAR_MODULUS = 80.0
BULK_MODULUS = 160.0
REFERENCE_SHEAR = 80.0
REFERENCE_LAME = 160.0 - 160.0 / 3.0
TANGENT_UNIT = 100.0
QUADRATURE_WEIGHT = 0.125
PAIR_WEIGHTS = (1.0, 1.0, 1.0, 2.0, 2.0, 2.0)
TENSOR_PAIRS = ((0, 0), (1, 1), (2, 2), (1, 2), (0, 2), (0, 1))
TENSOR_ROWS = ((0, 5, 4), (5, 1, 3), (4, 3, 2))
VOXELS = float(GRID**3)
GAUSS_LOW = 0.5 - 0.5 / math.sqrt(3.0)
GAUSS_HIGH = 0.5 + 0.5 / math.sqrt(3.0)
OUTER_AT = 8


def halves(table):
    high = table.astype(np.float32).astype(ml_dtypes.bfloat16)
    low = (table - high.astype(np.float64)).astype(np.float32).astype(ml_dtypes.bfloat16)
    return high, low


def depth_tables():
    z = np.arange(GRID)
    k = np.arange(KEPT)
    theta = 2.0 * np.pi * np.outer(z, k) / GRID
    forward = np.stack([np.cos(theta), -np.sin(theta)], axis=0)
    weight = np.where(k == 0, 1.0, 2.0) / VOXELS
    inverse = forward * weight[None, None, :]
    planes = np.eye(PLANES)
    pair = np.eye(2)
    there = np.einsum("lL,rR,pzk->lrzRpLk", planes, pair, forward)
    back = np.einsum("lL,rR,pzk->RpLklrz", planes, pair, inverse)
    return there.reshape(512, 512), back.reshape(512, 512)


def row_tables():
    y = 2 * np.arange(32)[None, :] + np.arange(2)[:, None]
    ky = 4 * np.arange(16)[:, None] + np.arange(4)[None, :]
    theta = 2.0 * np.pi * np.einsum("de,rm->derm", ky, y) / GRID
    c, s = np.cos(theta), np.sin(theta)
    there = np.zeros((16, 2, 4, 2, 2, 32))
    there[:, 0, :, :, 0, :] = c
    there[:, 0, :, :, 1, :] = s
    there[:, 1, :, :, 0, :] = -s
    there[:, 1, :, :, 1, :] = c
    back = np.zeros((2, 2, 32, 16, 2, 4))
    ct, st = np.einsum("derm->rmde", c), np.einsum("derm->rmde", s)
    back[:, 0, :, :, 0, :] = ct
    back[:, 0, :, :, 1, :] = -st
    back[:, 1, :, :, 0, :] = st
    back[:, 1, :, :, 1, :] = ct
    return there.reshape(128, 128), back.reshape(128, 128)


def column_tables():
    d = np.arange(16)
    theta = 2.0 * np.pi * np.outer(d, d) / 16.0
    c, s = np.cos(theta), np.sin(theta)
    same = np.eye(4)
    there = np.zeros((2, 16, 4, 16, 2, 4))
    there[0, :, :, :, 0, :] = np.einsum("bd,ef->bedf", c, same)
    there[0, :, :, :, 1, :] = np.einsum("bd,ef->bedf", s, same)
    there[1, :, :, :, 0, :] = np.einsum("bd,ef->bedf", -s, same)
    there[1, :, :, :, 1, :] = np.einsum("bd,ef->bedf", c, same)
    there = there.reshape(128, 128)
    phi = 2.0 * np.pi * np.outer(np.arange(16), np.arange(4)) / GRID
    twist = np.stack([np.cos(phi), np.sin(phi)])[:, :, None, :, None]
    twist = np.broadcast_to(twist, (2, 16, 4, 4, KEPT)).reshape(2, 64, 128)
    quarter = 2.0 * np.pi * np.outer(np.arange(4), np.arange(4)) / 4.0
    cq, sq = np.rint(np.cos(quarter)), np.rint(np.sin(quarter))
    kept = np.eye(KEPT)
    four = np.zeros((2, 4, KEPT, 2, 4, KEPT))
    four[0, :, :, 0] = np.einsum("la,kK->lkaK", cq, kept)
    four[1, :, :, 0] = np.einsum("la,kK->lkaK", sq, kept)
    four[0, :, :, 1] = np.einsum("la,kK->lkaK", -sq, kept)
    four[1, :, :, 1] = np.einsum("la,kK->lkaK", cq, kept)
    four = four.reshape(256, 256)
    return there, there.T.copy(), twist.astype(np.float32), four, four.T.copy()


def split(x):
    high = x.astype(jnp.bfloat16)
    low = (x - high.astype(jnp.float32)).astype(jnp.bfloat16)
    return high, low


def mm(a, b):
    return jnp.dot(a, b, preferred_element_type=jnp.float32)


def data_by_table(high, low, table_high, table_low):
    return mm(high, table_high) + (mm(low, table_high) + mm(high, table_low))


def table_by_data(table_high, table_low, high, low):
    return mm(table_high, high) + (mm(table_low, high) + mm(table_high, low))


def slopes_of(bits, low, high):
    at = [jnp.where(bit == 1, high, low) for bit in bits]
    far = [jnp.where(bit == 1, low, high) for bit in bits]

    def slope(corner, axis):
        value = None
        for other in range(3):
            if other != axis:
                factor = at[other] if corner >> other & 1 else far[other]
                value = factor if value is None else value * factor
        return value if corner >> axis & 1 else -value

    return slope


def macro_strain(point, conn_ref, disp_ref):
    low, high = jnp.float32(GAUSS_LOW), jnp.float32(GAUSS_HIGH)
    bits = [lax.bitwise_and(lax.shift_right_logical(point, d), 1) for d in range(3)]
    slope = slopes_of(bits, low, high)
    element = lax.shift_right_logical(point, 3)
    grad = [[jnp.float32(0.0)] * 3 for _ in range(3)]
    for corner in range(8):
        node = conn_ref[element, corner]
        for k in range(3):
            u = disp_ref[k, node]
            for d in range(3):
                grad[k][d] = grad[k][d] + slope(corner, d) * u
    strain = []
    for i, j in TENSOR_PAIRS:
        strain.append(grad[i][i] if i == j else 0.5 * (grad[i][j] + grad[j][i]))
    return strain


def material(elastic, phases, flags):
    hard = phases == 1
    limit = jnp.where(hard, 1.2, 0.3)
    ratio = jnp.where(
        hard,
        3.0 * SHEAR_MODULUS / (3.0 * SHEAR_MODULUS + 10.0),
        3.0 * SHEAR_MODULUS / (3.0 * SHEAR_MODULUS + 2.0),
    )
    active = flags.astype(jnp.float32)
    volume = elastic[0] + elastic[1] + elastic[2]
    third = volume * (1.0 / 3.0)
    trial = [2.0 * SHEAR_MODULUS * (elastic[a] - third) for a in range(3)]
    trial += [2.0 * SHEAR_MODULUS * elastic[a] for a in range(3, 6)]
    normal = trial[0] * trial[0] + trial[1] * trial[1] + trial[2] * trial[2]
    shear = trial[3] * trial[3] + trial[4] * trial[4] + trial[5] * trial[5]
    equivalent = jnp.sqrt(1.5 * (normal + 2.0 * shear))
    bounded = jnp.maximum(equivalent, limit)
    inverse = 1.0 / bounded
    scaled = ratio * active
    softening = 1.0 - scaled * (equivalent - limit) * inverse
    pressure = BULK_MODULUS * volume
    stress = [trial[a] * softening + pressure for a in range(3)]
    stress += [trial[a] * softening for a in range(3, 6)]
    weight = 3.0 * SHEAR_MODULUS * scaled * limit * (inverse * inverse * inverse)
    return stress, trial, softening, weight


def every_fourth(ref, start, plane):
    return ref[pl.ds(start + plane, 32, stride=4), :]


def put_split(high_ref, low_ref, rows, cols, value):
    high, low = split(value)
    high_ref[rows, cols] = high
    low_ref[rows, cols] = low


def forward_planes(xh, xl, bh, bl, wh, wl, th, tl, out_ref):
    turned = data_by_table(xh[...], xl[...], wh[...], wl[...])
    for c in range(6):
        for s in range(4):
            block = turned[c * 32 : (c + 1) * 32, s * 128 : (s + 1) * 128]
            put_split(bh, bl, pl.ds(s * 32, 32), pl.ds(c * 128, 128), block)
    spectrum = table_by_data(th[...], tl[...], bh[...], bl[...])
    for c in range(6):
        out_ref[:, c * 8 : (c + 1) * 8, :] = spectrum[:, c * 128 : (c + 1) * 128].reshape(
            16, 8, 128
        )


def load_columns(in_ref, bh, bl):
    for c in range(6):
        block = in_ref[:, c * 8 : (c + 1) * 8, :].reshape(128, 128)
        put_split(bh, bl, slice(None), pl.ds(c * 128, 128), block)


def backward_planes(in_ref, xh, xl, bh, bl, wh, wl, th, tl):
    load_columns(in_ref, bh, bl)
    rows = table_by_data(th[...], tl[...], bh[...], bl[...])
    for c in range(6):
        for s in range(4):
            block = rows[s * 32 : (s + 1) * 32, c * 128 : (c + 1) * 128]
            put_split(xh, xl, pl.ds(c * 32, 32), pl.ds(s * 128, 128), block)
    return data_by_table(xh[...], xl[...], wh[...], wl[...])


def first_kernel(
    conn_hbm, disp_hbm, phase_hbm, flag_hbm, plastic_hbm, wh_hbm, wl_hbm, th_hbm, tl_hbm,
    out_ref, macro_ref,
    conn_ref, disp_ref, phase_ref, flag_ref, plastic_ref, wh, wl, th, tl, sems, xh, xl, bh, bl,
):
    pairs = (
        (conn_hbm, conn_ref), (disp_hbm, disp_ref), (plastic_hbm, plastic_ref),
        (phase_hbm, phase_ref), (flag_hbm.at[pl.ds(0, 128)], flag_ref),
        (wh_hbm, wh), (wl_hbm, wl), (th_hbm, th), (tl_hbm, tl),
    )
    copies = [pltpu.make_async_copy(a, b, sems.at[i]) for i, (a, b) in enumerate(pairs)]
    for copy in copies:
        copy.start()
    for copy in copies[:2]:
        copy.wait()
    macro = macro_strain(lax.axis_index("rve"), conn_ref, disp_ref)
    row = lax.broadcasted_iota(jnp.int32, (8, 128), 0)
    table = jnp.zeros((8, 128), jnp.float32)
    for c in range(6):
        table = jnp.where(row == c, macro[c], table)
    macro_ref[...] = table
    for copy in copies[2:5]:
        copy.wait()
    for plane in range(PLANES):
        elastic = [macro[c] - every_fourth(plastic_ref, c * 128, plane) for c in range(6)]
        phases = every_fourth(phase_ref, 0, plane)
        flags = every_fourth(flag_ref, 0, plane)
        stress = material(elastic, phases, flags)[0]
        for c in range(6):
            put_split(xh, xl, pl.ds(c * 32, 32), pl.ds(plane * 128, 128), stress[c])
    for copy in copies[5:]:
        copy.wait()
    forward_planes(xh, xl, bh, bl, wh, wl, th, tl, out_ref)


def middle_kernel(
    macro_ref, phase_ref, flag_ref, plastic_ref, in_ref,
    vh, vl, uh, ul, wh, wl, th, tl, out_ref, elastic_ref, xh, xl, bh, bl,
):
    macro = [macro_ref[c : c + 1, :] for c in range(6)]
    correction = backward_planes(in_ref, xh, xl, bh, bl, vh, vl, uh, ul)
    for plane in range(PLANES):
        lanes = slice(plane * 128, (plane + 1) * 128)
        elastic = []
        for c in range(6):
            before = macro[c] - every_fourth(plastic_ref, c * 128, plane)
            after = before - correction[c * 32 : (c + 1) * 32, lanes]
            elastic_ref[c * 32 : (c + 1) * 32, lanes] = after
            elastic.append(after)
        phases = every_fourth(phase_ref, 0, plane)
        flags = every_fourth(flag_ref, 128, plane)
        stress = material(elastic, phases, flags)[0]
        for c in range(6):
            put_split(xh, xl, pl.ds(c * 32, 32), pl.ds(plane * 128, 128), stress[c])
    forward_planes(xh, xl, bh, bl, wh, wl, th, tl, out_ref)


def last_kernel(
    phase_ref, flag_ref, elastic_ref, in_ref, vh, vl, uh, ul, out_ref, xh, xl, bh, bl
):
    correction = backward_planes(in_ref, xh, xl, bh, bl, vh, vl, uh, ul)
    sums = [None] * 28

    def collect(at, value):
        part = value.reshape(4, 8, 128)
        part = (part[0] + part[1]) + (part[2] + part[3])
        sums[at] = part if sums[at] is None else sums[at] + part

    for plane in range(PLANES):
        lanes = slice(plane * 128, (plane + 1) * 128)
        elastic = [
            elastic_ref[c * 32 : (c + 1) * 32, lanes] - correction[c * 32 : (c + 1) * 32, lanes]
            for c in range(6)
        ]
        phases = every_fourth(phase_ref, 0, plane)
        flags = every_fourth(flag_ref, 256, plane)
        stress, trial, softening, weight = material(elastic, phases, flags)
        for c in range(6):
            collect(c, stress[c])
        collect(6, softening)
        at = 7
        for a in range(6):
            scaled = weight * trial[a]
            for b in range(a, 6):
                collect(at, scaled * trial[b])
                at += 1
    row = lax.broadcasted_iota(jnp.int32, (128, 128), 0)
    lines = jnp.zeros((128, 128), jnp.float32)

    def place(at, value):
        return jnp.where(row == at, jnp.broadcast_to(value, (128, 128)), lines)

    totals = [jnp.sum(value, axis=0, keepdims=True) for value in sums]
    for c in range(7):
        lines = place(c, totals[c])
    at = 7
    for a in range(6):
        for b in range(a, 6):
            lines = place(OUTER_AT + 6 * a + b, totals[at])
            if a != b:
                lines = place(OUTER_AT + 6 * b + a, totals[at])
            at += 1
    ones = jnp.ones((SLABS, 128), jnp.float32)
    line = lax.dot_general(
        ones, lines, (((1,), (1,)), ((), ())),
        precision=lax.Precision.HIGHEST, preferred_element_type=jnp.float32,
    )
    out_ref[...] = line.reshape(SLABS, 1, 128)


def column_kernel(in_ref, th, tl, bh_table, bl_table, twist_ref, four, fourback, out_ref, bh, bl, yh, yl):
    load_columns(in_ref, bh, bl)
    mixed = table_by_data(th[...], tl[...], bh[...], bl[...])
    cosine, sine = twist_ref[0], twist_ref[1]
    for c in range(6):
        lanes = slice(c * 128, (c + 1) * 128)
        real, imag = mixed[:64, lanes], mixed[64:, lanes]
        rows = pl.ds(c * 64, 64)
        put_split(yh, yl, rows, pl.ds(0, 128), real * cosine + imag * sine)
        put_split(yh, yl, rows, pl.ds(128, 128), imag * cosine - real * sine)
    spectrum = mm(yh[...], four[...]) + mm(yl[...], four[...])
    tau = [spectrum[c * 64 : (c + 1) * 64] for c in range(6)]

    shape = (64, 256)
    row = lax.broadcasted_iota(jnp.int32, shape, 0)
    lane = lax.broadcasted_iota(jnp.int32, shape, 1)
    lane = lax.bitwise_and(lane, 127)
    kx = 16 * lax.shift_right_logical(lane, 5) + lax.shift_right_logical(row, 2)
    ky = 4 * lax.axis_index("slab") + lax.bitwise_and(row, 3)
    kz = lax.bitwise_and(lane, 31)
    half = GRID // 2
    keep = (kx != half) & (ky != half) & (kx + ky + kz > 0)
    xi = [
        jnp.where(kx < half, kx, kx - GRID).astype(jnp.float32),
        jnp.where(ky < half, ky, ky - GRID).astype(jnp.float32),
        kz.astype(jnp.float32),
    ]
    length = xi[0] * xi[0] + xi[1] * xi[1] + xi[2] * xi[2]
    inverse = jnp.where(keep, 1.0 / jnp.maximum(length, 1.0), 0.0)
    coupling = (REFERENCE_LAME + REFERENCE_SHEAR) / (
        REFERENCE_SHEAR * (REFERENCE_LAME + 2.0 * REFERENCE_SHEAR)
    )
    scaled = inverse * (1.0 / (2.0 * REFERENCE_SHEAR))
    traction = [
        tau[r[0]] * xi[0] + tau[r[1]] * xi[1] + tau[r[2]] * xi[2] for r in TENSOR_ROWS
    ]
    load = xi[0] * traction[0] + xi[1] * traction[1] + xi[2] * traction[2]
    load = load * (inverse * (REFERENCE_SHEAR * coupling))
    field = [scaled * (traction[i] - xi[i] * load) for i in range(3)]
    for c, (i, k) in enumerate(TENSOR_PAIRS):
        entry = xi[i] * field[k] + xi[k] * field[i]
        put_split(yh, yl, pl.ds(c * 64, 64), slice(None), entry)
    turned = mm(yh[...], fourback[...]) + mm(yl[...], fourback[...])
    for c in range(6):
        real, imag = turned[c * 64 : (c + 1) * 64, :128], turned[c * 64 : (c + 1) * 64, 128:]
        cols = pl.ds(c * 128, 128)
        put_split(bh, bl, pl.ds(0, 64), cols, real * cosine - imag * sine)
        put_split(bh, bl, pl.ds(64, 64), cols, real * sine + imag * cosine)
    result = table_by_data(bh_table[...], bl_table[...], bh[...], bl[...])
    for c in range(6):
        out_ref[:, c * 8 : (c + 1) * 8, :] = result[:, c * 128 : (c + 1) * 128].reshape(16, 8, 128)


def totals_kernel(in_ref, all_ref, stress_ref, tangent_ref):
    line = jnp.sum(in_ref[...].reshape(SLABS, 128), axis=0, keepdims=True)
    all_ref[...] = jnp.broadcast_to(line[None], all_ref.shape)
    line = line * (1.0 / VOXELS)
    stress_ref[...] = line[:, :6]
    at = lax.broadcasted_iota(jnp.int32, (1, 128), 1) - OUTER_AT
    a = at // 6
    b = at - 6 * a
    both = (a < 3) & (b < 3)
    shear = jnp.broadcast_to(line[:, 6:7], (1, 128)) * (2.0 * SHEAR_MODULUS)
    fixed = jnp.where(both, BULK_MODULUS - shear * (1.0 / 3.0), 0.0)
    fixed = fixed + jnp.where(a == b, shear, 0.0)
    whole = (fixed - line * jnp.where(b < 3, 1.0, 2.0)) * (1.0 / TANGENT_UNIT)
    for i in range(6):
        tangent_ref[i] = whole[:, OUTER_AT + 6 * i : OUTER_AT + 6 * i + 6]


def assembly_kernel(points, conn_ref, in_ref, stiffness_ref, forces_ref):
    sums = in_ref[...].reshape(points, 128) * (1.0 / VOXELS)
    shape = (points, 128)
    lane = lax.broadcasted_iota(jnp.int32, shape, 1)
    point = lax.broadcasted_iota(jnp.int32, shape, 0)
    element = lax.shift_right_logical(point, 3)
    bits = [lax.bitwise_and(lax.shift_right_logical(point, d), 1) for d in range(3)]
    slope = slopes_of(bits, GAUSS_LOW, GAUSS_HIGH)
    node = lane // 3
    part = lane - 3 * node
    elements = conn_ref.shape[0]
    grad = [jnp.zeros(shape, jnp.float32) for _ in range(3)]
    for corner in range(8):
        owner = jnp.full(shape, conn_ref[0, corner], jnp.int32)
        for e in range(1, elements):
            owner = jnp.where(element == e, conn_ref[e, corner], owner)
        here = (owner == node) & (lane < 60)
        for d in range(3):
            grad[d] = grad[d] + jnp.where(here, slope(corner, d), 0.0)
    basis = []
    for i, k in TENSOR_PAIRS:
        if i == k:
            basis.append(jnp.where(part == i, grad[i], 0.0))
        else:
            value = jnp.where(part == i, 0.5 * grad[k], 0.0)
            basis.append(value + jnp.where(part == k, 0.5 * grad[i], 0.0))
    mean_shear = 2.0 * SHEAR_MODULUS * sums[:, 6:7]

    def column(at):
        return jnp.broadcast_to(sums[:, at : at + 1], shape)

    mean_shear = jnp.broadcast_to(mean_shear, shape)
    on_diagonal = BULK_MODULUS + mean_shear * (2.0 / 3.0)
    off_diagonal = BULK_MODULUS - mean_shear * (1.0 / 3.0)
    answers = []
    force = jnp.zeros(shape, jnp.float32)
    scale = QUADRATURE_WEIGHT / TANGENT_UNIT
    for a in range(6):
        total = jnp.zeros(shape, jnp.float32)
        for b in range(6):
            low, high = min(a, b), max(a, b)
            entry = -PAIR_WEIGHTS[b] * column(OUTER_AT + 6 * low + high)
            if a == b:
                entry = entry + (on_diagonal if a < 3 else mean_shear)
            elif a < 3 and b < 3:
                entry = entry + off_diagonal
            total = total + entry * basis[b]
        answers.append(total * (PAIR_WEIGHTS[a] * scale))
        force = force + basis[a] * (column(a) * (PAIR_WEIGHTS[a] * QUADRATURE_WEIGHT))
    left = jnp.concatenate(basis, axis=0)
    right = jnp.concatenate(answers, axis=0)
    whole = lax.dot_general(
        left, right, (((0,), (0,)), ((), ())),
        precision=lax.Precision.HIGHEST, preferred_element_type=jnp.float32,
    )
    stiffness_ref[...] = whole[:60, :60]
    line = jnp.sum(force, axis=0, keepdims=True)
    part8 = lax.broadcasted_iota(jnp.int32, (8, 128), 0)
    lane8 = lax.broadcasted_iota(jnp.int32, (8, 128), 1)
    spread = jnp.where(lane8 % 3 == part8, jnp.broadcast_to(line, (8, 128)), 0.0)
    pick_row = lax.broadcasted_iota(jnp.int32, (128, 128), 0)
    pick_col = lax.broadcasted_iota(jnp.int32, (128, 128), 1)
    pick = (pick_row // 3 == pick_col).astype(jnp.float32)
    forces = jnp.dot(
        spread, pick, precision=lax.Precision.HIGHEST, preferred_element_type=jnp.float32
    )
    forces_ref[...] = forces[:3, :20]


SMEM = pl.BlockSpec(memory_space=pltpu.SMEM)
VMEM = pl.BlockSpec(memory_space=pltpu.VMEM)
HBM = pl.BlockSpec(memory_space=pltpu.HBM)
BF16 = jnp.bfloat16
F32 = jnp.float32
LIMIT = 16 * 1024 * 1024


def params():
    return pltpu.CompilerParams(vmem_limit_bytes=LIMIT)


def cost(flops, size):
    return pl.CostEstimate(flops=flops, bytes_accessed=size, transcendentals=0)


def plane_scratch():
    return [
        pltpu.VMEM((192, 512), BF16),
        pltpu.VMEM((192, 512), BF16),
        pltpu.VMEM((128, 768), BF16),
        pltpu.VMEM((128, 768), BF16),
    ]


def exchange(array):
    return lax.all_to_all(array, "slab", split_axis=0, concat_axis=0, tiled=True)


def on_device(phase_ids, yield_flags, plastic_strain, displacements, connectivity):
    points = lax.axis_size("rve")

    def rows(array):
        lead = math.prod(array.shape[:-2])
        array = array.reshape(lead, PLANES, 32, 128)
        return jnp.transpose(array, (0, 2, 1, 3)).reshape(lead * 128, 128)

    phases = rows(phase_ids)
    flags = rows(yield_flags)
    plastic = rows(plastic_strain)

    there, back = depth_tables()
    wh, wl = (jnp.asarray(t) for t in halves(there))
    vh, vl = (jnp.asarray(t) for t in halves(back))
    there, back = row_tables()
    th, tl = (jnp.asarray(t) for t in halves(there))
    uh, ul = (jnp.asarray(t) for t in halves(back))
    there, back, twist, four, fourback = column_tables()
    ch, cl = (jnp.asarray(t) for t in halves(there))
    dh, dl = (jnp.asarray(t) for t in halves(back))
    twist = jnp.asarray(twist)
    four = jnp.asarray(four.astype(ml_dtypes.bfloat16))
    fourback = jnp.asarray(fourback.astype(ml_dtypes.bfloat16))

    block = jax.ShapeDtypeStruct((16, 48, 128), F32)

    first = pl.pallas_call(
        first_kernel, out_shape=(block, jax.ShapeDtypeStruct((8, 128), F32)),
        in_specs=[HBM] * 9, out_specs=(VMEM, VMEM),
        scratch_shapes=[
            pltpu.SMEM(connectivity.shape, jnp.int32), pltpu.SMEM(displacements.shape[::-1], F32),
            pltpu.VMEM((128, 128), jnp.int32), pltpu.VMEM((128, 128), jnp.int32),
            pltpu.VMEM((768, 128), F32), pltpu.VMEM((512, 512), BF16), pltpu.VMEM((512, 512), BF16),
            pltpu.VMEM((128, 128), BF16), pltpu.VMEM((128, 128), BF16),
            pltpu.SemaphoreType.DMA((9,)), *plane_scratch(),
        ],
        compiler_params=params(), cost_estimate=cost(400_000_000, 2_000_000), name="first",
    )
    columns = pl.pallas_call(
        column_kernel, out_shape=block,
        in_specs=[VMEM] * 8, out_specs=VMEM,
        scratch_shapes=[
            pltpu.VMEM((128, 768), BF16), pltpu.VMEM((128, 768), BF16),
            pltpu.VMEM((384, 256), BF16), pltpu.VMEM((384, 256), BF16),
        ],
        compiler_params=params(), cost_estimate=cost(400_000_000, 2_000_000), name="columns",
    )
    middle = pl.pallas_call(
        middle_kernel, out_shape=(block, jax.ShapeDtypeStruct((192, 512), F32)),
        in_specs=[VMEM] * 13, out_specs=(VMEM, VMEM),
        scratch_shapes=plane_scratch(), compiler_params=params(),
        cost_estimate=cost(800_000_000, 4_000_000), name="middle",
    )
    last = pl.pallas_call(
        last_kernel, out_shape=jax.ShapeDtypeStruct((SLABS, 1, 128), F32),
        in_specs=[VMEM] * 8, out_specs=VMEM,
        scratch_shapes=plane_scratch(), compiler_params=params(),
        cost_estimate=cost(400_000_000, 2_000_000), name="last",
    )
    totals = pl.pallas_call(
        totals_kernel,
        out_shape=(
            jax.ShapeDtypeStruct((points, 1, 128), F32), jax.ShapeDtypeStruct((1, 6), F32),
            jax.ShapeDtypeStruct((6, 1, 6), F32),
        ),
        in_specs=[VMEM], out_specs=(VMEM, VMEM, VMEM), compiler_params=params(),
        cost_estimate=cost(10_000, 50_000), name="totals",
    )
    assembly = pl.pallas_call(
        functools.partial(assembly_kernel, points),
        out_shape=(jax.ShapeDtypeStruct((60, 60), F32), jax.ShapeDtypeStruct((3, 20), F32)),
        in_specs=[SMEM, VMEM], out_specs=(VMEM, VMEM), compiler_params=params(),
        cost_estimate=cost(10_000_000, 200_000), name="assembly",
    )

    def apply_columns(array):
        received = exchange(array)
        return exchange(columns(received, ch, cl, dh, dl, twist, four, fourback))

    operands = (connectivity, displacements.T, phases, flags, plastic, wh, wl, th, tl)
    spectrum, macro = first(
        *(pltpu.with_memory_space_constraint(operand, pltpu.HBM) for operand in operands)
    )
    planes = apply_columns(spectrum)
    spectrum, elastic = middle(
        macro, phases, flags, plastic, planes, vh, vl, uh, ul, wh, wl, th, tl
    )
    planes = apply_columns(spectrum)
    partial = last(phases, flags, elastic, planes, vh, vl, uh, ul)
    everyone, stress, tangent = totals(exchange(partial))
    everyone = lax.all_to_all(everyone, "rve", 0, 0, tiled=True)
    stiffness, forces = assembly(connectivity, everyone)
    return (stress, jnp.transpose(tangent, (1, 0, 2)), forces.T, stiffness)


def solution(mesh):
    return jax.shard_map(
        on_device,
        mesh=mesh,
        in_specs=(
            P("slab", None),
            P("rve", None, "slab", None),
            P("rve", None, "slab", None),
            P(),
            P(),
        ),
        out_specs=(P("rve", None), P("rve", None, None), P(), P()),
        check_vma=False,
    )
```

```python
import functools
import math

import jax
import jax.numpy as jnp
import ml_dtypes
import numpy as np
from jax import lax
from jax.experimental import pallas as pl
from jax.experimental.pallas import tpu as pltpu
from jax.sharding import PartitionSpec as P

GRID = 64
ITERS = 2
SLABS = 16
PLANES = GRID // SLABS
KEPT = GRID // 2

SHEAR_MODULUS = 80.0
BULK_MODULUS = 160.0
REFERENCE_SHEAR = 80.0
REFERENCE_LAME = 160.0 - 160.0 / 3.0
TANGENT_UNIT = 100.0
QUADRATURE_WEIGHT = 0.125
PAIR_WEIGHTS = (1.0, 1.0, 1.0, 2.0, 2.0, 2.0)
TENSOR_PAIRS = ((0, 0), (1, 1), (2, 2), (1, 2), (0, 2), (0, 1))
TENSOR_ROWS = ((0, 5, 4), (5, 1, 3), (4, 3, 2))
VOXELS = float(GRID**3)
GAUSS_LOW = 0.5 - 0.5 / math.sqrt(3.0)
GAUSS_HIGH = 0.5 + 0.5 / math.sqrt(3.0)
OUTER_AT = 8


def halves(table):
    high = table.astype(np.float32).astype(ml_dtypes.bfloat16)
    low = (table - high.astype(np.float64)).astype(np.float32).astype(ml_dtypes.bfloat16)
    return high, low


def depth_tables():
    z = np.arange(GRID)
    k = np.arange(KEPT)
    theta = 2.0 * np.pi * np.outer(z, k) / GRID
    forward = np.stack([np.cos(theta), -np.sin(theta)], axis=0)
    weight = np.where(k == 0, 1.0, 2.0) / VOXELS
    inverse = forward * weight[None, None, :]
    planes = np.eye(PLANES)
    pair = np.eye(2)
    there = np.einsum("lL,rR,pzk->lrzRpLk", planes, pair, forward)
    back = np.einsum("lL,rR,pzk->RpLklrz", planes, pair, inverse)
    return there.reshape(512, 512), back.reshape(512, 512)


def row_tables():
    y = 2 * np.arange(32)[None, :] + np.arange(2)[:, None]
    ky = 4 * np.arange(16)[:, None] + np.arange(4)[None, :]
    theta = 2.0 * np.pi * np.einsum("de,rm->derm", ky, y) / GRID
    c, s = np.cos(theta), np.sin(theta)
    there = np.zeros((16, 2, 4, 2, 2, 32))
    there[:, 0, :, :, 0, :] = c
    there[:, 0, :, :, 1, :] = s
    there[:, 1, :, :, 0, :] = -s
    there[:, 1, :, :, 1, :] = c
    back = np.zeros((2, 2, 32, 16, 2, 4))
    ct, st = np.einsum("derm->rmde", c), np.einsum("derm->rmde", s)
    back[:, 0, :, :, 0, :] = ct
    back[:, 0, :, :, 1, :] = -st
    back[:, 1, :, :, 0, :] = st
    back[:, 1, :, :, 1, :] = ct
    return there.reshape(128, 128), back.reshape(128, 128)


def column_tables():
    d = np.arange(16)
    theta = 2.0 * np.pi * np.outer(d, d) / 16.0
    c, s = np.cos(theta), np.sin(theta)
    same = np.eye(4)
    there = np.zeros((2, 16, 4, 16, 2, 4))
    there[0, :, :, :, 0, :] = np.einsum("bd,ef->bedf", c, same)
    there[0, :, :, :, 1, :] = np.einsum("bd,ef->bedf", s, same)
    there[1, :, :, :, 0, :] = np.einsum("bd,ef->bedf", -s, same)
    there[1, :, :, :, 1, :] = np.einsum("bd,ef->bedf", c, same)
    there = there.reshape(128, 128)
    phi = 2.0 * np.pi * np.outer(np.arange(16), np.arange(4)) / GRID
    twist = np.stack([np.cos(phi), np.sin(phi)])[:, :, None, :, None]
    twist = np.broadcast_to(twist, (2, 16, 4, 4, KEPT)).reshape(2, 64, 128)
    quarter = 2.0 * np.pi * np.outer(np.arange(4), np.arange(4)) / 4.0
    cq, sq = np.rint(np.cos(quarter)), np.rint(np.sin(quarter))
    kept = np.eye(KEPT)
    four = np.zeros((2, 4, KEPT, 2, 4, KEPT))
    four[0, :, :, 0] = np.einsum("la,kK->lkaK", cq, kept)
    four[1, :, :, 0] = np.einsum("la,kK->lkaK", sq, kept)
    four[0, :, :, 1] = np.einsum("la,kK->lkaK", -sq, kept)
    four[1, :, :, 1] = np.einsum("la,kK->lkaK", cq, kept)
    four = four.reshape(256, 256)
    return there, there.T.copy(), twist.astype(np.float32), four, four.T.copy()


def split(x):
    high = x.astype(jnp.bfloat16)
    low = (x - high.astype(jnp.float32)).astype(jnp.bfloat16)
    return high, low


def mm(a, b):
    return jnp.dot(a, b, preferred_element_type=jnp.float32)


def data_by_table(high, low, table_high, table_low):
    return mm(high, table_high) + (mm(low, table_high) + mm(high, table_low))


def table_by_data(table_high, table_low, high, low):
    return mm(table_high, high) + (mm(table_low, high) + mm(table_high, low))


def slopes_of(bits, low, high):
    at = [jnp.where(bit == 1, high, low) for bit in bits]
    far = [jnp.where(bit == 1, low, high) for bit in bits]

    def slope(corner, axis):
        value = None
        for other in range(3):
            if other != axis:
                factor = at[other] if corner >> other & 1 else far[other]
                value = factor if value is None else value * factor
        return value if corner >> axis & 1 else -value

    return slope


def macro_strain(point, conn_ref, disp_ref):
    low, high = jnp.float32(GAUSS_LOW), jnp.float32(GAUSS_HIGH)
    bits = [lax.bitwise_and(lax.shift_right_logical(point, d), 1) for d in range(3)]
    slope = slopes_of(bits, low, high)
    element = lax.shift_right_logical(point, 3)
    grad = [[jnp.float32(0.0)] * 3 for _ in range(3)]
    for corner in range(8):
        node = conn_ref[element, corner]
        for k in range(3):
            u = disp_ref[k, node]
            for d in range(3):
                grad[k][d] = grad[k][d] + slope(corner, d) * u
    strain = []
    for i, j in TENSOR_PAIRS:
        strain.append(grad[i][i] if i == j else 0.5 * (grad[i][j] + grad[j][i]))
    return strain


def material(elastic, phases, flags):
    hard = phases == 1
    limit = jnp.where(hard, 1.2, 0.3)
    ratio = jnp.where(
        hard,
        3.0 * SHEAR_MODULUS / (3.0 * SHEAR_MODULUS + 10.0),
        3.0 * SHEAR_MODULUS / (3.0 * SHEAR_MODULUS + 2.0),
    )
    active = flags.astype(jnp.float32)
    volume = elastic[0] + elastic[1] + elastic[2]
    third = volume * (1.0 / 3.0)
    trial = [2.0 * SHEAR_MODULUS * (elastic[a] - third) for a in range(3)]
    trial += [2.0 * SHEAR_MODULUS * elastic[a] for a in range(3, 6)]
    normal = trial[0] * trial[0] + trial[1] * trial[1] + trial[2] * trial[2]
    shear = trial[3] * trial[3] + trial[4] * trial[4] + trial[5] * trial[5]
    equivalent = jnp.sqrt(1.5 * (normal + 2.0 * shear))
    bounded = jnp.maximum(equivalent, limit)
    inverse = 1.0 / bounded
    scaled = ratio * active
    softening = 1.0 - scaled * (equivalent - limit) * inverse
    pressure = BULK_MODULUS * volume
    stress = [trial[a] * softening + pressure for a in range(3)]
    stress += [trial[a] * softening for a in range(3, 6)]
    weight = 3.0 * SHEAR_MODULUS * scaled * limit * (inverse * inverse * inverse)
    return stress, trial, softening, weight


def every_fourth(ref, start, plane):
    return ref[pl.ds(start + plane, 32, stride=4), :]


def put_split(high_ref, low_ref, rows, cols, value):
    high, low = split(value)
    high_ref[rows, cols] = high
    low_ref[rows, cols] = low


def forward_planes(xh, xl, bh, bl, wh, wl, th, tl, out_ref):
    turned = data_by_table(xh[...], xl[...], wh[...], wl[...])
    for c in range(6):
        for s in range(4):
            block = turned[c * 32 : (c + 1) * 32, s * 128 : (s + 1) * 128]
            put_split(bh, bl, pl.ds(s * 32, 32), pl.ds(c * 128, 128), block)
    spectrum = table_by_data(th[...], tl[...], bh[...], bl[...])
    for c in range(6):
        out_ref[:, c * 8 : (c + 1) * 8, :] = spectrum[:, c * 128 : (c + 1) * 128].reshape(
            16, 8, 128
        )


def load_columns(in_ref, bh, bl):
    for c in range(6):
        block = in_ref[:, c * 8 : (c + 1) * 8, :].reshape(128, 128)
        put_split(bh, bl, slice(None), pl.ds(c * 128, 128), block)


def backward_planes(in_ref, xh, xl, bh, bl, wh, wl, th, tl):
    load_columns(in_ref, bh, bl)
    rows = table_by_data(th[...], tl[...], bh[...], bl[...])
    for c in range(6):
        for s in range(4):
            block = rows[s * 32 : (s + 1) * 32, c * 128 : (c + 1) * 128]
            put_split(xh, xl, pl.ds(c * 32, 32), pl.ds(s * 128, 128), block)
    return data_by_table(xh[...], xl[...], wh[...], wl[...])


def first_kernel(
    conn_hbm, disp_hbm, phase_hbm, flag_hbm, plastic_hbm, wh_hbm, wl_hbm, th_hbm, tl_hbm,
    out_ref, macro_ref,
    conn_ref, disp_ref, phase_ref, flag_ref, plastic_ref, wh, wl, th, tl, sems, xh, xl, bh, bl,
):
    pairs = (
        (conn_hbm, conn_ref), (disp_hbm, disp_ref), (plastic_hbm, plastic_ref),
        (phase_hbm, phase_ref), (flag_hbm.at[pl.ds(0, 128)], flag_ref),
        (wh_hbm, wh), (wl_hbm, wl), (th_hbm, th), (tl_hbm, tl),
    )
    copies = [pltpu.make_async_copy(a, b, sems.at[i]) for i, (a, b) in enumerate(pairs)]
    for copy in copies:
        copy.start()
    for copy in copies[:2]:
        copy.wait()
    macro = macro_strain(lax.axis_index("rve"), conn_ref, disp_ref)
    row = lax.broadcasted_iota(jnp.int32, (8, 128), 0)
    table = jnp.zeros((8, 128), jnp.float32)
    for c in range(6):
        table = jnp.where(row == c, macro[c], table)
    macro_ref[...] = table
    for copy in copies[2:5]:
        copy.wait()
    for plane in range(PLANES):
        elastic = [macro[c] - every_fourth(plastic_ref, c * 128, plane) for c in range(6)]
        phases = every_fourth(phase_ref, 0, plane)
        flags = every_fourth(flag_ref, 0, plane)
        stress = material(elastic, phases, flags)[0]
        for c in range(6):
            put_split(xh, xl, pl.ds(c * 32, 32), pl.ds(plane * 128, 128), stress[c])
    for copy in copies[5:]:
        copy.wait()
    forward_planes(xh, xl, bh, bl, wh, wl, th, tl, out_ref)


def middle_kernel(
    macro_ref, phase_ref, flag_ref, plastic_ref, in_ref,
    vh, vl, uh, ul, wh, wl, th, tl, out_ref, elastic_ref, xh, xl, bh, bl,
):
    macro = [macro_ref[c : c + 1, :] for c in range(6)]
    correction = backward_planes(in_ref, xh, xl, bh, bl, vh, vl, uh, ul)
    for plane in range(PLANES):
        lanes = slice(plane * 128, (plane + 1) * 128)
        elastic = []
        for c in range(6):
            before = macro[c] - every_fourth(plastic_ref, c * 128, plane)
            after = before - correction[c * 32 : (c + 1) * 32, lanes]
            elastic_ref[c * 32 : (c + 1) * 32, lanes] = after
            elastic.append(after)
        phases = every_fourth(phase_ref, 0, plane)
        flags = every_fourth(flag_ref, 128, plane)
        stress = material(elastic, phases, flags)[0]
        for c in range(6):
            put_split(xh, xl, pl.ds(c * 32, 32), pl.ds(plane * 128, 128), stress[c])
    forward_planes(xh, xl, bh, bl, wh, wl, th, tl, out_ref)


def last_kernel(
    phase_ref, flag_ref, elastic_ref, in_ref, vh, vl, uh, ul, out_ref, xh, xl, bh, bl
):
    correction = backward_planes(in_ref, xh, xl, bh, bl, vh, vl, uh, ul)
    sums = [None] * 28

    def collect(at, value):
        part = value.reshape(4, 8, 128)
        part = (part[0] + part[1]) + (part[2] + part[3])
        sums[at] = part if sums[at] is None else sums[at] + part

    for plane in range(PLANES):
        lanes = slice(plane * 128, (plane + 1) * 128)
        elastic = [
            elastic_ref[c * 32 : (c + 1) * 32, lanes] - correction[c * 32 : (c + 1) * 32, lanes]
            for c in range(6)
        ]
        phases = every_fourth(phase_ref, 0, plane)
        flags = every_fourth(flag_ref, 256, plane)
        stress, trial, softening, weight = material(elastic, phases, flags)
        for c in range(6):
            collect(c, stress[c])
        collect(6, softening)
        at = 7
        for a in range(6):
            scaled = weight * trial[a]
            for b in range(a, 6):
                collect(at, scaled * trial[b])
                at += 1
    row = lax.broadcasted_iota(jnp.int32, (128, 128), 0)
    lines = jnp.zeros((128, 128), jnp.float32)

    def place(at, value):
        return jnp.where(row == at, jnp.broadcast_to(value, (128, 128)), lines)

    totals = [jnp.sum(value, axis=0, keepdims=True) for value in sums]
    for c in range(7):
        lines = place(c, totals[c])
    at = 7
    for a in range(6):
        for b in range(a, 6):
            lines = place(OUTER_AT + 6 * a + b, totals[at])
            if a != b:
                lines = place(OUTER_AT + 6 * b + a, totals[at])
            at += 1
    ones = jnp.ones((SLABS, 128), jnp.float32)
    line = lax.dot_general(
        ones, lines, (((1,), (1,)), ((), ())),
        precision=lax.Precision.HIGHEST, preferred_element_type=jnp.float32,
    )
    out_ref[...] = line.reshape(SLABS, 1, 128)


def column_kernel(in_ref, th, tl, bh_table, bl_table, twist_ref, four, fourback, out_ref, bh, bl, yh, yl):
    load_columns(in_ref, bh, bl)
    mixed = table_by_data(th[...], tl[...], bh[...], bl[...])
    cosine, sine = twist_ref[0], twist_ref[1]
    for c in range(6):
        lanes = slice(c * 128, (c + 1) * 128)
        real, imag = mixed[:64, lanes], mixed[64:, lanes]
        rows = pl.ds(c * 64, 64)
        put_split(yh, yl, rows, pl.ds(0, 128), real * cosine + imag * sine)
        put_split(yh, yl, rows, pl.ds(128, 128), imag * cosine - real * sine)
    spectrum = mm(yh[...], four[...]) + mm(yl[...], four[...])
    tau = [spectrum[c * 64 : (c + 1) * 64] for c in range(6)]

    shape = (64, 256)
    row = lax.broadcasted_iota(jnp.int32, shape, 0)
    lane = lax.broadcasted_iota(jnp.int32, shape, 1)
    lane = lax.bitwise_and(lane, 127)
    kx = 16 * lax.shift_right_logical(lane, 5) + lax.shift_right_logical(row, 2)
    ky = 4 * lax.axis_index("slab") + lax.bitwise_and(row, 3)
    kz = lax.bitwise_and(lane, 31)
    half = GRID // 2
    keep = (kx != half) & (ky != half) & (kx + ky + kz > 0)
    xi = [
        jnp.where(kx < half, kx, kx - GRID).astype(jnp.float32),
        jnp.where(ky < half, ky, ky - GRID).astype(jnp.float32),
        kz.astype(jnp.float32),
    ]
    length = xi[0] * xi[0] + xi[1] * xi[1] + xi[2] * xi[2]
    inverse = jnp.where(keep, 1.0 / jnp.maximum(length, 1.0), 0.0)
    coupling = (REFERENCE_LAME + REFERENCE_SHEAR) / (
        REFERENCE_SHEAR * (REFERENCE_LAME + 2.0 * REFERENCE_SHEAR)
    )
    scaled = inverse * (1.0 / (2.0 * REFERENCE_SHEAR))
    traction = [
        tau[r[0]] * xi[0] + tau[r[1]] * xi[1] + tau[r[2]] * xi[2] for r in TENSOR_ROWS
    ]
    load = xi[0] * traction[0] + xi[1] * traction[1] + xi[2] * traction[2]
    load = load * (inverse * (REFERENCE_SHEAR * coupling))
    field = [scaled * (traction[i] - xi[i] * load) for i in range(3)]
    for c, (i, k) in enumerate(TENSOR_PAIRS):
        entry = xi[i] * field[k] + xi[k] * field[i]
        put_split(yh, yl, pl.ds(c * 64, 64), slice(None), entry)
    turned = mm(yh[...], fourback[...]) + mm(yl[...], fourback[...])
    for c in range(6):
        real, imag = turned[c * 64 : (c + 1) * 64, :128], turned[c * 64 : (c + 1) * 64, 128:]
        cols = pl.ds(c * 128, 128)
        put_split(bh, bl, pl.ds(0, 64), cols, real * cosine - imag * sine)
        put_split(bh, bl, pl.ds(64, 64), cols, real * sine + imag * cosine)
    result = table_by_data(bh_table[...], bl_table[...], bh[...], bl[...])
    for c in range(6):
        out_ref[:, c * 8 : (c + 1) * 8, :] = result[:, c * 128 : (c + 1) * 128].reshape(16, 8, 128)


def totals_kernel(in_ref, all_ref, stress_ref, tangent_ref):
    line = jnp.sum(in_ref[...].reshape(SLABS, 128), axis=0, keepdims=True)
    all_ref[...] = jnp.broadcast_to(line[None], all_ref.shape)
    line = line * (1.0 / VOXELS)
    stress_ref[...] = line[:, :6]
    at = lax.broadcasted_iota(jnp.int32, (1, 128), 1) - OUTER_AT
    a = at // 6
    b = at - 6 * a
    both = (a < 3) & (b < 3)
    shear = jnp.broadcast_to(line[:, 6:7], (1, 128)) * (2.0 * SHEAR_MODULUS)
    fixed = jnp.where(both, BULK_MODULUS - shear * (1.0 / 3.0), 0.0)
    fixed = fixed + jnp.where(a == b, shear, 0.0)
    whole = (fixed - line * jnp.where(b < 3, 1.0, 2.0)) * (1.0 / TANGENT_UNIT)
    for i in range(6):
        tangent_ref[i] = whole[:, OUTER_AT + 6 * i : OUTER_AT + 6 * i + 6]


def assembly_kernel(points, conn_ref, in_ref, stiffness_ref, forces_ref):
    half = points // 2
    sums = in_ref[...].reshape(points, 128) * (1.0 / VOXELS)
    sums = jnp.concatenate([sums[half:], sums[:half]], axis=0)
    shape = (points, 128)
    lane = lax.broadcasted_iota(jnp.int32, shape, 1)
    point = lax.broadcasted_iota(jnp.int32, shape, 0)
    element = lax.shift_right_logical(point, 3)
    bits = [lax.bitwise_and(lax.shift_right_logical(point, d), 1) for d in range(3)]
    slope = slopes_of(bits, GAUSS_LOW, GAUSS_HIGH)
    node = lane // 3
    part = lane - 3 * node
    elements = conn_ref.shape[0]
    grad = [jnp.zeros(shape, jnp.float32) for _ in range(3)]
    for corner in range(8):
        owner = jnp.full(shape, conn_ref[0, corner], jnp.int32)
        for e in range(1, elements):
            owner = jnp.where(element == e, conn_ref[e, corner], owner)
        here = (owner == node) & (lane < 60)
        for d in range(3):
            grad[d] = grad[d] + jnp.where(here, slope(corner, d), 0.0)
    basis = []
    for i, k in TENSOR_PAIRS:
        if i == k:
            basis.append(jnp.where(part == i, grad[i], 0.0))
        else:
            value = jnp.where(part == i, 0.5 * grad[k], 0.0)
            basis.append(value + jnp.where(part == k, 0.5 * grad[i], 0.0))
    mean_shear = 2.0 * SHEAR_MODULUS * sums[:, 6:7]

    def column(at):
        return jnp.broadcast_to(sums[:, at : at + 1], shape)

    mean_shear = jnp.broadcast_to(mean_shear, shape)
    on_diagonal = BULK_MODULUS + mean_shear * (2.0 / 3.0)
    off_diagonal = BULK_MODULUS - mean_shear * (1.0 / 3.0)
    answers = []
    force = jnp.zeros(shape, jnp.float32)
    scale = QUADRATURE_WEIGHT / TANGENT_UNIT
    for a in range(6):
        total = jnp.zeros(shape, jnp.float32)
        for b in range(6):
            low, high = min(a, b), max(a, b)
            entry = -PAIR_WEIGHTS[b] * column(OUTER_AT + 6 * low + high)
            if a == b:
                entry = entry + (on_diagonal if a < 3 else mean_shear)
            elif a < 3 and b < 3:
                entry = entry + off_diagonal
            total = total + entry * basis[b]
        answers.append(total * (PAIR_WEIGHTS[a] * scale))
        force = force + basis[a] * (column(a) * (PAIR_WEIGHTS[a] * QUADRATURE_WEIGHT))
    left = jnp.concatenate(basis, axis=0)
    right = jnp.concatenate(answers, axis=0)
    whole = lax.dot_general(
        left, right, (((0,), (0,)), ((), ())),
        precision=lax.Precision.HIGHEST, preferred_element_type=jnp.float32,
    )
    stiffness_ref[...] = whole[:60, :60]
    line = jnp.sum(force, axis=0, keepdims=True)
    part8 = lax.broadcasted_iota(jnp.int32, (8, 128), 0)
    lane8 = lax.broadcasted_iota(jnp.int32, (8, 128), 1)
    spread = jnp.where(lane8 % 3 == part8, jnp.broadcast_to(line, (8, 128)), 0.0)
    pick_row = lax.broadcasted_iota(jnp.int32, (128, 128), 0)
    pick_col = lax.broadcasted_iota(jnp.int32, (128, 128), 1)
    pick = (pick_row // 3 == pick_col).astype(jnp.float32)
    forces = jnp.dot(
        spread, pick, precision=lax.Precision.HIGHEST, preferred_element_type=jnp.float32
    )
    forces_ref[...] = forces[:3, :20]


SMEM = pl.BlockSpec(memory_space=pltpu.SMEM)
VMEM = pl.BlockSpec(memory_space=pltpu.VMEM)
HBM = pl.BlockSpec(memory_space=pltpu.HBM)
BF16 = jnp.bfloat16
F32 = jnp.float32
LIMIT = 16 * 1024 * 1024


def params():
    return pltpu.CompilerParams(vmem_limit_bytes=LIMIT)


def cost(flops, size):
    return pl.CostEstimate(flops=flops, bytes_accessed=size, transcendentals=0)


def plane_scratch():
    return [
        pltpu.VMEM((192, 512), BF16),
        pltpu.VMEM((192, 512), BF16),
        pltpu.VMEM((128, 768), BF16),
        pltpu.VMEM((128, 768), BF16),
    ]


def exchange(array):
    return lax.all_to_all(array, "slab", split_axis=0, concat_axis=0, tiled=True)


def on_device(phase_ids, yield_flags, plastic_strain, displacements, connectivity):
    points = lax.axis_size("rve")

    def rows(array):
        lead = math.prod(array.shape[:-2])
        array = array.reshape(lead, PLANES, 32, 128)
        return jnp.transpose(array, (0, 2, 1, 3)).reshape(lead * 128, 128)

    phases = rows(phase_ids)
    flags = rows(yield_flags)
    plastic = rows(plastic_strain)

    there, back = depth_tables()
    wh, wl = (jnp.asarray(t) for t in halves(there))
    vh, vl = (jnp.asarray(t) for t in halves(back))
    there, back = row_tables()
    th, tl = (jnp.asarray(t) for t in halves(there))
    uh, ul = (jnp.asarray(t) for t in halves(back))
    there, back, twist, four, fourback = column_tables()
    ch, cl = (jnp.asarray(t) for t in halves(there))
    dh, dl = (jnp.asarray(t) for t in halves(back))
    twist = jnp.asarray(twist)
    four = jnp.asarray(four.astype(ml_dtypes.bfloat16))
    fourback = jnp.asarray(fourback.astype(ml_dtypes.bfloat16))

    block = jax.ShapeDtypeStruct((16, 48, 128), F32)

    first = pl.pallas_call(
        first_kernel, out_shape=(block, jax.ShapeDtypeStruct((8, 128), F32)),
        in_specs=[HBM] * 9, out_specs=(VMEM, VMEM),
        scratch_shapes=[
            pltpu.SMEM(connectivity.shape, jnp.int32), pltpu.SMEM(displacements.shape[::-1], F32),
            pltpu.VMEM((128, 128), jnp.int32), pltpu.VMEM((128, 128), jnp.int32),
            pltpu.VMEM((768, 128), F32), pltpu.VMEM((512, 512), BF16), pltpu.VMEM((512, 512), BF16),
            pltpu.VMEM((128, 128), BF16), pltpu.VMEM((128, 128), BF16),
            pltpu.SemaphoreType.DMA((9,)), *plane_scratch(),
        ],
        compiler_params=params(), cost_estimate=cost(400_000_000, 2_000_000), name="first",
    )
    columns = pl.pallas_call(
        column_kernel, out_shape=block,
        in_specs=[VMEM] * 8, out_specs=VMEM,
        scratch_shapes=[
            pltpu.VMEM((128, 768), BF16), pltpu.VMEM((128, 768), BF16),
            pltpu.VMEM((384, 256), BF16), pltpu.VMEM((384, 256), BF16),
        ],
        compiler_params=params(), cost_estimate=cost(400_000_000, 2_000_000), name="columns",
    )
    middle = pl.pallas_call(
        middle_kernel, out_shape=(block, jax.ShapeDtypeStruct((192, 512), F32)),
        in_specs=[VMEM] * 13, out_specs=(VMEM, VMEM),
        scratch_shapes=plane_scratch(), compiler_params=params(),
        cost_estimate=cost(800_000_000, 4_000_000), name="middle",
    )
    last = pl.pallas_call(
        last_kernel, out_shape=jax.ShapeDtypeStruct((SLABS, 1, 128), F32),
        in_specs=[VMEM] * 8, out_specs=VMEM,
        scratch_shapes=plane_scratch(), compiler_params=params(),
        cost_estimate=cost(400_000_000, 2_000_000), name="last",
    )
    totals = pl.pallas_call(
        totals_kernel,
        out_shape=(
            jax.ShapeDtypeStruct((points, 1, 128), F32), jax.ShapeDtypeStruct((1, 6), F32),
            jax.ShapeDtypeStruct((6, 1, 6), F32),
        ),
        in_specs=[VMEM], out_specs=(VMEM, VMEM, VMEM), compiler_params=params(),
        cost_estimate=cost(10_000, 50_000), name="totals",
    )
    assembly = pl.pallas_call(
        functools.partial(assembly_kernel, points),
        out_shape=(jax.ShapeDtypeStruct((60, 60), F32), jax.ShapeDtypeStruct((3, 20), F32)),
        in_specs=[SMEM, VMEM], out_specs=(VMEM, VMEM), compiler_params=params(),
        cost_estimate=cost(10_000_000, 200_000), name="assembly",
    )

    def apply_columns(array):
        received = exchange(array)
        return exchange(columns(received, ch, cl, dh, dl, twist, four, fourback))

    operands = (connectivity, displacements.T, phases, flags, plastic, wh, wl, th, tl)
    spectrum, macro = first(
        *(pltpu.with_memory_space_constraint(operand, pltpu.HBM) for operand in operands)
    )
    planes = apply_columns(spectrum)
    spectrum, elastic = middle(
        macro, phases, flags, plastic, planes, vh, vl, uh, ul, wh, wl, th, tl
    )
    planes = apply_columns(spectrum)
    partial = last(phases, flags, elastic, planes, vh, vl, uh, ul)
    everyone, stress, tangent = totals(exchange(partial))
    half = points // 2
    turned = [*range(half, points), *range(half)]
    everyone = lax.all_to_all(
        everyone, "rve", 0, 0, tiled=True, axis_index_groups=[turned]
    )
    stiffness, forces = assembly(connectivity, everyone)
    return (stress, jnp.transpose(tangent, (1, 0, 2)), forces.T, stiffness)


def solution(mesh):
    return jax.shard_map(
        on_device,
        mesh=mesh,
        in_specs=(
            P("slab", None),
            P("rve", None, "slab", None),
            P("rve", None, "slab", None),
            P(),
            P(),
        ),
        out_specs=(P("rve", None), P("rve", None, None), P(), P()),
        check_vma=False,
    )
```

```python
import functools
import math

import jax
import jax.numpy as jnp
import ml_dtypes
import numpy as np
from jax import lax
from jax.experimental import pallas as pl
from jax.experimental.pallas import tpu as pltpu
from jax.sharding import PartitionSpec as P

GRID = 64
ITERS = 2
SLABS = 16
PLANES = GRID // SLABS
KEPT = GRID // 2

SHEAR_MODULUS = 80.0
BULK_MODULUS = 160.0
REFERENCE_SHEAR = 80.0
REFERENCE_LAME = 160.0 - 160.0 / 3.0
TANGENT_UNIT = 100.0
QUADRATURE_WEIGHT = 0.125
PAIR_WEIGHTS = (1.0, 1.0, 1.0, 2.0, 2.0, 2.0)
TENSOR_PAIRS = ((0, 0), (1, 1), (2, 2), (1, 2), (0, 2), (0, 1))
VOXELS = float(GRID**3)
GAUSS_LOW = 0.5 - 0.5 / math.sqrt(3.0)
GAUSS_HIGH = 0.5 + 0.5 / math.sqrt(3.0)
OUTER_AT = 8
FIELDS = 5


def halves(table):
    high = table.astype(np.float32).astype(ml_dtypes.bfloat16)
    low = (table - high.astype(np.float64)).astype(np.float32).astype(ml_dtypes.bfloat16)
    return high, low


def depth_tables():
    z = np.arange(GRID)
    k = np.arange(KEPT)
    theta = 2.0 * np.pi * np.outer(z, k) / GRID
    forward = np.stack([np.cos(theta), -np.sin(theta)], axis=0)
    weight = np.where(k == 0, 1.0, 2.0) / VOXELS
    inverse = forward * weight[None, None, :]
    pair = np.eye(2)
    there = np.einsum("rR,pzk->rzRpk", pair, forward)
    back = np.einsum("rR,pzk->Rpkrz", pair, inverse)
    return there.reshape(128, 128), back.reshape(128, 128)


def row_tables():
    y = 2 * np.arange(32)[None, :] + np.arange(2)[:, None]
    ky = 4 * np.arange(16)[:, None] + np.arange(4)[None, :]
    theta = 2.0 * np.pi * np.einsum("de,rm->derm", ky, y) / GRID
    c, s = np.cos(theta), np.sin(theta)
    there = np.zeros((16, 2, 4, 2, 2, 32))
    there[:, 0, :, :, 0, :] = c
    there[:, 0, :, :, 1, :] = s
    there[:, 1, :, :, 0, :] = -s
    there[:, 1, :, :, 1, :] = c
    back = np.zeros((2, 2, 32, 16, 2, 4))
    ct, st = np.einsum("derm->rmde", c), np.einsum("derm->rmde", s)
    back[:, 0, :, :, 0, :] = ct
    back[:, 0, :, :, 1, :] = -st
    back[:, 1, :, :, 0, :] = st
    back[:, 1, :, :, 1, :] = ct
    return there.reshape(128, 128), back.reshape(128, 128)


def column_tables():
    d = np.arange(16)
    theta = 2.0 * np.pi * np.outer(d, d) / 16.0
    c, s = np.cos(theta), np.sin(theta)
    same = np.eye(4)
    there = np.zeros((2, 16, 4, 16, 2, 4))
    there[0, :, :, :, 0, :] = np.einsum("bd,ef->bedf", c, same)
    there[0, :, :, :, 1, :] = np.einsum("bd,ef->bedf", s, same)
    there[1, :, :, :, 0, :] = np.einsum("bd,ef->bedf", -s, same)
    there[1, :, :, :, 1, :] = np.einsum("bd,ef->bedf", c, same)
    there = there.reshape(128, 128)
    phi = 2.0 * np.pi * np.outer(np.arange(16), np.arange(4)) / GRID
    twist = np.stack([np.cos(phi), np.sin(phi)])[:, :, None, :, None]
    twist = np.broadcast_to(twist, (2, 16, 4, 4, KEPT)).reshape(2, 64, 128)
    quarter = 2.0 * np.pi * np.outer(np.arange(4), np.arange(4)) / 4.0
    cq, sq = np.rint(np.cos(quarter)), np.rint(np.sin(quarter))
    kept = np.eye(KEPT)
    four = np.zeros((2, 4, KEPT, 2, 4, KEPT))
    four[0, :, :, 0] = np.einsum("la,kK->lkaK", cq, kept)
    four[1, :, :, 0] = np.einsum("la,kK->lkaK", sq, kept)
    four[0, :, :, 1] = np.einsum("la,kK->lkaK", -sq, kept)
    four[1, :, :, 1] = np.einsum("la,kK->lkaK", cq, kept)
    four = four.reshape(256, 256)
    return there, there.T.copy(), twist.astype(np.float32), four, four.T.copy()


def right_table(table):
    high, low = halves(table)
    return np.block([[high, low], [high, np.zeros_like(low)]])


def left_table(table):
    return np.ascontiguousarray(right_table(table.T).T)


def split(x):
    high = x.astype(jnp.bfloat16)
    low = (x - high.astype(jnp.float32)).astype(jnp.bfloat16)
    return high, low


def mm(a, b):
    return jnp.dot(a, b, preferred_element_type=jnp.float32)


def from_left(table_ref, data_ref):
    both = mm(table_ref[...], data_ref[...])
    return both[:128] + both[128:]


def from_right(data_ref, table_ref):
    both = mm(data_ref[...], table_ref[...])
    return both[:, :128] + both[:, 128:]


def swap_chunks(tiles):
    lane = lax.broadcasted_iota(jnp.int32, tiles[0].shape, 1)
    low = lane < 64
    even = lax.bitwise_and(lane, 32) == 0
    halfway = [None] * 4
    for i in range(2):
        first, second = tiles[i], tiles[i + 2]
        halfway[i] = jnp.where(low, first, pltpu.roll(second, 64, 1))
        halfway[i + 2] = jnp.where(low, pltpu.roll(first, 64, 1), second)
    result = []
    for i in (0, 2):
        first, second = halfway[i], halfway[i + 1]
        result.append(jnp.where(even, first, pltpu.roll(second, 32, 1)))
        result.append(jnp.where(even, pltpu.roll(first, 96, 1), second))
    return result


def slopes_of(bits, low, high):
    at = [jnp.where(bit == 1, high, low) for bit in bits]
    far = [jnp.where(bit == 1, low, high) for bit in bits]

    def slope(corner, axis):
        value = None
        for other in range(3):
            if other != axis:
                factor = at[other] if corner >> other & 1 else far[other]
                value = factor if value is None else value * factor
        return value if corner >> axis & 1 else -value

    return slope


def macro_strain(point, conn_ref, disp_ref):
    low, high = jnp.float32(GAUSS_LOW), jnp.float32(GAUSS_HIGH)
    bits = [lax.bitwise_and(lax.shift_right_logical(point, d), 1) for d in range(3)]
    slope = slopes_of(bits, low, high)
    element = lax.shift_right_logical(point, 3)
    grad = [[jnp.float32(0.0)] * 3 for _ in range(3)]
    for corner in range(8):
        node = conn_ref[element, corner]
        for k in range(3):
            u = disp_ref[k, node]
            for d in range(3):
                grad[k][d] = grad[k][d] + slope(corner, d) * u
    strain = []
    for i, j in TENSOR_PAIRS:
        strain.append(grad[i][i] if i == j else 0.5 * (grad[i][j] + grad[j][i]))
    return strain


def material(elastic, phases, flags):
    hard = phases == 1
    limit = jnp.where(hard, 1.2, 0.3)
    ratio = jnp.where(
        hard,
        3.0 * SHEAR_MODULUS / (3.0 * SHEAR_MODULUS + 10.0),
        3.0 * SHEAR_MODULUS / (3.0 * SHEAR_MODULUS + 2.0),
    )
    active = flags.astype(jnp.float32)
    volume = elastic[0] + elastic[1] + elastic[2]
    third = volume * (1.0 / 3.0)
    trial = [2.0 * SHEAR_MODULUS * (elastic[a] - third) for a in range(3)]
    trial += [2.0 * SHEAR_MODULUS * elastic[a] for a in range(3, 6)]
    normal = trial[0] * trial[0] + trial[1] * trial[1] + trial[2] * trial[2]
    shear = trial[3] * trial[3] + trial[4] * trial[4] + trial[5] * trial[5]
    equivalent = jnp.sqrt(1.5 * (normal + 2.0 * shear))
    bounded = jnp.maximum(equivalent, limit)
    inverse = 1.0 / bounded
    scaled = ratio * active
    softening = 1.0 - scaled * (equivalent - limit) * inverse
    pressure = BULK_MODULUS * volume
    stress = [trial[a] * softening + pressure for a in range(3)]
    stress += [trial[a] * softening for a in range(3, 6)]
    weight = 3.0 * SHEAR_MODULUS * scaled * limit * (inverse * inverse * inverse)
    return stress, trial, softening, weight


def every_fourth(ref, start, plane):
    return ref[pl.ds(start + plane, 32, stride=4), :]


def put_rows(ref, rows, value):
    high, low = split(value)
    ref[rows, 0:128] = high
    ref[rows, 128:256] = low


def put_columns(ref, start, count, columns, value):
    high, low = split(value)
    ref[pl.ds(start, count), columns] = high
    ref[pl.ds(128 + start, count), columns] = low


def plane_waves():
    row = lax.broadcasted_iota(jnp.int32, (128, 128), 0)
    lane = lax.broadcasted_iota(jnp.int32, (128, 128), 1)
    ky = 4 * lax.shift_right_logical(row, 3) + lax.bitwise_and(row, 3)
    ky = jnp.where(ky < GRID // 2, ky, ky - GRID)
    return ky.astype(jnp.float32), lax.bitwise_and(lane, 31).astype(jnp.float32)


def forward_planes(xs, bs, depth, rows, out_ref):
    turned = from_right(xs, depth)
    tiles = swap_chunks([turned[l * 192 : (l + 1) * 192] for l in range(PLANES)])
    for c in range(6):
        for s in range(4):
            block = tiles[s][c * 32 : (c + 1) * 32]
            put_columns(bs, s * 32, 32, pl.ds(c * 128, 128), block)
    spectrum = from_left(rows, bs)
    xx, yy, zz, yz, xz, xy = (spectrum[:, c * 128 : (c + 1) * 128] for c in range(6))
    wave_y, wave_z = plane_waves()
    fields = (xx, xy, xz, wave_y * yy + wave_z * yz, wave_y * yz + wave_z * zz)
    for c, field in enumerate(fields):
        out_ref[:, c * 8 : (c + 1) * 8, :] = field.reshape(16, 8, 128)


def backward_planes(in_ref, bs, xs, depth, rows):
    xx, xy, xz, y, z = (
        in_ref[:, c * 8 : (c + 1) * 8, :].reshape(128, 128) for c in range(FIELDS)
    )
    wave_y, wave_z = plane_waves()
    yy, zz = 2.0 * (wave_y * y), 2.0 * (wave_z * z)
    for c, value in enumerate((xx, yy, zz, wave_y * z + wave_z * y, xz, xy)):
        put_columns(bs, 0, 128, pl.ds(c * 128, 128), value)
    lines = from_left(rows, bs)
    tiles = [
        jnp.concatenate(
            [lines[s * 32 : (s + 1) * 32, c * 128 : (c + 1) * 128] for c in range(6)], axis=0
        )
        for s in range(4)
    ]
    for l, tile in enumerate(swap_chunks(tiles)):
        put_rows(xs, pl.ds(l * 192, 192), tile)
    return from_right(xs, depth)


def basis_of(points, conn_ref):
    shape = (points, 128)
    lane = lax.broadcasted_iota(jnp.int32, shape, 1)
    point = lax.broadcasted_iota(jnp.int32, shape, 0)
    element = lax.shift_right_logical(point, 3)
    bits = [lax.bitwise_and(lax.shift_right_logical(point, d), 1) for d in range(3)]
    slope = slopes_of(bits, GAUSS_LOW, GAUSS_HIGH)
    node = lane // 3
    part = lane - 3 * node
    elements = conn_ref.shape[0]
    grad = [jnp.zeros(shape, jnp.float32) for _ in range(3)]
    for corner in range(8):
        owner = jnp.full(shape, conn_ref[0, corner], jnp.int32)
        for e in range(1, elements):
            owner = jnp.where(element == e, conn_ref[e, corner], owner)
        here = (owner == node) & (lane < 60)
        for d in range(3):
            grad[d] = grad[d] + jnp.where(here, slope(corner, d), 0.0)
    basis = []
    for i, k in TENSOR_PAIRS:
        if i == k:
            basis.append(jnp.where(part == i, grad[i], 0.0))
        else:
            value = jnp.where(part == i, 0.5 * grad[k], 0.0)
            basis.append(value + jnp.where(part == k, 0.5 * grad[i], 0.0))
    return jnp.concatenate(basis, axis=0)


def first_kernel(
    points, conn_hbm, disp_hbm, phase_hbm, flag_hbm, plastic_hbm, depth_hbm, rows_hbm,
    out_ref, macro_ref, basis_ref, turned_ref,
    conn_ref, disp_ref, phase_ref, flag_ref, plastic_ref, depth, rows, sems, xs, bs,
):
    pairs = (
        (conn_hbm, conn_ref), (disp_hbm, disp_ref), (plastic_hbm, plastic_ref),
        (phase_hbm, phase_ref), (flag_hbm.at[pl.ds(0, 128)], flag_ref),
        (depth_hbm, depth), (rows_hbm, rows),
    )
    copies = [pltpu.make_async_copy(a, b, sems.at[i]) for i, (a, b) in enumerate(pairs)]
    for copy in copies:
        copy.start()
    for copy in copies[:2]:
        copy.wait()
    macro = macro_strain(lax.axis_index("rve"), conn_ref, disp_ref)
    row = lax.broadcasted_iota(jnp.int32, (8, 128), 0)
    table = jnp.zeros((8, 128), jnp.float32)
    for c in range(6):
        table = jnp.where(row == c, macro[c], table)
    macro_ref[...] = table
    basis = basis_of(points, conn_ref)
    basis_ref[...] = basis
    high, low = split(jnp.transpose(basis))
    turned_ref[0] = high
    turned_ref[1] = low
    for copy in copies[2:5]:
        copy.wait()
    for plane in range(PLANES):
        elastic = [macro[c] - every_fourth(plastic_ref, c * 128, plane) for c in range(6)]
        phases = every_fourth(phase_ref, 0, plane)
        flags = every_fourth(flag_ref, 0, plane)
        stress = material(elastic, phases, flags)[0]
        for c in range(6):
            put_rows(xs, pl.ds(plane * 192 + c * 32, 32), stress[c])
    for copy in copies[5:]:
        copy.wait()
    forward_planes(xs, bs, depth, rows, out_ref)


def middle_kernel(
    macro_ref, phase_ref, flag_ref, plastic_ref, in_ref, back_depth, back_rows, depth, rows,
    out_ref, elastic_ref, xs, bs,
):
    macro = [macro_ref[c : c + 1, :] for c in range(6)]
    correction = backward_planes(in_ref, bs, xs, back_depth, back_rows)
    for plane in range(PLANES):
        elastic = []
        for c in range(6):
            at = plane * 192 + c * 32
            before = macro[c] - every_fourth(plastic_ref, c * 128, plane)
            after = before - correction[at : at + 32]
            elastic_ref[at : at + 32, :] = after
            elastic.append(after)
        phases = every_fourth(phase_ref, 0, plane)
        flags = every_fourth(flag_ref, 128, plane)
        stress = material(elastic, phases, flags)[0]
        for c in range(6):
            put_rows(xs, pl.ds(plane * 192 + c * 32, 32), stress[c])
    forward_planes(xs, bs, depth, rows, out_ref)


def last_kernel(
    phase_ref, flag_ref, elastic_ref, in_ref, back_depth, back_rows, out_ref, xs, bs
):
    correction = backward_planes(in_ref, bs, xs, back_depth, back_rows)
    sums = [None] * 28

    def collect(at, value):
        part = value.reshape(4, 8, 128)
        part = (part[0] + part[1]) + (part[2] + part[3])
        sums[at] = part if sums[at] is None else sums[at] + part

    for plane in range(PLANES):
        starts = [plane * 192 + c * 32 for c in range(6)]
        elastic = [elastic_ref[at : at + 32, :] - correction[at : at + 32] for at in starts]
        phases = every_fourth(phase_ref, 0, plane)
        flags = every_fourth(flag_ref, 256, plane)
        stress, trial, softening, weight = material(elastic, phases, flags)
        for c in range(6):
            collect(c, stress[c])
        collect(6, softening)
        at = 7
        for a in range(6):
            scaled = weight * trial[a]
            for b in range(a, 6):
                collect(at, scaled * trial[b])
                at += 1
    row = lax.broadcasted_iota(jnp.int32, (128, 128), 0)
    lines = jnp.zeros((128, 128), jnp.float32)

    def place(at, value):
        return jnp.where(row == at, jnp.broadcast_to(value, (128, 128)), lines)

    totals = [jnp.sum(value, axis=0, keepdims=True) for value in sums]
    for c in range(7):
        lines = place(c, totals[c])
    at = 7
    for a in range(6):
        for b in range(a, 6):
            lines = place(OUTER_AT + 6 * a + b, totals[at])
            if a != b:
                lines = place(OUTER_AT + 6 * b + a, totals[at])
            at += 1
    ones = jnp.ones((SLABS, 128), jnp.float32)
    line = lax.dot_general(
        ones, lines, (((1,), (1,)), ((), ())),
        precision=lax.Precision.HIGHEST, preferred_element_type=jnp.float32,
    )
    out_ref[...] = line.reshape(SLABS, 1, 128)


def column_kernel(in_ref, columns, back_columns, twist_ref, four, back_four, out_ref, bs, ys):
    count = 64 * FIELDS
    for c in range(FIELDS):
        block = in_ref[:, c * 8 : (c + 1) * 8, :].reshape(128, 128)
        put_columns(bs, 0, 128, pl.ds(c * 128, 128), block)
    mixed = from_left(columns, bs)
    cosine, sine = twist_ref[0], twist_ref[1]

    def put(c, lanes, value):
        high, low = split(value)
        ys[pl.ds(c * 64, 64), lanes] = high
        ys[pl.ds(count + c * 64, 64), lanes] = low

    for c in range(FIELDS):
        lanes = slice(c * 128, (c + 1) * 128)
        real, imag = mixed[:64, lanes], mixed[64:, lanes]
        put(c, pl.ds(0, 128), real * cosine + imag * sine)
        put(c, pl.ds(128, 128), imag * cosine - real * sine)
    both = mm(ys[...], four[...])
    spectrum = both[:count] + both[count:]
    xx, xy, xz, y, z = (spectrum[c * 64 : (c + 1) * 64] for c in range(FIELDS))

    shape = (64, 256)
    row = lax.broadcasted_iota(jnp.int32, shape, 0)
    lane = lax.broadcasted_iota(jnp.int32, shape, 1)
    lane = lax.bitwise_and(lane, 127)
    kx = 16 * lax.shift_right_logical(lane, 5) + lax.shift_right_logical(row, 2)
    ky = 4 * lax.axis_index("slab") + lax.bitwise_and(row, 3)
    kz = lax.bitwise_and(lane, 31)
    half = GRID // 2
    keep = (kx != half) & (ky != half) & (kx + ky + kz > 0)
    xi = [
        jnp.where(kx < half, kx, kx - GRID).astype(jnp.float32),
        jnp.where(ky < half, ky, ky - GRID).astype(jnp.float32),
        kz.astype(jnp.float32),
    ]
    length = xi[0] * xi[0] + xi[1] * xi[1] + xi[2] * xi[2]
    inverse = jnp.where(keep, 1.0 / jnp.maximum(length, 1.0), 0.0)
    coupling = (REFERENCE_LAME + REFERENCE_SHEAR) / (
        REFERENCE_SHEAR * (REFERENCE_LAME + 2.0 * REFERENCE_SHEAR)
    )
    scaled = inverse * (1.0 / (2.0 * REFERENCE_SHEAR))
    traction = [xi[0] * xx + xi[1] * xy + xi[2] * xz, xi[0] * xy + y, xi[0] * xz + z]
    load = xi[0] * traction[0] + xi[1] * traction[1] + xi[2] * traction[2]
    load = load * (inverse * (REFERENCE_SHEAR * coupling))
    field = [scaled * (traction[i] - xi[i] * load) for i in range(3)]
    put(0, slice(None), 2.0 * (xi[0] * field[0]))
    put(1, slice(None), xi[0] * field[1] + xi[1] * field[0])
    put(2, slice(None), xi[0] * field[2] + xi[2] * field[0])
    put(3, slice(None), field[1])
    put(4, slice(None), field[2])
    both = mm(ys[...], back_four[...])
    turned = both[:count] + both[count:]
    for c in range(FIELDS):
        real, imag = turned[c * 64 : (c + 1) * 64, :128], turned[c * 64 : (c + 1) * 64, 128:]
        lanes = pl.ds(c * 128, 128)
        put_columns(bs, 0, 64, lanes, real * cosine - imag * sine)
        put_columns(bs, 64, 64, lanes, real * sine + imag * cosine)
    result = from_left(back_columns, bs)
    for c in range(FIELDS):
        out_ref[:, c * 8 : (c + 1) * 8, :] = result[:, c * 128 : (c + 1) * 128].reshape(16, 8, 128)


def totals_kernel(in_ref, all_ref, stress_ref, tangent_ref):
    line = jnp.sum(in_ref[...].reshape(SLABS, 128), axis=0, keepdims=True)
    all_ref[...] = jnp.broadcast_to(line[None], all_ref.shape)
    line = line * (1.0 / VOXELS)
    stress_ref[...] = line[:, :6]
    at = lax.broadcasted_iota(jnp.int32, (1, 128), 1) - OUTER_AT
    a = at // 6
    b = at - 6 * a
    both = (a < 3) & (b < 3)
    shear = jnp.broadcast_to(line[:, 6:7], (1, 128)) * (2.0 * SHEAR_MODULUS)
    fixed = jnp.where(both, BULK_MODULUS - shear * (1.0 / 3.0), 0.0)
    fixed = fixed + jnp.where(a == b, shear, 0.0)
    whole = (fixed - line * jnp.where(b < 3, 1.0, 2.0)) * (1.0 / TANGENT_UNIT)
    for i in range(6):
        tangent_ref[i] = whole[:, OUTER_AT + 6 * i : OUTER_AT + 6 * i + 6]


def assembly_kernel(points, basis_ref, turned_ref, in_ref, stiffness_ref, forces_ref):
    half = points // 2
    shape = (points, 128)
    sums = in_ref[...].reshape(points, 128) * (1.0 / VOXELS)
    sums = jnp.concatenate([sums[half:], sums[:half]], axis=0)
    basis = [basis_ref[a * points : (a + 1) * points, :] for a in range(6)]
    mean_shear = 2.0 * SHEAR_MODULUS * sums[:, 6:7]

    def column(at):
        return jnp.broadcast_to(sums[:, at : at + 1], shape)

    mean_shear = jnp.broadcast_to(mean_shear, shape)
    on_diagonal = BULK_MODULUS + mean_shear * (2.0 / 3.0)
    off_diagonal = BULK_MODULUS - mean_shear * (1.0 / 3.0)
    answers = []
    force = jnp.zeros(shape, jnp.float32)
    scale = QUADRATURE_WEIGHT / TANGENT_UNIT
    for a in range(6):
        total = jnp.zeros(shape, jnp.float32)
        for b in range(6):
            low, high = min(a, b), max(a, b)
            entry = -PAIR_WEIGHTS[b] * column(OUTER_AT + 6 * low + high)
            if a == b:
                entry = entry + (on_diagonal if a < 3 else mean_shear)
            elif a < 3 and b < 3:
                entry = entry + off_diagonal
            total = total + entry * basis[b]
        answers.append(total * (PAIR_WEIGHTS[a] * scale))
        force = force + basis[a] * (column(a) * (PAIR_WEIGHTS[a] * QUADRATURE_WEIGHT))
    high, low = split(jnp.concatenate(answers, axis=0))
    left_high, left_low = turned_ref[0], turned_ref[1]
    whole = mm(left_high, high) + (mm(left_low, high) + mm(left_high, low))
    stiffness_ref[...] = whole[:60, :60]
    line = jnp.sum(force, axis=0, keepdims=True)
    part8 = lax.broadcasted_iota(jnp.int32, (8, 128), 0)
    lane8 = lax.broadcasted_iota(jnp.int32, (8, 128), 1)
    spread = jnp.where(lane8 % 3 == part8, jnp.broadcast_to(line, (8, 128)), 0.0)
    pick_row = lax.broadcasted_iota(jnp.int32, (128, 128), 0)
    pick_col = lax.broadcasted_iota(jnp.int32, (128, 128), 1)
    pick = (pick_row // 3 == pick_col).astype(jnp.float32)
    forces = jnp.dot(
        spread, pick, precision=lax.Precision.HIGHEST, preferred_element_type=jnp.float32
    )
    forces_ref[...] = forces[:3, :20]


VMEM = pl.BlockSpec(memory_space=pltpu.VMEM)
HBM = pl.BlockSpec(memory_space=pltpu.HBM)
BF16 = jnp.bfloat16
F32 = jnp.float32
LIMIT = 16 * 1024 * 1024


def params():
    return pltpu.CompilerParams(vmem_limit_bytes=LIMIT)


def cost(flops, size):
    return pl.CostEstimate(flops=flops, bytes_accessed=size, transcendentals=0)


def plane_scratch():
    return [pltpu.VMEM((768, 256), BF16), pltpu.VMEM((256, 768), BF16)]


def exchange(array):
    return lax.all_to_all(array, "slab", split_axis=0, concat_axis=0, tiled=True)


def on_device(phase_ids, yield_flags, plastic_strain, displacements, connectivity):
    points = lax.axis_size("rve")

    def rows(array):
        lead = math.prod(array.shape[:-2])
        array = array.reshape(lead, PLANES, 32, 128)
        return jnp.transpose(array, (0, 2, 1, 3)).reshape(lead * 128, 128)

    phases = rows(phase_ids)
    flags = rows(yield_flags)
    plastic = rows(plastic_strain)

    there, back = depth_tables()
    depth, back_depth = jnp.asarray(right_table(there)), jnp.asarray(right_table(back))
    there, back = row_tables()
    line, back_line = jnp.asarray(left_table(there)), jnp.asarray(left_table(back))
    there, back, twist, four, back_four = column_tables()
    column, back_column = jnp.asarray(left_table(there)), jnp.asarray(left_table(back))
    twist = jnp.asarray(twist)
    four = jnp.asarray(four.astype(ml_dtypes.bfloat16))
    back_four = jnp.asarray(back_four.astype(ml_dtypes.bfloat16))

    block = jax.ShapeDtypeStruct((16, 8 * FIELDS, 128), F32)

    first = pl.pallas_call(
        functools.partial(first_kernel, points),
        out_shape=(
            block, jax.ShapeDtypeStruct((8, 128), F32),
            jax.ShapeDtypeStruct((6 * points, 128), F32),
            jax.ShapeDtypeStruct((2, 128, 6 * points), BF16),
        ),
        in_specs=[HBM] * 7, out_specs=(VMEM,) * 4,
        scratch_shapes=[
            pltpu.SMEM(connectivity.shape, jnp.int32), pltpu.SMEM(displacements.shape[::-1], F32),
            pltpu.VMEM((128, 128), jnp.int32), pltpu.VMEM((128, 128), jnp.int32),
            pltpu.VMEM((768, 128), F32), pltpu.VMEM((256, 256), BF16), pltpu.VMEM((256, 256), BF16),
            pltpu.SemaphoreType.DMA((7,)), *plane_scratch(),
        ],
        compiler_params=params(), cost_estimate=cost(400_000_000, 2_000_000), name="first",
    )
    columns = pl.pallas_call(
        column_kernel, out_shape=block,
        in_specs=[VMEM] * 6, out_specs=VMEM,
        scratch_shapes=[
            pltpu.VMEM((256, 128 * FIELDS), BF16), pltpu.VMEM((128 * FIELDS, 256), BF16),
        ],
        compiler_params=params(), cost_estimate=cost(400_000_000, 2_000_000), name="columns",
    )
    middle = pl.pallas_call(
        middle_kernel, out_shape=(block, jax.ShapeDtypeStruct((768, 128), F32)),
        in_specs=[VMEM] * 9, out_specs=(VMEM, VMEM),
        scratch_shapes=plane_scratch(), compiler_params=params(),
        cost_estimate=cost(800_000_000, 4_000_000), name="middle",
    )
    last = pl.pallas_call(
        last_kernel, out_shape=jax.ShapeDtypeStruct((SLABS, 1, 128), F32),
        in_specs=[VMEM] * 6, out_specs=VMEM,
        scratch_shapes=plane_scratch(), compiler_params=params(),
        cost_estimate=cost(400_000_000, 2_000_000), name="last",
    )
    totals = pl.pallas_call(
        totals_kernel,
        out_shape=(
            jax.ShapeDtypeStruct((points, 1, 128), F32), jax.ShapeDtypeStruct((1, 6), F32),
            jax.ShapeDtypeStruct((6, 1, 6), F32),
        ),
        in_specs=[VMEM], out_specs=(VMEM, VMEM, VMEM), compiler_params=params(),
        cost_estimate=cost(10_000, 50_000), name="totals",
    )
    assembly = pl.pallas_call(
        functools.partial(assembly_kernel, points),
        out_shape=(jax.ShapeDtypeStruct((60, 60), F32), jax.ShapeDtypeStruct((3, 20), F32)),
        in_specs=[VMEM] * 3, out_specs=(VMEM, VMEM), compiler_params=params(),
        cost_estimate=cost(10_000_000, 200_000), name="assembly",
    )

    def apply_columns(array):
        return exchange(
            columns(exchange(array), column, back_column, twist, four, back_four)
        )

    operands = (connectivity, displacements.T, phases, flags, plastic, depth, line)
    spectrum, macro, basis, turned_basis = first(
        *(pltpu.with_memory_space_constraint(operand, pltpu.HBM) for operand in operands)
    )
    planes = apply_columns(spectrum)
    spectrum, elastic = middle(
        macro, phases, flags, plastic, planes, back_depth, back_line, depth, line
    )
    planes = apply_columns(spectrum)
    partial = last(phases, flags, elastic, planes, back_depth, back_line)
    everyone, stress, tangent = totals(exchange(partial))
    half = points // 2
    turned = [*range(half, points), *range(half)]
    everyone = lax.all_to_all(
        everyone, "rve", 0, 0, tiled=True, axis_index_groups=[turned]
    )
    stiffness, forces = assembly(basis, turned_basis, everyone)
    return (stress, jnp.transpose(tangent, (1, 0, 2)), forces.T, stiffness)


def solution(mesh):
    return jax.shard_map(
        on_device,
        mesh=mesh,
        in_specs=(
            P("slab", None),
            P("rve", None, "slab", None),
            P("rve", None, "slab", None),
            P(),
            P(),
        ),
        out_specs=(P("rve", None), P("rve", None, None), P(), P()),
        check_vma=False,
    )
```

```python
import functools
import math

import jax
import jax.numpy as jnp
import ml_dtypes
import numpy as np
from jax import lax
from jax.experimental import pallas as pl
from jax.experimental.pallas import tpu as pltpu
from jax.sharding import PartitionSpec as P

GRID = 64
ITERS = 2
SLABS = 16
PLANES = GRID // SLABS
KEPT = GRID // 2

SHEAR_MODULUS = 80.0
BULK_MODULUS = 160.0
REFERENCE_SHEAR = 80.0
REFERENCE_LAME = 160.0 - 160.0 / 3.0
TANGENT_UNIT = 100.0
QUADRATURE_WEIGHT = 0.125
PAIR_WEIGHTS = (1.0, 1.0, 1.0, 2.0, 2.0, 2.0)
TENSOR_PAIRS = ((0, 0), (1, 1), (2, 2), (1, 2), (0, 2), (0, 1))
VOXELS = float(GRID**3)
GAUSS_LOW = 0.5 - 0.5 / math.sqrt(3.0)
GAUSS_HIGH = 0.5 + 0.5 / math.sqrt(3.0)
OUTER_AT = 8
FIELDS = 5


def halves(table):
    high = table.astype(np.float32).astype(ml_dtypes.bfloat16)
    low = (table - high.astype(np.float64)).astype(np.float32).astype(ml_dtypes.bfloat16)
    return high, low


def depth_tables():
    z = np.arange(GRID)
    k = np.arange(KEPT)
    theta = 2.0 * np.pi * np.outer(z, k) / GRID
    forward = np.stack([np.cos(theta), -np.sin(theta)], axis=0)
    weight = np.where(k == 0, 1.0, 2.0) / VOXELS
    inverse = forward * weight[None, None, :]
    pair = np.eye(2)
    there = np.einsum("rR,pzk->rzRpk", pair, forward)
    back = np.einsum("rR,pzk->Rpkrz", pair, inverse)
    return there.reshape(128, 128), back.reshape(128, 128)


def row_tables():
    y = 2 * np.arange(32)[None, :] + np.arange(2)[:, None]
    ky = 4 * np.arange(16)[:, None] + np.arange(4)[None, :]
    theta = 2.0 * np.pi * np.einsum("de,rm->derm", ky, y) / GRID
    c, s = np.cos(theta), np.sin(theta)
    there = np.zeros((16, 2, 4, 2, 2, 32))
    there[:, 0, :, :, 0, :] = c
    there[:, 0, :, :, 1, :] = s
    there[:, 1, :, :, 0, :] = -s
    there[:, 1, :, :, 1, :] = c
    back = np.zeros((2, 2, 32, 16, 2, 4))
    ct, st = np.einsum("derm->rmde", c), np.einsum("derm->rmde", s)
    back[:, 0, :, :, 0, :] = ct
    back[:, 0, :, :, 1, :] = -st
    back[:, 1, :, :, 0, :] = st
    back[:, 1, :, :, 1, :] = ct
    return there.reshape(128, 128), back.reshape(128, 128)


def column_tables():
    d = np.arange(16)
    theta = 2.0 * np.pi * np.outer(d, d) / 16.0
    c, s = np.cos(theta), np.sin(theta)
    same = np.eye(4)
    there = np.zeros((2, 16, 4, 16, 2, 4))
    there[0, :, :, :, 0, :] = np.einsum("bd,ef->bedf", c, same)
    there[0, :, :, :, 1, :] = np.einsum("bd,ef->bedf", s, same)
    there[1, :, :, :, 0, :] = np.einsum("bd,ef->bedf", -s, same)
    there[1, :, :, :, 1, :] = np.einsum("bd,ef->bedf", c, same)
    there = there.reshape(128, 128)
    phi = 2.0 * np.pi * np.outer(np.arange(16), np.arange(4)) / GRID
    twist = np.stack([np.cos(phi), np.sin(phi)])[:, :, None, :, None]
    twist = np.broadcast_to(twist, (2, 16, 4, 4, KEPT)).reshape(2, 64, 128)
    quarter = 2.0 * np.pi * np.outer(np.arange(4), np.arange(4)) / 4.0
    cq, sq = np.rint(np.cos(quarter)), np.rint(np.sin(quarter))
    kept = np.eye(KEPT)
    four = np.zeros((2, 4, KEPT, 2, 4, KEPT))
    four[0, :, :, 0] = np.einsum("la,kK->lkaK", cq, kept)
    four[1, :, :, 0] = np.einsum("la,kK->lkaK", sq, kept)
    four[0, :, :, 1] = np.einsum("la,kK->lkaK", -sq, kept)
    four[1, :, :, 1] = np.einsum("la,kK->lkaK", cq, kept)
    four = four.reshape(256, 256)
    return there, there.T.copy(), twist.astype(np.float32), four, four.T.copy()


def right_table(table):
    high, low = halves(table)
    return np.block([[high, low], [high, np.zeros_like(low)]])


def left_table(table):
    return np.ascontiguousarray(right_table(table.T).T)


def split(x):
    high = x.astype(jnp.bfloat16)
    low = (x - high.astype(jnp.float32)).astype(jnp.bfloat16)
    return high, low


def mm(a, b):
    return jnp.dot(a, b, preferred_element_type=jnp.float32)


def from_left(table_ref, data_ref):
    both = mm(table_ref[...], data_ref[...])
    return both[:128] + both[128:]


def from_right(data_ref, table_ref):
    both = mm(data_ref[...], table_ref[...])
    return both[:, :128] + both[:, 128:]


def swap_chunks(tiles):
    lane = lax.broadcasted_iota(jnp.int32, tiles[0].shape, 1)
    low = lane < 64
    even = lax.bitwise_and(lane, 32) == 0
    halfway = [None] * 4
    for i in range(2):
        first, second = tiles[i], tiles[i + 2]
        halfway[i] = jnp.where(low, first, pltpu.roll(second, 64, 1))
        halfway[i + 2] = jnp.where(low, pltpu.roll(first, 64, 1), second)
    result = []
    for i in (0, 2):
        first, second = halfway[i], halfway[i + 1]
        result.append(jnp.where(even, first, pltpu.roll(second, 32, 1)))
        result.append(jnp.where(even, pltpu.roll(first, 96, 1), second))
    return result


def slopes_of(bits, low, high):
    at = [jnp.where(bit == 1, high, low) for bit in bits]
    far = [jnp.where(bit == 1, low, high) for bit in bits]

    def slope(corner, axis):
        value = None
        for other in range(3):
            if other != axis:
                factor = at[other] if corner >> other & 1 else far[other]
                value = factor if value is None else value * factor
        return value if corner >> axis & 1 else -value

    return slope


def macro_strain(point, conn_ref, disp_ref):
    low, high = jnp.float32(GAUSS_LOW), jnp.float32(GAUSS_HIGH)
    bits = [lax.bitwise_and(lax.shift_right_logical(point, d), 1) for d in range(3)]
    slope = slopes_of(bits, low, high)
    element = lax.shift_right_logical(point, 3)
    grad = [[jnp.float32(0.0)] * 3 for _ in range(3)]
    for corner in range(8):
        node = conn_ref[element, corner]
        for k in range(3):
            u = disp_ref[k, node]
            for d in range(3):
                grad[k][d] = grad[k][d] + slope(corner, d) * u
    strain = []
    for i, j in TENSOR_PAIRS:
        strain.append(grad[i][i] if i == j else 0.5 * (grad[i][j] + grad[j][i]))
    return strain


def material(elastic, phases, flags):
    hard = phases == 1
    limit = jnp.where(hard, 1.2, 0.3)
    ratio = jnp.where(
        hard,
        3.0 * SHEAR_MODULUS / (3.0 * SHEAR_MODULUS + 10.0),
        3.0 * SHEAR_MODULUS / (3.0 * SHEAR_MODULUS + 2.0),
    )
    active = flags.astype(jnp.float32)
    volume = elastic[0] + elastic[1] + elastic[2]
    third = volume * (1.0 / 3.0)
    trial = [2.0 * SHEAR_MODULUS * (elastic[a] - third) for a in range(3)]
    trial += [2.0 * SHEAR_MODULUS * elastic[a] for a in range(3, 6)]
    normal = trial[0] * trial[0] + trial[1] * trial[1] + trial[2] * trial[2]
    shear = trial[3] * trial[3] + trial[4] * trial[4] + trial[5] * trial[5]
    equivalent = jnp.sqrt(1.5 * (normal + 2.0 * shear))
    bounded = jnp.maximum(equivalent, limit)
    inverse = 1.0 / bounded
    scaled = ratio * active
    softening = 1.0 - scaled * (equivalent - limit) * inverse
    pressure = BULK_MODULUS * volume
    stress = [trial[a] * softening + pressure for a in range(3)]
    stress += [trial[a] * softening for a in range(3, 6)]
    weight = 3.0 * SHEAR_MODULUS * scaled * limit * (inverse * inverse * inverse)
    return stress, trial, softening, weight


def every_fourth(ref, start, plane):
    return ref[pl.ds(start + plane, 32, stride=4), :]


def put_rows(ref, rows, value):
    high, low = split(value)
    ref[rows, 0:128] = high
    ref[rows, 128:256] = low


def put_columns(ref, start, count, columns, value):
    high, low = split(value)
    ref[pl.ds(start, count), columns] = high
    ref[pl.ds(128 + start, count), columns] = low


def plane_waves():
    row = lax.broadcasted_iota(jnp.int32, (128, 128), 0)
    lane = lax.broadcasted_iota(jnp.int32, (128, 128), 1)
    ky = 4 * lax.shift_right_logical(row, 3) + lax.bitwise_and(row, 3)
    ky = jnp.where(ky < GRID // 2, ky, ky - GRID)
    return ky.astype(jnp.float32), lax.bitwise_and(lane, 31).astype(jnp.float32)


def forward_planes(xs, bs, depth, rows, out_ref):
    turned = from_right(xs, depth)
    tiles = swap_chunks([turned[l * 192 : (l + 1) * 192] for l in range(PLANES)])
    for c in range(6):
        for s in range(4):
            block = tiles[s][c * 32 : (c + 1) * 32]
            put_columns(bs, s * 32, 32, pl.ds(c * 128, 128), block)
    spectrum = from_left(rows, bs)
    xx, yy, zz, yz, xz, xy = (spectrum[:, c * 128 : (c + 1) * 128] for c in range(6))
    wave_y, wave_z = plane_waves()
    fields = (xx, xy, xz, wave_y * yy + wave_z * yz, wave_y * yz + wave_z * zz)
    for c, field in enumerate(fields):
        out_ref[:, c * 8 : (c + 1) * 8, :] = field.reshape(16, 8, 128)


def backward_planes(in_ref, bs, xs, depth, rows):
    xx, xy, xz, y, z = (
        in_ref[:, c * 8 : (c + 1) * 8, :].reshape(128, 128) for c in range(FIELDS)
    )
    wave_y, wave_z = plane_waves()
    yy, zz = 2.0 * (wave_y * y), 2.0 * (wave_z * z)
    for c, value in enumerate((xx, yy, zz, wave_y * z + wave_z * y, xz, xy)):
        put_columns(bs, 0, 128, pl.ds(c * 128, 128), value)
    lines = from_left(rows, bs)
    tiles = [
        jnp.concatenate(
            [lines[s * 32 : (s + 1) * 32, c * 128 : (c + 1) * 128] for c in range(6)], axis=0
        )
        for s in range(4)
    ]
    for l, tile in enumerate(swap_chunks(tiles)):
        put_rows(xs, pl.ds(l * 192, 192), tile)
    return from_right(xs, depth)


def basis_of(points, conn_ref):
    shape = (points, 128)
    lane = lax.broadcasted_iota(jnp.int32, shape, 1)
    point = lax.broadcasted_iota(jnp.int32, shape, 0)
    element = lax.shift_right_logical(point, 3)
    bits = [lax.bitwise_and(lax.shift_right_logical(point, d), 1) for d in range(3)]
    slope = slopes_of(bits, GAUSS_LOW, GAUSS_HIGH)
    node = lane // 3
    part = lane - 3 * node
    elements = conn_ref.shape[0]
    grad = [jnp.zeros(shape, jnp.float32) for _ in range(3)]
    for corner in range(8):
        owner = jnp.full(shape, conn_ref[0, corner], jnp.int32)
        for e in range(1, elements):
            owner = jnp.where(element == e, conn_ref[e, corner], owner)
        here = (owner == node) & (lane < 60)
        for d in range(3):
            grad[d] = grad[d] + jnp.where(here, slope(corner, d), 0.0)
    basis = []
    for i, k in TENSOR_PAIRS:
        if i == k:
            basis.append(jnp.where(part == i, grad[i], 0.0))
        else:
            value = jnp.where(part == i, 0.5 * grad[k], 0.0)
            basis.append(value + jnp.where(part == k, 0.5 * grad[i], 0.0))
    return jnp.concatenate(basis, axis=0)


def first_kernel(
    points, conn_hbm, disp_hbm, phase_hbm, flag_hbm, plastic_hbm, depth_hbm, rows_hbm,
    out_ref, macro_ref, basis_ref, turned_ref,
    conn_ref, disp_ref, phase_ref, flag_ref, plastic_ref, depth, rows, sems, xs, bs,
):
    pairs = (
        (conn_hbm, conn_ref), (disp_hbm, disp_ref), (plastic_hbm, plastic_ref),
        (phase_hbm, phase_ref), (flag_hbm.at[pl.ds(0, 128)], flag_ref),
        (depth_hbm, depth), (rows_hbm, rows),
    )
    copies = [pltpu.make_async_copy(a, b, sems.at[i]) for i, (a, b) in enumerate(pairs)]
    for copy in copies:
        copy.start()
    for copy in copies[:2]:
        copy.wait()
    macro = macro_strain(lax.axis_index("rve"), conn_ref, disp_ref)
    row = lax.broadcasted_iota(jnp.int32, (8, 128), 0)
    table = jnp.zeros((8, 128), jnp.float32)
    for c in range(6):
        table = jnp.where(row == c, macro[c], table)
    macro_ref[...] = table
    basis = basis_of(points, conn_ref)
    basis_ref[...] = basis
    high, low = split(jnp.transpose(basis))
    turned_ref[0] = high
    turned_ref[1] = low
    for copy in copies[2:5]:
        copy.wait()
    for plane in range(PLANES):
        elastic = [macro[c] - every_fourth(plastic_ref, c * 128, plane) for c in range(6)]
        phases = every_fourth(phase_ref, 0, plane)
        flags = every_fourth(flag_ref, 0, plane)
        stress = material(elastic, phases, flags)[0]
        for c in range(6):
            put_rows(xs, pl.ds(plane * 192 + c * 32, 32), stress[c])
    for copy in copies[5:]:
        copy.wait()
    forward_planes(xs, bs, depth, rows, out_ref)


def middle_kernel(
    macro_ref, phase_ref, flag_ref, plastic_ref, in_ref, back_depth, back_rows, depth, rows,
    out_ref, elastic_ref, xs, bs,
):
    macro = [macro_ref[c : c + 1, :] for c in range(6)]
    correction = backward_planes(in_ref, bs, xs, back_depth, back_rows)
    for plane in range(PLANES):
        elastic = []
        for c in range(6):
            at = plane * 192 + c * 32
            before = macro[c] - every_fourth(plastic_ref, c * 128, plane)
            after = before - correction[at : at + 32]
            elastic_ref[at : at + 32, :] = after
            elastic.append(after)
        phases = every_fourth(phase_ref, 0, plane)
        flags = every_fourth(flag_ref, 128, plane)
        stress = material(elastic, phases, flags)[0]
        for c in range(6):
            put_rows(xs, pl.ds(plane * 192 + c * 32, 32), stress[c])
    forward_planes(xs, bs, depth, rows, out_ref)


def last_kernel(
    phase_ref, flag_ref, elastic_ref, in_ref, back_depth, back_rows, out_ref, xs, bs
):
    correction = backward_planes(in_ref, bs, xs, back_depth, back_rows)
    sums = [None] * 28

    def collect(at, value):
        part = value.reshape(4, 8, 128)
        part = (part[0] + part[1]) + (part[2] + part[3])
        sums[at] = part if sums[at] is None else sums[at] + part

    for plane in range(PLANES):
        starts = [plane * 192 + c * 32 for c in range(6)]
        elastic = [elastic_ref[at : at + 32, :] - correction[at : at + 32] for at in starts]
        phases = every_fourth(phase_ref, 0, plane)
        flags = every_fourth(flag_ref, 256, plane)
        stress, trial, softening, weight = material(elastic, phases, flags)
        for c in range(6):
            collect(c, stress[c])
        collect(6, softening)
        at = 7
        for a in range(6):
            scaled = weight * trial[a]
            for b in range(a, 6):
                collect(at, scaled * trial[b])
                at += 1
    row = lax.broadcasted_iota(jnp.int32, (128, 128), 0)
    lines = jnp.zeros((128, 128), jnp.float32)

    def place(at, value):
        return jnp.where(row == at, jnp.broadcast_to(value, (128, 128)), lines)

    totals = [jnp.sum(value, axis=0, keepdims=True) for value in sums]
    for c in range(7):
        lines = place(c, totals[c])
    at = 7
    for a in range(6):
        for b in range(a, 6):
            lines = place(OUTER_AT + 6 * a + b, totals[at])
            if a != b:
                lines = place(OUTER_AT + 6 * b + a, totals[at])
            at += 1
    ones = jnp.ones((SLABS, 128), jnp.float32)
    line = lax.dot_general(
        ones, lines, (((1,), (1,)), ((), ())),
        precision=lax.Precision.HIGHEST, preferred_element_type=jnp.float32,
    )
    out_ref[...] = line.reshape(SLABS, 1, 128)


def column_kernel(in_ref, columns, back_columns, twist_ref, four, back_four, out_ref, bs, ys):
    count = 64 * FIELDS
    for c in range(FIELDS):
        block = in_ref[:, c * 8 : (c + 1) * 8, :].reshape(128, 128)
        put_columns(bs, 0, 128, pl.ds(c * 128, 128), block)
    mixed = from_left(columns, bs)
    cosine, sine = twist_ref[0], twist_ref[1]

    def put(c, lanes, value):
        high, low = split(value)
        ys[pl.ds(c * 64, 64), lanes] = high
        ys[pl.ds(count + c * 64, 64), lanes] = low

    for c in range(FIELDS):
        lanes = slice(c * 128, (c + 1) * 128)
        real, imag = mixed[:64, lanes], mixed[64:, lanes]
        put(c, pl.ds(0, 128), real * cosine + imag * sine)
        put(c, pl.ds(128, 128), imag * cosine - real * sine)
    both = mm(ys[...], four[...])
    spectrum = both[:count] + both[count:]
    xx, xy, xz, y, z = (spectrum[c * 64 : (c + 1) * 64] for c in range(FIELDS))

    shape = (64, 256)
    row = lax.broadcasted_iota(jnp.int32, shape, 0)
    lane = lax.broadcasted_iota(jnp.int32, shape, 1)
    lane = lax.bitwise_and(lane, 127)
    kx = 16 * lax.shift_right_logical(lane, 5) + lax.shift_right_logical(row, 2)
    ky = 4 * lax.axis_index("slab") + lax.bitwise_and(row, 3)
    kz = lax.bitwise_and(lane, 31)
    half = GRID // 2
    keep = (kx != half) & (ky != half) & (kx + ky + kz > 0)
    xi = [
        jnp.where(kx < half, kx, kx - GRID).astype(jnp.float32),
        jnp.where(ky < half, ky, ky - GRID).astype(jnp.float32),
        kz.astype(jnp.float32),
    ]
    length = xi[0] * xi[0] + xi[1] * xi[1] + xi[2] * xi[2]
    inverse = jnp.where(keep, 1.0 / jnp.maximum(length, 1.0), 0.0)
    coupling = (REFERENCE_LAME + REFERENCE_SHEAR) / (
        REFERENCE_SHEAR * (REFERENCE_LAME + 2.0 * REFERENCE_SHEAR)
    )
    scaled = inverse * (1.0 / (2.0 * REFERENCE_SHEAR))
    traction = [xi[0] * xx + xi[1] * xy + xi[2] * xz, xi[0] * xy + y, xi[0] * xz + z]
    load = xi[0] * traction[0] + xi[1] * traction[1] + xi[2] * traction[2]
    load = load * (inverse * (REFERENCE_SHEAR * coupling))
    field = [scaled * (traction[i] - xi[i] * load) for i in range(3)]
    put(0, slice(None), 2.0 * (xi[0] * field[0]))
    put(1, slice(None), xi[0] * field[1] + xi[1] * field[0])
    put(2, slice(None), xi[0] * field[2] + xi[2] * field[0])
    put(3, slice(None), field[1])
    put(4, slice(None), field[2])
    both = mm(ys[...], back_four[...])
    turned = both[:count] + both[count:]
    for c in range(FIELDS):
        real, imag = turned[c * 64 : (c + 1) * 64, :128], turned[c * 64 : (c + 1) * 64, 128:]
        lanes = pl.ds(c * 128, 128)
        put_columns(bs, 0, 64, lanes, real * cosine - imag * sine)
        put_columns(bs, 64, 64, lanes, real * sine + imag * cosine)
    result = from_left(back_columns, bs)
    for c in range(FIELDS):
        out_ref[:, c * 8 : (c + 1) * 8, :] = result[:, c * 128 : (c + 1) * 128].reshape(16, 8, 128)


def totals_kernel(in_ref, all_ref):
    line = jnp.sum(in_ref[...].reshape(SLABS, 128), axis=0, keepdims=True)
    all_ref[...] = jnp.broadcast_to(line[None], all_ref.shape)


def own_outputs(line, stress_ref, tangent_ref):
    stress_ref[...] = line[:, :6]
    at = lax.broadcasted_iota(jnp.int32, (1, 128), 1) - OUTER_AT
    a = at // 6
    b = at - 6 * a
    both = (a < 3) & (b < 3)
    shear = jnp.broadcast_to(line[:, 6:7], (1, 128)) * (2.0 * SHEAR_MODULUS)
    fixed = jnp.where(both, BULK_MODULUS - shear * (1.0 / 3.0), 0.0)
    fixed = fixed + jnp.where(a == b, shear, 0.0)
    whole = (fixed - line * jnp.where(b < 3, 1.0, 2.0)) * (1.0 / TANGENT_UNIT)
    for i in range(6):
        tangent_ref[i] = whole[:, OUTER_AT + 6 * i : OUTER_AT + 6 * i + 6]


def assembly_kernel(
    points, basis_ref, turned_ref, in_ref, stress_ref, tangent_ref, stiffness_ref, forces_ref
):
    half = points // 2
    own = lax.rem(lax.axis_index("rve") + points - half, points)
    own_outputs(in_ref[own] * (1.0 / VOXELS), stress_ref, tangent_ref)
    shape = (points, 128)
    sums = in_ref[...].reshape(points, 128) * (1.0 / VOXELS)
    sums = jnp.concatenate([sums[half:], sums[:half]], axis=0)
    basis = [basis_ref[a * points : (a + 1) * points, :] for a in range(6)]
    mean_shear = 2.0 * SHEAR_MODULUS * sums[:, 6:7]

    def column(at):
        return jnp.broadcast_to(sums[:, at : at + 1], shape)

    mean_shear = jnp.broadcast_to(mean_shear, shape)
    on_diagonal = BULK_MODULUS + mean_shear * (2.0 / 3.0)
    off_diagonal = BULK_MODULUS - mean_shear * (1.0 / 3.0)
    answers = []
    force = jnp.zeros(shape, jnp.float32)
    scale = QUADRATURE_WEIGHT / TANGENT_UNIT
    for a in range(6):
        total = jnp.zeros(shape, jnp.float32)
        for b in range(6):
            low, high = min(a, b), max(a, b)
            entry = -PAIR_WEIGHTS[b] * column(OUTER_AT + 6 * low + high)
            if a == b:
                entry = entry + (on_diagonal if a < 3 else mean_shear)
            elif a < 3 and b < 3:
                entry = entry + off_diagonal
            total = total + entry * basis[b]
        answers.append(total * (PAIR_WEIGHTS[a] * scale))
        force = force + basis[a] * (column(a) * (PAIR_WEIGHTS[a] * QUADRATURE_WEIGHT))
    high, low = split(jnp.concatenate(answers, axis=0))
    left_high, left_low = turned_ref[0], turned_ref[1]
    whole = mm(left_high, high) + (mm(left_low, high) + mm(left_high, low))
    stiffness_ref[...] = whole[:60, :60]
    line = jnp.sum(force, axis=0, keepdims=True)
    part8 = lax.broadcasted_iota(jnp.int32, (8, 128), 0)
    lane8 = lax.broadcasted_iota(jnp.int32, (8, 128), 1)
    spread = jnp.where(lane8 % 3 == part8, jnp.broadcast_to(line, (8, 128)), 0.0)
    pick_row = lax.broadcasted_iota(jnp.int32, (128, 128), 0)
    pick_col = lax.broadcasted_iota(jnp.int32, (128, 128), 1)
    pick = (pick_row // 3 == pick_col).astype(jnp.float32)
    forces = jnp.dot(
        spread, pick, precision=lax.Precision.HIGHEST, preferred_element_type=jnp.float32
    )
    forces_ref[...] = forces[:3, :20]


VMEM = pl.BlockSpec(memory_space=pltpu.VMEM)
HBM = pl.BlockSpec(memory_space=pltpu.HBM)
BF16 = jnp.bfloat16
F32 = jnp.float32
LIMIT = 16 * 1024 * 1024


def params():
    return pltpu.CompilerParams(vmem_limit_bytes=LIMIT)


def cost(flops, size):
    return pl.CostEstimate(flops=flops, bytes_accessed=size, transcendentals=0)


def plane_scratch():
    return [pltpu.VMEM((768, 256), BF16), pltpu.VMEM((256, 768), BF16)]


def exchange(array):
    return lax.all_to_all(array, "slab", split_axis=0, concat_axis=0, tiled=True)


def on_device(phase_ids, yield_flags, plastic_strain, displacements, connectivity):
    points = lax.axis_size("rve")

    def rows(array):
        lead = math.prod(array.shape[:-2])
        array = array.reshape(lead, PLANES, 32, 128)
        return jnp.transpose(array, (0, 2, 1, 3)).reshape(lead * 128, 128)

    phases = rows(phase_ids)
    flags = rows(yield_flags)
    plastic = rows(plastic_strain)

    there, back = depth_tables()
    depth, back_depth = jnp.asarray(right_table(there)), jnp.asarray(right_table(back))
    there, back = row_tables()
    line, back_line = jnp.asarray(left_table(there)), jnp.asarray(left_table(back))
    there, back, twist, four, back_four = column_tables()
    column, back_column = jnp.asarray(left_table(there)), jnp.asarray(left_table(back))
    twist = jnp.asarray(twist)
    four = jnp.asarray(four.astype(ml_dtypes.bfloat16))
    back_four = jnp.asarray(back_four.astype(ml_dtypes.bfloat16))

    block = jax.ShapeDtypeStruct((16, 8 * FIELDS, 128), F32)

    first = pl.pallas_call(
        functools.partial(first_kernel, points),
        out_shape=(
            block, jax.ShapeDtypeStruct((8, 128), F32),
            jax.ShapeDtypeStruct((6 * points, 128), F32),
            jax.ShapeDtypeStruct((2, 128, 6 * points), BF16),
        ),
        in_specs=[HBM] * 7, out_specs=(VMEM,) * 4,
        scratch_shapes=[
            pltpu.SMEM(connectivity.shape, jnp.int32), pltpu.SMEM(displacements.shape[::-1], F32),
            pltpu.VMEM((128, 128), jnp.int32), pltpu.VMEM((128, 128), jnp.int32),
            pltpu.VMEM((768, 128), F32), pltpu.VMEM((256, 256), BF16), pltpu.VMEM((256, 256), BF16),
            pltpu.SemaphoreType.DMA((7,)), *plane_scratch(),
        ],
        compiler_params=params(), cost_estimate=cost(400_000_000, 2_000_000), name="first",
    )
    columns = pl.pallas_call(
        column_kernel, out_shape=block,
        in_specs=[VMEM] * 6, out_specs=VMEM,
        scratch_shapes=[
            pltpu.VMEM((256, 128 * FIELDS), BF16), pltpu.VMEM((128 * FIELDS, 256), BF16),
        ],
        compiler_params=params(), cost_estimate=cost(400_000_000, 2_000_000), name="columns",
    )
    middle = pl.pallas_call(
        middle_kernel, out_shape=(block, jax.ShapeDtypeStruct((768, 128), F32)),
        in_specs=[VMEM] * 9, out_specs=(VMEM, VMEM),
        scratch_shapes=plane_scratch(), compiler_params=params(),
        cost_estimate=cost(800_000_000, 4_000_000), name="middle",
    )
    last = pl.pallas_call(
        last_kernel, out_shape=jax.ShapeDtypeStruct((SLABS, 1, 128), F32),
        in_specs=[VMEM] * 6, out_specs=VMEM,
        scratch_shapes=plane_scratch(), compiler_params=params(),
        cost_estimate=cost(400_000_000, 2_000_000), name="last",
    )
    totals = pl.pallas_call(
        totals_kernel, out_shape=jax.ShapeDtypeStruct((points, 1, 128), F32),
        in_specs=[VMEM], out_specs=VMEM, compiler_params=params(),
        cost_estimate=cost(10_000, 50_000), name="totals",
    )
    assembly = pl.pallas_call(
        functools.partial(assembly_kernel, points),
        out_shape=(
            jax.ShapeDtypeStruct((1, 6), F32), jax.ShapeDtypeStruct((6, 1, 6), F32),
            jax.ShapeDtypeStruct((60, 60), F32), jax.ShapeDtypeStruct((3, 20), F32),
        ),
        in_specs=[VMEM] * 3, out_specs=(VMEM,) * 4, compiler_params=params(),
        cost_estimate=cost(10_000_000, 200_000), name="assembly",
    )

    def apply_columns(array):
        return exchange(
            columns(exchange(array), column, back_column, twist, four, back_four)
        )

    operands = (connectivity, displacements.T, phases, flags, plastic, depth, line)
    spectrum, macro, basis, turned_basis = first(
        *(pltpu.with_memory_space_constraint(operand, pltpu.HBM) for operand in operands)
    )
    planes = apply_columns(spectrum)
    spectrum, elastic = middle(
        macro, phases, flags, plastic, planes, back_depth, back_line, depth, line
    )
    planes = apply_columns(spectrum)
    partial = last(phases, flags, elastic, planes, back_depth, back_line)
    everyone = totals(exchange(partial))
    half = points // 2
    turned = [*range(half, points), *range(half)]
    everyone = lax.all_to_all(
        everyone, "rve", 0, 0, tiled=True, axis_index_groups=[turned]
    )
    stress, tangent, stiffness, forces = assembly(basis, turned_basis, everyone)
    return (stress, jnp.transpose(tangent, (1, 0, 2)), forces.T, stiffness)


def solution(mesh):
    return jax.shard_map(
        on_device,
        mesh=mesh,
        in_specs=(
            P("slab", None),
            P("rve", None, "slab", None),
            P("rve", None, "slab", None),
            P(),
            P(),
        ),
        out_specs=(P("rve", None), P("rve", None, None), P(), P()),
        check_vma=False,
    )
```

```python
import functools
import math

import jax
import jax.numpy as jnp
import ml_dtypes
import numpy as np
from jax import lax
from jax.experimental import pallas as pl
from jax.experimental.pallas import tpu as pltpu
from jax.sharding import PartitionSpec as P

GRID = 64
ITERS = 2
SLABS = 16
PLANES = GRID // SLABS
KEPT = GRID // 2

SHEAR_MODULUS = 80.0
BULK_MODULUS = 160.0
REFERENCE_SHEAR = 80.0
REFERENCE_LAME = 160.0 - 160.0 / 3.0
TANGENT_UNIT = 100.0
QUADRATURE_WEIGHT = 0.125
PAIR_WEIGHTS = (1.0, 1.0, 1.0, 2.0, 2.0, 2.0)
TENSOR_PAIRS = ((0, 0), (1, 1), (2, 2), (1, 2), (0, 2), (0, 1))
VOXELS = float(GRID**3)
GAUSS_LOW = 0.5 - 0.5 / math.sqrt(3.0)
GAUSS_HIGH = 0.5 + 0.5 / math.sqrt(3.0)
OUTER_AT = 8
FIELDS = 5


def halves(table):
    high = table.astype(np.float32).astype(ml_dtypes.bfloat16)
    low = (table - high.astype(np.float64)).astype(np.float32).astype(ml_dtypes.bfloat16)
    return high, low


def depth_tables():
    z = np.arange(GRID)
    k = np.arange(KEPT)
    theta = 2.0 * np.pi * np.outer(z, k) / GRID
    forward = np.stack([np.cos(theta), -np.sin(theta)], axis=0)
    weight = np.where(k == 0, 1.0, 2.0) / VOXELS
    inverse = forward * weight[None, None, :]
    pair = np.eye(2)
    there = np.einsum("rR,pzk->rzRpk", pair, forward)
    back = np.einsum("rR,pzk->Rpkrz", pair, inverse)
    return there.reshape(128, 128), back.reshape(128, 128)


def row_tables():
    y = 2 * np.arange(32)[None, :] + np.arange(2)[:, None]
    ky = 4 * np.arange(16)[:, None] + np.arange(4)[None, :]
    theta = 2.0 * np.pi * np.einsum("de,rm->derm", ky, y) / GRID
    c, s = np.cos(theta), np.sin(theta)
    there = np.zeros((16, 2, 4, 2, 2, 32))
    there[:, 0, :, :, 0, :] = c
    there[:, 0, :, :, 1, :] = s
    there[:, 1, :, :, 0, :] = -s
    there[:, 1, :, :, 1, :] = c
    back = np.zeros((2, 2, 32, 16, 2, 4))
    ct, st = np.einsum("derm->rmde", c), np.einsum("derm->rmde", s)
    back[:, 0, :, :, 0, :] = ct
    back[:, 0, :, :, 1, :] = -st
    back[:, 1, :, :, 0, :] = st
    back[:, 1, :, :, 1, :] = ct
    return there.reshape(128, 128), back.reshape(128, 128)


def column_tables():
    d = np.arange(16)
    theta = 2.0 * np.pi * np.outer(d, d) / 16.0
    c, s = np.cos(theta), np.sin(theta)
    same = np.eye(4)
    there = np.zeros((2, 16, 4, 16, 2, 4))
    there[0, :, :, :, 0, :] = np.einsum("bd,ef->bedf", c, same)
    there[0, :, :, :, 1, :] = np.einsum("bd,ef->bedf", s, same)
    there[1, :, :, :, 0, :] = np.einsum("bd,ef->bedf", -s, same)
    there[1, :, :, :, 1, :] = np.einsum("bd,ef->bedf", c, same)
    there = there.reshape(128, 128)
    phi = 2.0 * np.pi * np.outer(np.arange(16), np.arange(4)) / GRID
    twist = np.stack([np.cos(phi), np.sin(phi)])[:, :, None, :, None]
    twist = np.broadcast_to(twist, (2, 16, 4, 4, KEPT)).reshape(2, 64, 128)
    quarter = 2.0 * np.pi * np.outer(np.arange(4), np.arange(4)) / 4.0
    cq, sq = np.rint(np.cos(quarter)), np.rint(np.sin(quarter))
    kept = np.eye(KEPT)
    four = np.zeros((2, 4, KEPT, 2, 4, KEPT))
    four[0, :, :, 0] = np.einsum("la,kK->lkaK", cq, kept)
    four[1, :, :, 0] = np.einsum("la,kK->lkaK", sq, kept)
    four[0, :, :, 1] = np.einsum("la,kK->lkaK", -sq, kept)
    four[1, :, :, 1] = np.einsum("la,kK->lkaK", cq, kept)
    four = four.reshape(256, 256)
    return there, there.T.copy(), twist.astype(np.float32), four, four.T.copy()


def right_table(table):
    high, low = halves(table)
    return np.block([[high, low], [high, np.zeros_like(low)]])


def left_table(table):
    return np.ascontiguousarray(right_table(table.T).T)


def split(x):
    high = x.astype(jnp.bfloat16)
    low = (x - high.astype(jnp.float32)).astype(jnp.bfloat16)
    return high, low


def mm(a, b):
    return jnp.dot(a, b, preferred_element_type=jnp.float32)


def from_left(table_ref, data_ref):
    both = mm(table_ref[...], data_ref[...])
    return both[:128] + both[128:]


def from_left_chained(table_ref, data_ref):
    total = mm(table_ref[:128, :], data_ref[...])
    return total + mm(table_ref[128:, :128], data_ref[:128, :])


def from_right(data_ref, table_ref):
    results = []
    for l in range(PLANES):
        both = mm(data_ref[l * 192 : (l + 1) * 192, :], table_ref[l])
        results.append(both[:, :128] + both[:, 128:])
    return results


def gather_chunks(tiles):
    lane = lax.broadcasted_iota(jnp.int32, tiles[0].shape, 1)
    odd = lax.bitwise_and(lane, 32) != 0
    upper = lax.bitwise_and(lane, 64) != 0
    tiles = [jnp.where(odd, tiles[(j + 1) % 4], tiles[j]) for j in range(4)]
    tiles = [jnp.where(upper, tiles[(j + 2) % 4], tiles[j]) for j in range(4)]
    return [tiles[-k % 4] for k in range(4)]


def roll_chunks(tile, count):
    return pltpu.roll(tile, 32 * (count % 4), 1) if count % 4 else tile


def slopes_of(bits, low, high):
    at = [jnp.where(bit == 1, high, low) for bit in bits]
    far = [jnp.where(bit == 1, low, high) for bit in bits]

    def slope(corner, axis):
        value = None
        for other in range(3):
            if other != axis:
                factor = at[other] if corner >> other & 1 else far[other]
                value = factor if value is None else value * factor
        return value if corner >> axis & 1 else -value

    return slope


def macro_strain(point, conn_ref, disp_ref):
    low, high = jnp.float32(GAUSS_LOW), jnp.float32(GAUSS_HIGH)
    bits = [lax.bitwise_and(lax.shift_right_logical(point, d), 1) for d in range(3)]
    slope = slopes_of(bits, low, high)
    element = lax.shift_right_logical(point, 3)
    grad = [[jnp.float32(0.0)] * 3 for _ in range(3)]
    for corner in range(8):
        node = conn_ref[element, corner]
        for k in range(3):
            u = disp_ref[k, node]
            for d in range(3):
                grad[k][d] = grad[k][d] + slope(corner, d) * u
    strain = []
    for i, j in TENSOR_PAIRS:
        strain.append(grad[i][i] if i == j else 0.5 * (grad[i][j] + grad[j][i]))
    return strain


def material(elastic, phases, flags):
    hard = phases == 1
    limit = jnp.where(hard, 1.2, 0.3)
    ratio = jnp.where(
        hard,
        3.0 * SHEAR_MODULUS / (3.0 * SHEAR_MODULUS + 10.0),
        3.0 * SHEAR_MODULUS / (3.0 * SHEAR_MODULUS + 2.0),
    )
    active = flags.astype(jnp.float32)
    volume = elastic[0] + elastic[1] + elastic[2]
    third = volume * (1.0 / 3.0)
    trial = [2.0 * SHEAR_MODULUS * (elastic[a] - third) for a in range(3)]
    trial += [2.0 * SHEAR_MODULUS * elastic[a] for a in range(3, 6)]
    normal = trial[0] * trial[0] + trial[1] * trial[1] + trial[2] * trial[2]
    shear = trial[3] * trial[3] + trial[4] * trial[4] + trial[5] * trial[5]
    equivalent = jnp.sqrt(1.5 * (normal + 2.0 * shear))
    bounded = jnp.maximum(equivalent, limit)
    inverse = 1.0 / bounded
    scaled = ratio * active
    softening = 1.0 - scaled * (equivalent - limit) * inverse
    pressure = BULK_MODULUS * volume
    stress = [trial[a] * softening + pressure for a in range(3)]
    stress += [trial[a] * softening for a in range(3, 6)]
    weight = 3.0 * SHEAR_MODULUS * scaled * limit * (inverse * inverse * inverse)
    return stress, trial, softening, weight


def every_fourth(ref, start, plane):
    return ref[pl.ds(start + plane, 32, stride=4), :]


def put_rows(ref, rows, value):
    high, low = split(value)
    ref[rows, 0:128] = high
    ref[rows, 128:256] = low


def put_columns(ref, start, count, columns, value):
    high, low = split(value)
    ref[pl.ds(start, count), columns] = high
    ref[pl.ds(128 + start, count), columns] = low


def plane_waves():
    row = lax.broadcasted_iota(jnp.int32, (128, 128), 0)
    lane = lax.broadcasted_iota(jnp.int32, (128, 128), 1)
    ky = 4 * lax.shift_right_logical(row, 3) + lax.bitwise_and(row, 3)
    ky = jnp.where(ky < GRID // 2, ky, ky - GRID)
    return ky.astype(jnp.float32), lax.bitwise_and(lane, 31).astype(jnp.float32)


def forward_planes(xs, bs, depth, rows, out_ref):
    tiles = gather_chunks(from_right(xs, depth))
    tiles = [roll_chunks(tile, -s) for s, tile in enumerate(tiles)]
    for c in range(6):
        for s in range(4):
            block = tiles[s][c * 32 : (c + 1) * 32]
            put_columns(bs, s * 32, 32, pl.ds(c * 128, 128), block)
    spectrum = from_left(rows, bs)
    xx, yy, zz, yz, xz, xy = (spectrum[:, c * 128 : (c + 1) * 128] for c in range(6))
    wave_y, wave_z = plane_waves()
    fields = (xx, xy, xz, wave_y * yy + wave_z * yz, wave_y * yz + wave_z * zz)
    for c, field in enumerate(fields):
        out_ref[:, c * 8 : (c + 1) * 8, :] = field.reshape(16, 8, 128)


def backward_planes(in_ref, bs, xs, depth, rows):
    xx, xy, xz, y, z = (
        in_ref[:, c * 8 : (c + 1) * 8, :].reshape(128, 128) for c in range(FIELDS)
    )
    wave_y, wave_z = plane_waves()
    yy, zz = 2.0 * (wave_y * y), 2.0 * (wave_z * z)
    for c, value in enumerate((xx, yy, zz, wave_y * z + wave_z * y, xz, xy)):
        put_columns(bs, 0, 128, pl.ds(c * 128, 128), value)
    lines = from_left(rows, bs)
    tiles = [
        jnp.concatenate(
            [lines[s * 32 : (s + 1) * 32, c * 128 : (c + 1) * 128] for c in range(6)], axis=0
        )
        for s in range(4)
    ]
    tiles = [roll_chunks(tile, s) for s, tile in enumerate(tiles)]
    for l, tile in enumerate(gather_chunks(tiles)):
        put_rows(xs, pl.ds(l * 192, 192), tile)
    return from_right(xs, depth)


def basis_of(points, conn_ref):
    shape = (points, 128)
    lane = lax.broadcasted_iota(jnp.int32, shape, 1)
    point = lax.broadcasted_iota(jnp.int32, shape, 0)
    element = lax.shift_right_logical(point, 3)
    bits = [lax.bitwise_and(lax.shift_right_logical(point, d), 1) for d in range(3)]
    slope = slopes_of(bits, GAUSS_LOW, GAUSS_HIGH)
    node = lane // 3
    part = lane - 3 * node
    elements = conn_ref.shape[0]
    grad = [jnp.zeros(shape, jnp.float32) for _ in range(3)]
    for corner in range(8):
        owner = jnp.full(shape, conn_ref[0, corner], jnp.int32)
        for e in range(1, elements):
            owner = jnp.where(element == e, conn_ref[e, corner], owner)
        here = (owner == node) & (lane < 60)
        for d in range(3):
            grad[d] = grad[d] + jnp.where(here, slope(corner, d), 0.0)
    basis = []
    for i, k in TENSOR_PAIRS:
        if i == k:
            basis.append(jnp.where(part == i, grad[i], 0.0))
        else:
            value = jnp.where(part == i, 0.5 * grad[k], 0.0)
            basis.append(value + jnp.where(part == k, 0.5 * grad[i], 0.0))
    return jnp.concatenate(basis, axis=0)


def first_kernel(
    points, conn_hbm, disp_hbm, phase_hbm, flag_hbm, plastic_hbm, depth_hbm, rows_hbm,
    out_ref, macro_ref, basis_ref, turned_ref,
    conn_ref, disp_ref, phase_ref, flag_ref, plastic_ref, depth, rows, sems, xs, bs,
):
    pairs = (
        (conn_hbm, conn_ref), (disp_hbm, disp_ref), (plastic_hbm, plastic_ref),
        (phase_hbm, phase_ref), (flag_hbm.at[pl.ds(0, 128)], flag_ref),
        (depth_hbm, depth), (rows_hbm, rows),
    )
    copies = [pltpu.make_async_copy(a, b, sems.at[i]) for i, (a, b) in enumerate(pairs)]
    for copy in copies:
        copy.start()
    for copy in copies[:2]:
        copy.wait()
    macro = macro_strain(lax.axis_index("rve"), conn_ref, disp_ref)
    row = lax.broadcasted_iota(jnp.int32, (8, 128), 0)
    table = jnp.zeros((8, 128), jnp.float32)
    for c in range(6):
        table = jnp.where(row == c, macro[c], table)
    macro_ref[...] = table
    for copy in copies[2:]:
        copy.wait()
    for plane in range(PLANES):
        elastic = [macro[c] - every_fourth(plastic_ref, c * 128, plane) for c in range(6)]
        phases = every_fourth(phase_ref, 0, plane)
        flags = every_fourth(flag_ref, 0, plane)
        stress = material(elastic, phases, flags)[0]
        for c in range(6):
            put_rows(xs, pl.ds(plane * 192 + c * 32, 32), stress[c])
    basis = basis_of(points, conn_ref)
    basis_ref[...] = basis
    high, low = split(jnp.transpose(basis))
    turned_ref[0] = high
    turned_ref[1] = low
    forward_planes(xs, bs, depth, rows, out_ref)


def middle_kernel(
    macro_ref, phase_ref, flag_ref, plastic_ref, in_ref, back_depth, back_rows, depth, rows,
    out_ref, elastic_ref, xs, bs,
):
    macro = [macro_ref[c : c + 1, :] for c in range(6)]
    correction = backward_planes(in_ref, bs, xs, back_depth, back_rows)
    for plane in range(PLANES):
        elastic = []
        for c in range(6):
            at = plane * 192 + c * 32
            before = macro[c] - every_fourth(plastic_ref, c * 128, plane)
            after = before - correction[plane][c * 32 : (c + 1) * 32]
            elastic_ref[at : at + 32, :] = after
            elastic.append(after)
        phases = every_fourth(phase_ref, 0, plane)
        flags = every_fourth(flag_ref, 128, plane)
        stress = material(elastic, phases, flags)[0]
        for c in range(6):
            put_rows(xs, pl.ds(plane * 192 + c * 32, 32), stress[c])
    forward_planes(xs, bs, depth, rows, out_ref)


def last_kernel(
    phase_ref, flag_ref, elastic_ref, in_ref, back_depth, back_rows, out_ref, xs, bs
):
    correction = backward_planes(in_ref, bs, xs, back_depth, back_rows)
    sums = [None] * 28

    def collect(at, value):
        part = value.reshape(4, 8, 128)
        part = (part[0] + part[1]) + (part[2] + part[3])
        sums[at] = part if sums[at] is None else sums[at] + part

    for plane in range(PLANES):
        elastic = [
            elastic_ref[plane * 192 + c * 32 : plane * 192 + (c + 1) * 32, :]
            - correction[plane][c * 32 : (c + 1) * 32]
            for c in range(6)
        ]
        phases = every_fourth(phase_ref, 0, plane)
        flags = every_fourth(flag_ref, 256, plane)
        stress, trial, softening, weight = material(elastic, phases, flags)
        for c in range(6):
            collect(c, stress[c])
        collect(6, softening)
        at = 7
        for a in range(6):
            scaled = weight * trial[a]
            for b in range(a, 6):
                collect(at, scaled * trial[b])
                at += 1
    row = lax.broadcasted_iota(jnp.int32, (128, 128), 0)
    lines = jnp.zeros((128, 128), jnp.float32)

    def place(at, value):
        return jnp.where(row == at, jnp.broadcast_to(value, (128, 128)), lines)

    totals = [jnp.sum(value, axis=0, keepdims=True) for value in sums]
    for c in range(7):
        lines = place(c, totals[c])
    at = 7
    for a in range(6):
        for b in range(a, 6):
            lines = place(OUTER_AT + 6 * a + b, totals[at])
            if a != b:
                lines = place(OUTER_AT + 6 * b + a, totals[at])
            at += 1
    ones = jnp.ones((SLABS, 128), jnp.float32)
    line = lax.dot_general(
        ones, lines, (((1,), (1,)), ((), ())),
        precision=lax.Precision.HIGHEST, preferred_element_type=jnp.float32,
    )
    out_ref[...] = line.reshape(SLABS, 1, 128)


def column_kernel(in_ref, columns, back_columns, twist_ref, four, back_four, out_ref, bs, ys):
    count = 64 * FIELDS
    for c in range(FIELDS):
        block = in_ref[:, c * 8 : (c + 1) * 8, :].reshape(128, 128)
        put_columns(bs, 0, 128, pl.ds(c * 128, 128), block)
    mixed = from_left_chained(columns, bs)
    cosine, sine = twist_ref[0], twist_ref[1]

    def put(c, lanes, value):
        high, low = split(value)
        ys[pl.ds(c * 64, 64), lanes] = high
        ys[pl.ds(count + c * 64, 64), lanes] = low

    for c in range(FIELDS):
        lanes = slice(c * 128, (c + 1) * 128)
        real, imag = mixed[:64, lanes], mixed[64:, lanes]
        put(c, pl.ds(0, 128), real * cosine + imag * sine)
        put(c, pl.ds(128, 128), imag * cosine - real * sine)
    spectrum = mm(ys[:count, :], four[...])
    spectrum = spectrum + mm(ys[count:, :], four[...])
    xx, xy, xz, y, z = (spectrum[c * 64 : (c + 1) * 64] for c in range(FIELDS))

    shape = (64, 256)
    row = lax.broadcasted_iota(jnp.int32, shape, 0)
    lane = lax.broadcasted_iota(jnp.int32, shape, 1)
    lane = lax.bitwise_and(lane, 127)
    kx = 16 * lax.shift_right_logical(lane, 5) + lax.shift_right_logical(row, 2)
    ky = 4 * lax.axis_index("slab") + lax.bitwise_and(row, 3)
    kz = lax.bitwise_and(lane, 31)
    half = GRID // 2
    keep = (kx != half) & (ky != half) & (kx + ky + kz > 0)
    xi = [
        jnp.where(kx < half, kx, kx - GRID).astype(jnp.float32),
        jnp.where(ky < half, ky, ky - GRID).astype(jnp.float32),
        kz.astype(jnp.float32),
    ]
    length = xi[0] * xi[0] + xi[1] * xi[1] + xi[2] * xi[2]
    inverse = jnp.where(keep, 1.0 / jnp.maximum(length, 1.0), 0.0)
    coupling = (REFERENCE_LAME + REFERENCE_SHEAR) / (
        REFERENCE_SHEAR * (REFERENCE_LAME + 2.0 * REFERENCE_SHEAR)
    )
    scaled = inverse * (1.0 / (2.0 * REFERENCE_SHEAR))
    traction = [xi[0] * xx + xi[1] * xy + xi[2] * xz, xi[0] * xy + y, xi[0] * xz + z]
    load = xi[0] * traction[0] + xi[1] * traction[1] + xi[2] * traction[2]
    load = load * (inverse * (REFERENCE_SHEAR * coupling))
    field = [scaled * (traction[i] - xi[i] * load) for i in range(3)]
    put(0, slice(None), 2.0 * (xi[0] * field[0]))
    put(1, slice(None), xi[0] * field[1] + xi[1] * field[0])
    put(2, slice(None), xi[0] * field[2] + xi[2] * field[0])
    put(3, slice(None), field[1])
    put(4, slice(None), field[2])
    turned = mm(ys[:count, :], back_four[...])
    turned = turned + mm(ys[count:, :], back_four[...])
    for c in range(FIELDS):
        real, imag = turned[c * 64 : (c + 1) * 64, :128], turned[c * 64 : (c + 1) * 64, 128:]
        lanes = pl.ds(c * 128, 128)
        put_columns(bs, 0, 64, lanes, real * cosine - imag * sine)
        put_columns(bs, 64, 64, lanes, real * sine + imag * cosine)
    result = from_left_chained(back_columns, bs)
    for c in range(FIELDS):
        out_ref[:, c * 8 : (c + 1) * 8, :] = result[:, c * 128 : (c + 1) * 128].reshape(16, 8, 128)


def totals_kernel(in_ref, all_ref):
    line = jnp.sum(in_ref[...].reshape(SLABS, 128), axis=0, keepdims=True)
    all_ref[...] = jnp.broadcast_to(line[None], all_ref.shape)


def own_outputs(line, stress_ref, tangent_ref):
    stress_ref[...] = line[:, :6]
    at = lax.broadcasted_iota(jnp.int32, (1, 128), 1) - OUTER_AT
    a = at // 6
    b = at - 6 * a
    both = (a < 3) & (b < 3)
    shear = jnp.broadcast_to(line[:, 6:7], (1, 128)) * (2.0 * SHEAR_MODULUS)
    fixed = jnp.where(both, BULK_MODULUS - shear * (1.0 / 3.0), 0.0)
    fixed = fixed + jnp.where(a == b, shear, 0.0)
    whole = (fixed - line * jnp.where(b < 3, 1.0, 2.0)) * (1.0 / TANGENT_UNIT)
    for i in range(6):
        tangent_ref[i] = whole[:, OUTER_AT + 6 * i : OUTER_AT + 6 * i + 6]


def assembly_kernel(
    points, basis_ref, turned_ref, in_ref, stress_ref, tangent_ref, stiffness_ref, forces_ref
):
    half = points // 2
    own = lax.rem(lax.axis_index("rve") + points - half, points)
    own_outputs(in_ref[own] * (1.0 / VOXELS), stress_ref, tangent_ref)
    shape = (points, 128)
    sums = in_ref[...].reshape(points, 128) * (1.0 / VOXELS)
    sums = jnp.concatenate([sums[half:], sums[:half]], axis=0)
    basis = [basis_ref[a * points : (a + 1) * points, :] for a in range(6)]
    mean_shear = 2.0 * SHEAR_MODULUS * sums[:, 6:7]

    def column(at):
        return jnp.broadcast_to(sums[:, at : at + 1], shape)

    mean_shear = jnp.broadcast_to(mean_shear, shape)
    on_diagonal = BULK_MODULUS + mean_shear * (2.0 / 3.0)
    off_diagonal = BULK_MODULUS - mean_shear * (1.0 / 3.0)
    answers = []
    force = jnp.zeros(shape, jnp.float32)
    scale = QUADRATURE_WEIGHT / TANGENT_UNIT
    for a in range(6):
        total = jnp.zeros(shape, jnp.float32)
        for b in range(6):
            low, high = min(a, b), max(a, b)
            entry = -PAIR_WEIGHTS[b] * column(OUTER_AT + 6 * low + high)
            if a == b:
                entry = entry + (on_diagonal if a < 3 else mean_shear)
            elif a < 3 and b < 3:
                entry = entry + off_diagonal
            total = total + entry * basis[b]
        answers.append(total * (PAIR_WEIGHTS[a] * scale))
        force = force + basis[a] * (column(a) * (PAIR_WEIGHTS[a] * QUADRATURE_WEIGHT))
    high, low = split(jnp.concatenate(answers, axis=0))
    left_high, left_low = turned_ref[0], turned_ref[1]
    whole = mm(left_high, high) + (mm(left_low, high) + mm(left_high, low))
    stiffness_ref[...] = whole[:60, :60]
    line = jnp.sum(force, axis=0, keepdims=True)
    part8 = lax.broadcasted_iota(jnp.int32, (8, 128), 0)
    lane8 = lax.broadcasted_iota(jnp.int32, (8, 128), 1)
    spread = jnp.where(lane8 % 3 == part8, jnp.broadcast_to(line, (8, 128)), 0.0)
    pick_row = lax.broadcasted_iota(jnp.int32, (128, 128), 0)
    pick_col = lax.broadcasted_iota(jnp.int32, (128, 128), 1)
    pick = (pick_row // 3 == pick_col).astype(jnp.float32)
    forces = jnp.dot(
        spread, pick, precision=lax.Precision.HIGHEST, preferred_element_type=jnp.float32
    )
    forces_ref[...] = forces[:3, :20]


VMEM = pl.BlockSpec(memory_space=pltpu.VMEM)
HBM = pl.BlockSpec(memory_space=pltpu.HBM)
BF16 = jnp.bfloat16
F32 = jnp.float32
LIMIT = 16 * 1024 * 1024


def params():
    return pltpu.CompilerParams(vmem_limit_bytes=LIMIT)


def cost(flops, size):
    return pl.CostEstimate(flops=flops, bytes_accessed=size, transcendentals=0)


def plane_scratch():
    return [pltpu.VMEM((768, 256), BF16), pltpu.VMEM((256, 768), BF16)]


def exchange(array):
    return lax.all_to_all(array, "slab", split_axis=0, concat_axis=0, tiled=True)


def on_device(phase_ids, yield_flags, plastic_strain, displacements, connectivity):
    points = lax.axis_size("rve")

    def rows(array):
        lead = math.prod(array.shape[:-2])
        array = array.reshape(lead, PLANES, 32, 128)
        return jnp.transpose(array, (0, 2, 1, 3)).reshape(lead * 128, 128)

    phases = rows(phase_ids)
    flags = rows(yield_flags)
    plastic = rows(plastic_strain)

    there, back = depth_tables()
    depth, back_depth = (
        jnp.asarray(np.stack([right_table(np.roll(t, 32 * l, axis)) for l in range(PLANES)]))
        for t, axis in ((there, 1), (back, 0))
    )
    there, back = row_tables()
    line, back_line = jnp.asarray(left_table(there)), jnp.asarray(left_table(back))
    there, back, twist, four, back_four = column_tables()
    column, back_column = jnp.asarray(left_table(there)), jnp.asarray(left_table(back))
    twist = jnp.asarray(twist)
    four = jnp.asarray(four.astype(ml_dtypes.bfloat16))
    back_four = jnp.asarray(back_four.astype(ml_dtypes.bfloat16))

    block = jax.ShapeDtypeStruct((16, 8 * FIELDS, 128), F32)

    first = pl.pallas_call(
        functools.partial(first_kernel, points),
        out_shape=(
            block, jax.ShapeDtypeStruct((8, 128), F32),
            jax.ShapeDtypeStruct((6 * points, 128), F32),
            jax.ShapeDtypeStruct((2, 128, 6 * points), BF16),
        ),
        in_specs=[HBM] * 7, out_specs=(VMEM,) * 4,
        scratch_shapes=[
            pltpu.SMEM(connectivity.shape, jnp.int32), pltpu.SMEM(displacements.shape[::-1], F32),
            pltpu.VMEM((128, 128), jnp.int32), pltpu.VMEM((128, 128), jnp.int32),
            pltpu.VMEM((768, 128), F32), pltpu.VMEM((PLANES, 256, 256), BF16),
            pltpu.VMEM((256, 256), BF16),
            pltpu.SemaphoreType.DMA((7,)), *plane_scratch(),
        ],
        compiler_params=params(), cost_estimate=cost(400_000_000, 2_000_000), name="first",
    )
    columns = pl.pallas_call(
        column_kernel, out_shape=block,
        in_specs=[VMEM] * 6, out_specs=VMEM,
        scratch_shapes=[
            pltpu.VMEM((256, 128 * FIELDS), BF16), pltpu.VMEM((128 * FIELDS, 256), BF16),
        ],
        compiler_params=params(), cost_estimate=cost(400_000_000, 2_000_000), name="columns",
    )
    middle = pl.pallas_call(
        middle_kernel, out_shape=(block, jax.ShapeDtypeStruct((768, 128), F32)),
        in_specs=[VMEM] * 9, out_specs=(VMEM, VMEM),
        scratch_shapes=plane_scratch(), compiler_params=params(),
        cost_estimate=cost(800_000_000, 4_000_000), name="middle",
    )
    last = pl.pallas_call(
        last_kernel, out_shape=jax.ShapeDtypeStruct((SLABS, 1, 128), F32),
        in_specs=[VMEM] * 6, out_specs=VMEM,
        scratch_shapes=plane_scratch(), compiler_params=params(),
        cost_estimate=cost(400_000_000, 2_000_000), name="last",
    )
    totals = pl.pallas_call(
        totals_kernel, out_shape=jax.ShapeDtypeStruct((points, 1, 128), F32),
        in_specs=[VMEM], out_specs=VMEM, compiler_params=params(),
        cost_estimate=cost(10_000, 50_000), name="totals",
    )
    assembly = pl.pallas_call(
        functools.partial(assembly_kernel, points),
        out_shape=(
            jax.ShapeDtypeStruct((1, 6), F32), jax.ShapeDtypeStruct((6, 1, 6), F32),
            jax.ShapeDtypeStruct((60, 60), F32), jax.ShapeDtypeStruct((3, 20), F32),
        ),
        in_specs=[VMEM] * 3, out_specs=(VMEM,) * 4, compiler_params=params(),
        cost_estimate=cost(10_000_000, 200_000), name="assembly",
    )

    def apply_columns(array):
        return exchange(
            columns(exchange(array), column, back_column, twist, four, back_four)
        )

    operands = (connectivity, displacements.T, phases, flags, plastic, depth, line)
    spectrum, macro, basis, turned_basis = first(
        *(pltpu.with_memory_space_constraint(operand, pltpu.HBM) for operand in operands)
    )
    planes = apply_columns(spectrum)
    spectrum, elastic = middle(
        macro, phases, flags, plastic, planes, back_depth, back_line, depth, line
    )
    planes = apply_columns(spectrum)
    partial = last(phases, flags, elastic, planes, back_depth, back_line)
    everyone = totals(exchange(partial))
    half = points // 2
    turned = [*range(half, points), *range(half)]
    everyone = lax.all_to_all(
        everyone, "rve", 0, 0, tiled=True, axis_index_groups=[turned]
    )
    stress, tangent, stiffness, forces = assembly(basis, turned_basis, everyone)
    return (stress, jnp.transpose(tangent, (1, 0, 2)), forces.T, stiffness)


def solution(mesh):
    return jax.shard_map(
        on_device,
        mesh=mesh,
        in_specs=(
            P("slab", None),
            P("rve", None, "slab", None),
            P("rve", None, "slab", None),
            P(),
            P(),
        ),
        out_specs=(P("rve", None), P("rve", None, None), P(), P()),
        check_vma=False,
    )
```

```python
import functools
import math

import jax
import jax.numpy as jnp
import ml_dtypes
import numpy as np
from jax import lax
from jax.experimental import pallas as pl
from jax.experimental.pallas import tpu as pltpu
from jax.sharding import PartitionSpec as P

GRID = 64
ITERS = 2
SLABS = 16
PLANES = GRID // SLABS
KEPT = GRID // 2

SHEAR_MODULUS = 80.0
BULK_MODULUS = 160.0
REFERENCE_SHEAR = 80.0
REFERENCE_LAME = 160.0 - 160.0 / 3.0
TANGENT_UNIT = 100.0
QUADRATURE_WEIGHT = 0.125
PAIR_WEIGHTS = (1.0, 1.0, 1.0, 2.0, 2.0, 2.0)
TENSOR_PAIRS = ((0, 0), (1, 1), (2, 2), (1, 2), (0, 2), (0, 1))
VOXELS = float(GRID**3)
GAUSS_LOW = 0.5 - 0.5 / math.sqrt(3.0)
GAUSS_HIGH = 0.5 + 0.5 / math.sqrt(3.0)
OUTER_AT = 8
FIELDS = 5


def halves(table):
    high = table.astype(np.float32).astype(ml_dtypes.bfloat16)
    low = (table - high.astype(np.float64)).astype(np.float32).astype(ml_dtypes.bfloat16)
    return high, low


def depth_tables():
    z = np.arange(GRID)
    k = np.arange(KEPT)
    theta = 2.0 * np.pi * np.outer(z, k) / GRID
    forward = np.stack([np.cos(theta), -np.sin(theta)], axis=0)
    weight = np.where(k == 0, 1.0, 2.0) / VOXELS
    inverse = forward * weight[None, None, :]
    pair = np.eye(2)
    there = np.einsum("rR,pzk->rzRpk", pair, forward)
    back = np.einsum("rR,pzk->Rpkrz", pair, inverse)
    return there.reshape(128, 128), back.reshape(128, 128)


def row_tables():
    y = 2 * np.arange(32)[None, :] + np.arange(2)[:, None]
    ky = 4 * np.arange(16)[:, None] + np.arange(4)[None, :]
    theta = 2.0 * np.pi * np.einsum("de,rm->derm", ky, y) / GRID
    c, s = np.cos(theta), np.sin(theta)
    there = np.zeros((16, 2, 4, 2, 2, 32))
    there[:, 0, :, :, 0, :] = c
    there[:, 0, :, :, 1, :] = s
    there[:, 1, :, :, 0, :] = -s
    there[:, 1, :, :, 1, :] = c
    back = np.zeros((2, 2, 32, 16, 2, 4))
    ct, st = np.einsum("derm->rmde", c), np.einsum("derm->rmde", s)
    back[:, 0, :, :, 0, :] = ct
    back[:, 0, :, :, 1, :] = -st
    back[:, 1, :, :, 0, :] = st
    back[:, 1, :, :, 1, :] = ct
    return there.reshape(128, 128), back.reshape(128, 128)


def column_tables():
    d = np.arange(16)
    theta = 2.0 * np.pi * np.outer(d, d) / 16.0
    c, s = np.cos(theta), np.sin(theta)
    same = np.eye(4)
    there = np.zeros((2, 16, 4, 16, 2, 4))
    there[0, :, :, :, 0, :] = np.einsum("bd,ef->bedf", c, same)
    there[0, :, :, :, 1, :] = np.einsum("bd,ef->bedf", s, same)
    there[1, :, :, :, 0, :] = np.einsum("bd,ef->bedf", -s, same)
    there[1, :, :, :, 1, :] = np.einsum("bd,ef->bedf", c, same)
    there = there.reshape(128, 128)
    phi = 2.0 * np.pi * np.outer(np.arange(16), np.arange(4)) / GRID
    twist = np.stack([np.cos(phi), np.sin(phi)])[:, :, None, :, None]
    twist = np.broadcast_to(twist, (2, 16, 4, 4, KEPT)).reshape(2, 64, 128)
    quarter = 2.0 * np.pi * np.outer(np.arange(4), np.arange(4)) / 4.0
    cq, sq = np.rint(np.cos(quarter)), np.rint(np.sin(quarter))
    kept = np.eye(KEPT)
    four = np.zeros((2, 4, KEPT, 2, 4, KEPT))
    four[0, :, :, 0] = np.einsum("la,kK->lkaK", cq, kept)
    four[1, :, :, 0] = np.einsum("la,kK->lkaK", sq, kept)
    four[0, :, :, 1] = np.einsum("la,kK->lkaK", -sq, kept)
    four[1, :, :, 1] = np.einsum("la,kK->lkaK", cq, kept)
    four = four.reshape(256, 256)
    return there, there.T.copy(), twist.astype(np.float32), four, four.T.copy()


def right_table(table):
    high, low = halves(table)
    return np.block([[high, low], [high, np.zeros_like(low)]])


def left_table(table):
    return np.ascontiguousarray(right_table(table.T).T)


def split(x):
    high = x.astype(jnp.bfloat16)
    low = (x - high.astype(jnp.float32)).astype(jnp.bfloat16)
    return high, low


def mm(a, b):
    return jnp.dot(a, b, preferred_element_type=jnp.float32)


def from_left(table_ref, data_ref):
    both = mm(table_ref[...], data_ref[...])
    return both[:128] + both[128:]


def from_left_chained(table_ref, data_ref):
    total = mm(table_ref[:128, :], data_ref[...])
    return total + mm(table_ref[128:, :128], data_ref[:128, :])


def from_right(data_ref, table_ref):
    results = []
    for l in range(PLANES):
        both = mm(data_ref[l * 192 : (l + 1) * 192, :], table_ref[l])
        results.append(both[:, :128] + both[:, 128:])
    return results


def gather_chunks(tiles):
    lane = lax.broadcasted_iota(jnp.int32, tiles[0].shape, 1)
    odd = lax.bitwise_and(lane, 32) != 0
    upper = lax.bitwise_and(lane, 64) != 0
    tiles = [jnp.where(odd, tiles[(j + 1) % 4], tiles[j]) for j in range(4)]
    tiles = [jnp.where(upper, tiles[(j + 2) % 4], tiles[j]) for j in range(4)]
    return [tiles[-k % 4] for k in range(4)]


def roll_chunks(tile, count):
    return pltpu.roll(tile, 32 * (count % 4), 1) if count % 4 else tile


def slopes_of(bits, low, high):
    at = [jnp.where(bit == 1, high, low) for bit in bits]
    far = [jnp.where(bit == 1, low, high) for bit in bits]

    def slope(corner, axis):
        value = None
        for other in range(3):
            if other != axis:
                factor = at[other] if corner >> other & 1 else far[other]
                value = factor if value is None else value * factor
        return value if corner >> axis & 1 else -value

    return slope


def macro_strain(point, conn_ref, disp_ref):
    low, high = jnp.float32(GAUSS_LOW), jnp.float32(GAUSS_HIGH)
    bits = [lax.bitwise_and(lax.shift_right_logical(point, d), 1) for d in range(3)]
    slope = slopes_of(bits, low, high)
    element = lax.shift_right_logical(point, 3)
    grad = [[jnp.float32(0.0)] * 3 for _ in range(3)]
    for corner in range(8):
        node = conn_ref[element, corner]
        for k in range(3):
            u = disp_ref[k, node]
            for d in range(3):
                grad[k][d] = grad[k][d] + slope(corner, d) * u
    strain = []
    for i, j in TENSOR_PAIRS:
        strain.append(grad[i][i] if i == j else 0.5 * (grad[i][j] + grad[j][i]))
    return strain


def material(elastic, phases, flags):
    hard = phases == 1
    limit = jnp.where(hard, 1.2, 0.3)
    ratio = jnp.where(
        hard,
        3.0 * SHEAR_MODULUS / (3.0 * SHEAR_MODULUS + 10.0),
        3.0 * SHEAR_MODULUS / (3.0 * SHEAR_MODULUS + 2.0),
    )
    active = flags.astype(jnp.float32)
    volume = elastic[0] + elastic[1] + elastic[2]
    third = volume * (1.0 / 3.0)
    trial = [2.0 * SHEAR_MODULUS * (elastic[a] - third) for a in range(3)]
    trial += [2.0 * SHEAR_MODULUS * elastic[a] for a in range(3, 6)]
    normal = trial[0] * trial[0] + trial[1] * trial[1] + trial[2] * trial[2]
    shear = trial[3] * trial[3] + trial[4] * trial[4] + trial[5] * trial[5]
    equivalent = jnp.sqrt(1.5 * (normal + 2.0 * shear))
    bounded = jnp.maximum(equivalent, limit)
    inverse = 1.0 / bounded
    scaled = ratio * active
    softening = 1.0 - scaled * (equivalent - limit) * inverse
    pressure = BULK_MODULUS * volume
    stress = [trial[a] * softening + pressure for a in range(3)]
    stress += [trial[a] * softening for a in range(3, 6)]
    weight = 3.0 * SHEAR_MODULUS * scaled * limit * (inverse * inverse * inverse)
    return stress, trial, softening, weight


def every_fourth(ref, start, plane):
    return ref[pl.ds(start + plane, 32, stride=4), :]


def put_rows(ref, rows, value):
    high, low = split(value)
    ref[rows, 0:128] = high
    ref[rows, 128:256] = low


def put_columns(ref, start, count, columns, value):
    high, low = split(value)
    ref[pl.ds(start, count), columns] = high
    ref[pl.ds(128 + start, count), columns] = low


def plane_waves():
    row = lax.broadcasted_iota(jnp.int32, (8, 128), 0)
    lane = lax.broadcasted_iota(jnp.int32, (8, 128), 1)
    inner = lax.bitwise_and(row, 3).astype(jnp.float32)
    depth = lax.bitwise_and(lane, 31).astype(jnp.float32)
    starts = [4.0 * d if d < 8 else 4.0 * d - GRID for d in range(16)]
    wave_y = jnp.concatenate([inner + start for start in starts], axis=0)
    return wave_y, jnp.concatenate([depth] * 16, axis=0)


def forward_planes(xs, bs, depth, rows, out_ref):
    tiles = gather_chunks(from_right(xs, depth))
    tiles = [roll_chunks(tile, -s) for s, tile in enumerate(tiles)]
    for c in range(6):
        for s in range(4):
            block = tiles[s][c * 32 : (c + 1) * 32]
            put_columns(bs, s * 32, 32, pl.ds(c * 128, 128), block)
    spectrum = from_left(rows, bs)
    xx, yy, zz, yz, xz, xy = (spectrum[:, c * 128 : (c + 1) * 128] for c in range(6))
    wave_y, wave_z = plane_waves()
    fields = (xx, xy, xz, wave_y * yy + wave_z * yz, wave_y * yz + wave_z * zz)
    for c, field in enumerate(fields):
        out_ref[:, c * 8 : (c + 1) * 8, :] = field.reshape(16, 8, 128)


def backward_planes(in_ref, bs, xs, depth, rows):
    xx, xy, xz, y, z = (
        in_ref[:, c * 8 : (c + 1) * 8, :].reshape(128, 128) for c in range(FIELDS)
    )
    wave_y, wave_z = plane_waves()
    yy, zz = 2.0 * (wave_y * y), 2.0 * (wave_z * z)
    for c, value in enumerate((xx, yy, zz, wave_y * z + wave_z * y, xz, xy)):
        put_columns(bs, 0, 128, pl.ds(c * 128, 128), value)
    lines = from_left(rows, bs)
    tiles = [
        jnp.concatenate(
            [lines[s * 32 : (s + 1) * 32, c * 128 : (c + 1) * 128] for c in range(6)], axis=0
        )
        for s in range(4)
    ]
    tiles = [roll_chunks(tile, s) for s, tile in enumerate(tiles)]
    for l, tile in enumerate(gather_chunks(tiles)):
        put_rows(xs, pl.ds(l * 192, 192), tile)
    return from_right(xs, depth)


def basis_of(points, conn_ref):
    shape = (points, 128)
    lane = lax.broadcasted_iota(jnp.int32, shape, 1)
    point = lax.broadcasted_iota(jnp.int32, shape, 0)
    element = lax.shift_right_logical(point, 3)
    bits = [lax.bitwise_and(lax.shift_right_logical(point, d), 1) for d in range(3)]
    slope = slopes_of(bits, GAUSS_LOW, GAUSS_HIGH)
    node = lane // 3
    part = lane - 3 * node
    elements = conn_ref.shape[0]
    grad = [jnp.zeros(shape, jnp.float32) for _ in range(3)]
    for corner in range(8):
        owner = jnp.full(shape, conn_ref[0, corner], jnp.int32)
        for e in range(1, elements):
            owner = jnp.where(element == e, conn_ref[e, corner], owner)
        here = (owner == node) & (lane < 60)
        for d in range(3):
            grad[d] = grad[d] + jnp.where(here, slope(corner, d), 0.0)
    basis = []
    for i, k in TENSOR_PAIRS:
        if i == k:
            basis.append(jnp.where(part == i, grad[i], 0.0))
        else:
            value = jnp.where(part == i, 0.5 * grad[k], 0.0)
            basis.append(value + jnp.where(part == k, 0.5 * grad[i], 0.0))
    return jnp.concatenate(basis, axis=0)


def first_kernel(
    points, conn_hbm, disp_hbm, phase_hbm, flag_hbm, plastic_hbm, depth_hbm, rows_hbm,
    out_ref, macro_ref, basis_ref, turned_ref,
    conn_ref, disp_ref, phase_ref, flag_ref, plastic_ref, depth, rows, sems, xs, bs,
):
    pairs = (
        (conn_hbm, conn_ref), (disp_hbm, disp_ref), (plastic_hbm, plastic_ref),
        (phase_hbm, phase_ref), (flag_hbm.at[pl.ds(0, 128)], flag_ref),
        (depth_hbm, depth), (rows_hbm, rows),
    )
    copies = [pltpu.make_async_copy(a, b, sems.at[i]) for i, (a, b) in enumerate(pairs)]
    for copy in copies:
        copy.start()
    for copy in copies[:2]:
        copy.wait()
    macro = macro_strain(lax.axis_index("rve"), conn_ref, disp_ref)
    row = lax.broadcasted_iota(jnp.int32, (8, 128), 0)
    table = jnp.zeros((8, 128), jnp.float32)
    for c in range(6):
        table = jnp.where(row == c, macro[c], table)
    macro_ref[...] = table
    for copy in copies[2:5]:
        copy.wait()
    for plane in range(PLANES):
        elastic = [macro[c] - every_fourth(plastic_ref, c * 128, plane) for c in range(6)]
        phases = every_fourth(phase_ref, 0, plane)
        flags = every_fourth(flag_ref, 0, plane)
        stress = material(elastic, phases, flags)[0]
        for c in range(6):
            put_rows(xs, pl.ds(plane * 192 + c * 32, 32), stress[c])
    for copy in copies[5:]:
        copy.wait()
    basis = basis_of(points, conn_ref)
    basis_ref[...] = basis
    high, low = split(jnp.transpose(basis))
    turned_ref[0] = high
    turned_ref[1] = low
    forward_planes(xs, bs, depth, rows, out_ref)


def middle_kernel(
    macro_ref, phase_ref, flag_ref, plastic_ref, in_ref, back_depth, back_rows, depth, rows,
    out_ref, elastic_ref, xs, bs,
):
    macro = [macro_ref[c : c + 1, :] for c in range(6)]
    correction = backward_planes(in_ref, bs, xs, back_depth, back_rows)
    for plane in range(PLANES):
        elastic = []
        for c in range(6):
            at = plane * 192 + c * 32
            before = macro[c] - every_fourth(plastic_ref, c * 128, plane)
            after = before - correction[plane][c * 32 : (c + 1) * 32]
            elastic_ref[at : at + 32, :] = after
            elastic.append(after)
        phases = every_fourth(phase_ref, 0, plane)
        flags = every_fourth(flag_ref, 128, plane)
        stress = material(elastic, phases, flags)[0]
        for c in range(6):
            put_rows(xs, pl.ds(plane * 192 + c * 32, 32), stress[c])
    forward_planes(xs, bs, depth, rows, out_ref)


def last_kernel(
    phase_ref, flag_ref, elastic_ref, in_ref, back_depth, back_rows, out_ref, xs, bs
):
    correction = backward_planes(in_ref, bs, xs, back_depth, back_rows)
    sums = [None] * 28

    def collect(at, value):
        part = value.reshape(4, 8, 128)
        part = (part[0] + part[1]) + (part[2] + part[3])
        sums[at] = part if sums[at] is None else sums[at] + part

    for plane in range(PLANES):
        elastic = [
            elastic_ref[plane * 192 + c * 32 : plane * 192 + (c + 1) * 32, :]
            - correction[plane][c * 32 : (c + 1) * 32]
            for c in range(6)
        ]
        phases = every_fourth(phase_ref, 0, plane)
        flags = every_fourth(flag_ref, 256, plane)
        stress, trial, softening, weight = material(elastic, phases, flags)
        for c in range(6):
            collect(c, stress[c])
        collect(6, softening)
        at = 7
        for a in range(6):
            scaled = weight * trial[a]
            for b in range(a, 6):
                collect(at, scaled * trial[b])
                at += 1
    row = lax.broadcasted_iota(jnp.int32, (8, 128), 0)
    groups = [jnp.zeros((8, 128), jnp.float32)] * 16
    totals = [jnp.sum(value, axis=0, keepdims=True) for value in sums]

    def place(at, value):
        here = jnp.broadcast_to(value, (8, 128))
        groups[at // 8] = jnp.where(row == at % 8, here, groups[at // 8])

    for c in range(7):
        place(c, totals[c])
    at = 7
    for a in range(6):
        for b in range(a, 6):
            place(OUTER_AT + 6 * a + b, totals[at])
            if a != b:
                place(OUTER_AT + 6 * b + a, totals[at])
            at += 1
    lines = jnp.concatenate(groups, axis=0)
    ones = jnp.ones((SLABS, 128), jnp.float32)
    line = lax.dot_general(
        ones, lines, (((1,), (1,)), ((), ())),
        precision=lax.Precision.HIGHEST, preferred_element_type=jnp.float32,
    )
    out_ref[...] = line.reshape(SLABS, 1, 128)


def column_kernel(in_ref, columns, back_columns, twist_ref, four, back_four, out_ref, bs, ys):
    count = 64 * FIELDS
    for c in range(FIELDS):
        block = in_ref[:, c * 8 : (c + 1) * 8, :].reshape(128, 128)
        put_columns(bs, 0, 128, pl.ds(c * 128, 128), block)
    mixed = from_left_chained(columns, bs)
    cosine, sine = twist_ref[0], twist_ref[1]

    def put(c, lanes, value):
        high, low = split(value)
        ys[pl.ds(c * 64, 64), lanes] = high
        ys[pl.ds(count + c * 64, 64), lanes] = low

    for c in range(FIELDS):
        lanes = slice(c * 128, (c + 1) * 128)
        real, imag = mixed[:64, lanes], mixed[64:, lanes]
        put(c, pl.ds(0, 128), real * cosine + imag * sine)
        put(c, pl.ds(128, 128), imag * cosine - real * sine)
    spectrum = mm(ys[:count, :], four[...])
    spectrum = spectrum + mm(ys[count:, :], four[...])
    xx, xy, xz, y, z = (spectrum[c * 64 : (c + 1) * 64] for c in range(FIELDS))

    shape = (64, 128)
    row = lax.broadcasted_iota(jnp.int32, shape, 0)
    lane = lax.broadcasted_iota(jnp.int32, shape, 1)
    kx = 16 * lax.shift_right_logical(lane, 5) + lax.shift_right_logical(row, 2)
    ky = 4 * lax.axis_index("slab") + lax.bitwise_and(row, 3)
    kz = lax.bitwise_and(lane, 31)
    half = GRID // 2
    keep = (kx != half) & (ky != half) & (kx + ky + kz > 0)
    xi = [
        jnp.where(kx < half, kx, kx - GRID).astype(jnp.float32),
        jnp.where(ky < half, ky, ky - GRID).astype(jnp.float32),
        kz.astype(jnp.float32),
    ]
    length = xi[0] * xi[0] + xi[1] * xi[1] + xi[2] * xi[2]
    inverse = jnp.where(keep, 1.0 / jnp.maximum(length, 1.0), 0.0)
    coupling = (REFERENCE_LAME + REFERENCE_SHEAR) / (
        REFERENCE_SHEAR * (REFERENCE_LAME + 2.0 * REFERENCE_SHEAR)
    )
    xi = [jnp.concatenate([value, value], axis=1) for value in xi]
    inverse = jnp.concatenate([inverse, inverse], axis=1)
    scaled = inverse * (1.0 / (2.0 * REFERENCE_SHEAR))
    traction = [xi[0] * xx + xi[1] * xy + xi[2] * xz, xi[0] * xy + y, xi[0] * xz + z]
    load = xi[0] * traction[0] + xi[1] * traction[1] + xi[2] * traction[2]
    load = load * (inverse * (REFERENCE_SHEAR * coupling))
    field = [scaled * (traction[i] - xi[i] * load) for i in range(3)]
    put(0, slice(None), 2.0 * (xi[0] * field[0]))
    put(1, slice(None), xi[0] * field[1] + xi[1] * field[0])
    put(2, slice(None), xi[0] * field[2] + xi[2] * field[0])
    put(3, slice(None), field[1])
    put(4, slice(None), field[2])
    turned = mm(ys[:count, :], back_four[...])
    turned = turned + mm(ys[count:, :], back_four[...])
    for c in range(FIELDS):
        real, imag = turned[c * 64 : (c + 1) * 64, :128], turned[c * 64 : (c + 1) * 64, 128:]
        lanes = pl.ds(c * 128, 128)
        put_columns(bs, 0, 64, lanes, real * cosine - imag * sine)
        put_columns(bs, 64, 64, lanes, real * sine + imag * cosine)
    result = from_left_chained(back_columns, bs)
    for c in range(FIELDS):
        out_ref[:, c * 8 : (c + 1) * 8, :] = result[:, c * 128 : (c + 1) * 128].reshape(16, 8, 128)


def totals_kernel(in_ref, all_ref):
    line = jnp.sum(in_ref[...].reshape(SLABS, 128), axis=0, keepdims=True)
    all_ref[...] = jnp.broadcast_to(line[None], all_ref.shape)


def own_outputs(line, stress_ref, tangent_ref):
    stress_ref[...] = line[:, :6]
    at = lax.broadcasted_iota(jnp.int32, (1, 128), 1) - OUTER_AT
    a = at // 6
    b = at - 6 * a
    both = (a < 3) & (b < 3)
    shear = jnp.broadcast_to(line[:, 6:7], (1, 128)) * (2.0 * SHEAR_MODULUS)
    fixed = jnp.where(both, BULK_MODULUS - shear * (1.0 / 3.0), 0.0)
    fixed = fixed + jnp.where(a == b, shear, 0.0)
    whole = (fixed - line * jnp.where(b < 3, 1.0, 2.0)) * (1.0 / TANGENT_UNIT)
    for i in range(6):
        tangent_ref[i] = whole[:, OUTER_AT + 6 * i : OUTER_AT + 6 * i + 6]


def assembly_kernel(
    points, basis_ref, turned_ref, in_ref, stress_ref, tangent_ref, stiffness_ref, forces_ref
):
    start = first_of(points)
    own = lax.rem(lax.axis_index("rve") + points - start, points)
    own_outputs(in_ref[own] * (1.0 / VOXELS), stress_ref, tangent_ref)
    shape = (points, 128)
    sums = in_ref[...].reshape(points, 128) * (1.0 / VOXELS)
    sums = jnp.concatenate([sums[points - start :], sums[: points - start]], axis=0)
    basis = [basis_ref[a * points : (a + 1) * points, :] for a in range(6)]
    mean_shear = 2.0 * SHEAR_MODULUS * sums[:, 6:7]

    def column(at):
        return jnp.broadcast_to(sums[:, at : at + 1], shape)

    mean_shear = jnp.broadcast_to(mean_shear, shape)
    on_diagonal = BULK_MODULUS + mean_shear * (2.0 / 3.0)
    off_diagonal = BULK_MODULUS - mean_shear * (1.0 / 3.0)
    answers = []
    force = jnp.zeros(shape, jnp.float32)
    scale = QUADRATURE_WEIGHT / TANGENT_UNIT
    for a in range(6):
        total = jnp.zeros(shape, jnp.float32)
        for b in range(6):
            low, high = min(a, b), max(a, b)
            entry = -PAIR_WEIGHTS[b] * column(OUTER_AT + 6 * low + high)
            if a == b:
                entry = entry + (on_diagonal if a < 3 else mean_shear)
            elif a < 3 and b < 3:
                entry = entry + off_diagonal
            total = total + entry * basis[b]
        answers.append(total * (PAIR_WEIGHTS[a] * scale))
        force = force + basis[a] * (column(a) * (PAIR_WEIGHTS[a] * QUADRATURE_WEIGHT))
    high, low = split(jnp.concatenate(answers, axis=0))
    left_high, left_low = turned_ref[0], turned_ref[1]
    whole = mm(left_high, high) + (mm(left_low, high) + mm(left_high, low))
    stiffness_ref[...] = whole[:60, :60]
    line = jnp.sum(force, axis=0, keepdims=True)
    part8 = lax.broadcasted_iota(jnp.int32, (8, 128), 0)
    lane8 = lax.broadcasted_iota(jnp.int32, (8, 128), 1)
    spread = jnp.where(lane8 % 3 == part8, jnp.broadcast_to(line, (8, 128)), 0.0)
    pick_row = lax.broadcasted_iota(jnp.int32, (128, 128), 0)
    pick_col = lax.broadcasted_iota(jnp.int32, (128, 128), 1)
    pick = (pick_row // 3 == pick_col).astype(jnp.float32)
    forces = jnp.dot(
        spread, pick, precision=lax.Precision.HIGHEST, preferred_element_type=jnp.float32
    )
    forces_ref[...] = forces[:3, :20]


VMEM = pl.BlockSpec(memory_space=pltpu.VMEM)
HBM = pl.BlockSpec(memory_space=pltpu.HBM)
BF16 = jnp.bfloat16
F32 = jnp.float32
LIMIT = 16 * 1024 * 1024


def params():
    return pltpu.CompilerParams(vmem_limit_bytes=LIMIT)


def cost(flops, size):
    return pl.CostEstimate(flops=flops, bytes_accessed=size, transcendentals=0)


def plane_scratch():
    return [pltpu.VMEM((768, 256), BF16), pltpu.VMEM((256, 768), BF16)]


def first_of(points):
    return points // 2 + 1 if points > 1 else 0


def exchange(array):
    return lax.all_to_all(array, "slab", split_axis=0, concat_axis=0, tiled=True)


def on_device(phase_ids, yield_flags, plastic_strain, displacements, connectivity):
    points = lax.axis_size("rve")

    def rows(array):
        lead = math.prod(array.shape[:-2])
        array = array.reshape(lead, PLANES, 32, 128)
        return jnp.transpose(array, (0, 2, 1, 3)).reshape(lead * 128, 128)

    phases = rows(phase_ids)
    flags = rows(yield_flags)
    plastic = rows(plastic_strain)

    there, back = depth_tables()
    depth, back_depth = (
        jnp.asarray(np.stack([right_table(np.roll(t, 32 * l, axis)) for l in range(PLANES)]))
        for t, axis in ((there, 1), (back, 0))
    )
    there, back = row_tables()
    line, back_line = jnp.asarray(left_table(there)), jnp.asarray(left_table(back))
    there, back, twist, four, back_four = column_tables()
    column, back_column = jnp.asarray(left_table(there)), jnp.asarray(left_table(back))
    twist = jnp.asarray(twist)
    four = jnp.asarray(four.astype(ml_dtypes.bfloat16))
    back_four = jnp.asarray(back_four.astype(ml_dtypes.bfloat16))

    block = jax.ShapeDtypeStruct((16, 8 * FIELDS, 128), F32)

    first = pl.pallas_call(
        functools.partial(first_kernel, points),
        out_shape=(
            block, jax.ShapeDtypeStruct((8, 128), F32),
            jax.ShapeDtypeStruct((6 * points, 128), F32),
            jax.ShapeDtypeStruct((2, 128, 6 * points), BF16),
        ),
        in_specs=[HBM] * 7, out_specs=(VMEM,) * 4,
        scratch_shapes=[
            pltpu.SMEM(connectivity.shape, jnp.int32), pltpu.SMEM(displacements.shape[::-1], F32),
            pltpu.VMEM((128, 128), jnp.int32), pltpu.VMEM((128, 128), jnp.int32),
            pltpu.VMEM((768, 128), F32), pltpu.VMEM((PLANES, 256, 256), BF16),
            pltpu.VMEM((256, 256), BF16),
            pltpu.SemaphoreType.DMA((7,)), *plane_scratch(),
        ],
        compiler_params=params(), cost_estimate=cost(400_000_000, 2_000_000), name="first",
    )
    columns = pl.pallas_call(
        column_kernel, out_shape=block,
        in_specs=[VMEM] * 6, out_specs=VMEM,
        scratch_shapes=[
            pltpu.VMEM((256, 128 * FIELDS), BF16), pltpu.VMEM((128 * FIELDS, 256), BF16),
        ],
        compiler_params=params(), cost_estimate=cost(400_000_000, 2_000_000), name="columns",
    )
    middle = pl.pallas_call(
        middle_kernel, out_shape=(block, jax.ShapeDtypeStruct((768, 128), F32)),
        in_specs=[VMEM] * 9, out_specs=(VMEM, VMEM),
        scratch_shapes=plane_scratch(), compiler_params=params(),
        cost_estimate=cost(800_000_000, 4_000_000), name="middle",
    )
    last = pl.pallas_call(
        last_kernel, out_shape=jax.ShapeDtypeStruct((SLABS, 1, 128), F32),
        in_specs=[VMEM] * 6, out_specs=VMEM,
        scratch_shapes=plane_scratch(), compiler_params=params(),
        cost_estimate=cost(400_000_000, 2_000_000), name="last",
    )
    totals = pl.pallas_call(
        totals_kernel, out_shape=jax.ShapeDtypeStruct((points, 1, 128), F32),
        in_specs=[VMEM], out_specs=VMEM, compiler_params=params(),
        cost_estimate=cost(10_000, 50_000), name="totals",
    )
    assembly = pl.pallas_call(
        functools.partial(assembly_kernel, points),
        out_shape=(
            jax.ShapeDtypeStruct((1, 6), F32), jax.ShapeDtypeStruct((6, 1, 6), F32),
            jax.ShapeDtypeStruct((60, 60), F32), jax.ShapeDtypeStruct((3, 20), F32),
        ),
        in_specs=[VMEM] * 3, out_specs=(VMEM,) * 4, compiler_params=params(),
        cost_estimate=cost(10_000_000, 200_000), name="assembly",
    )

    def apply_columns(array):
        return exchange(
            columns(exchange(array), column, back_column, twist, four, back_four)
        )

    operands = (connectivity, displacements.T, phases, flags, plastic, depth, line)
    spectrum, macro, basis, turned_basis = first(
        *(pltpu.with_memory_space_constraint(operand, pltpu.HBM) for operand in operands)
    )
    planes = apply_columns(spectrum)
    spectrum, elastic = middle(
        macro, phases, flags, plastic, planes, back_depth, back_line, depth, line
    )
    planes = apply_columns(spectrum)
    partial = last(phases, flags, elastic, planes, back_depth, back_line)
    everyone = totals(exchange(partial))
    turned = [(g + first_of(points)) % points for g in range(points)]
    everyone = lax.all_to_all(
        everyone, "rve", 0, 0, tiled=True, axis_index_groups=[turned]
    )
    stress, tangent, stiffness, forces = assembly(basis, turned_basis, everyone)
    return (stress, jnp.transpose(tangent, (1, 0, 2)), forces.T, stiffness)


def solution(mesh):
    return jax.shard_map(
        on_device,
        mesh=mesh,
        in_specs=(
            P("slab", None),
            P("rve", None, "slab", None),
            P("rve", None, "slab", None),
            P(),
            P(),
        ),
        out_specs=(P("rve", None), P("rve", None, None), P(), P()),
        check_vma=False,
    )
```

```python
import functools
import math

import jax
import jax.numpy as jnp
import ml_dtypes
import numpy as np
from jax import lax
from jax.experimental import pallas as pl
from jax.experimental.pallas import tpu as pltpu
from jax.sharding import PartitionSpec as P

GRID = 64
ITERS = 2
SLABS = 16
PLANES = GRID // SLABS
KEPT = GRID // 2

SHEAR_MODULUS = 80.0
BULK_MODULUS = 160.0
REFERENCE_SHEAR = 80.0
REFERENCE_LAME = 160.0 - 160.0 / 3.0
TANGENT_UNIT = 100.0
QUADRATURE_WEIGHT = 0.125
PAIR_WEIGHTS = (1.0, 1.0, 1.0, 2.0, 2.0, 2.0)
TENSOR_PAIRS = ((0, 0), (1, 1), (2, 2), (1, 2), (0, 2), (0, 1))
VOXELS = float(GRID**3)
GAUSS_LOW = 0.5 - 0.5 / math.sqrt(3.0)
GAUSS_HIGH = 0.5 + 0.5 / math.sqrt(3.0)
OUTER_AT = 8
FIELDS = 5


def halves(table):
    high = table.astype(np.float32).astype(ml_dtypes.bfloat16)
    low = (table - high.astype(np.float64)).astype(np.float32).astype(ml_dtypes.bfloat16)
    return high, low


def depth_tables():
    z = np.arange(GRID)
    k = np.arange(KEPT)
    theta = 2.0 * np.pi * np.outer(z, k) / GRID
    forward = np.stack([np.cos(theta), -np.sin(theta)], axis=0)
    weight = np.where(k == 0, 1.0, 2.0) / VOXELS
    inverse = forward * weight[None, None, :]
    pair = np.eye(2)
    there = np.einsum("rR,pzk->rzRpk", pair, forward)
    back = np.einsum("rR,pzk->Rpkrz", pair, inverse)
    return there.reshape(128, 128), back.reshape(128, 128)


def row_tables():
    y = 2 * np.arange(32)[None, :] + np.arange(2)[:, None]
    ky = 4 * np.arange(16)[:, None] + np.arange(4)[None, :]
    theta = 2.0 * np.pi * np.einsum("de,rm->derm", ky, y) / GRID
    c, s = np.cos(theta), np.sin(theta)
    there = np.zeros((16, 2, 4, 2, 2, 32))
    there[:, 0, :, :, 0, :] = c
    there[:, 0, :, :, 1, :] = s
    there[:, 1, :, :, 0, :] = -s
    there[:, 1, :, :, 1, :] = c
    back = np.zeros((2, 2, 32, 16, 2, 4))
    ct, st = np.einsum("derm->rmde", c), np.einsum("derm->rmde", s)
    back[:, 0, :, :, 0, :] = ct
    back[:, 0, :, :, 1, :] = -st
    back[:, 1, :, :, 0, :] = st
    back[:, 1, :, :, 1, :] = ct
    return there.reshape(128, 128), back.reshape(128, 128)


def column_tables():
    d = np.arange(16)
    theta = 2.0 * np.pi * np.outer(d, d) / 16.0
    c, s = np.cos(theta), np.sin(theta)
    same = np.eye(4)
    there = np.zeros((2, 16, 4, 16, 2, 4))
    there[0, :, :, :, 0, :] = np.einsum("bd,ef->bedf", c, same)
    there[0, :, :, :, 1, :] = np.einsum("bd,ef->bedf", s, same)
    there[1, :, :, :, 0, :] = np.einsum("bd,ef->bedf", -s, same)
    there[1, :, :, :, 1, :] = np.einsum("bd,ef->bedf", c, same)
    there = there.reshape(128, 128)
    phi = 2.0 * np.pi * np.outer(np.arange(16), np.arange(4)) / GRID
    twist = np.stack([np.cos(phi), np.sin(phi)])[:, :, None, :, None]
    twist = np.broadcast_to(twist, (2, 16, 4, 4, KEPT)).reshape(2, 64, 128)
    quarter = 2.0 * np.pi * np.outer(np.arange(4), np.arange(4)) / 4.0
    cq, sq = np.rint(np.cos(quarter)), np.rint(np.sin(quarter))
    kept = np.eye(KEPT)
    four = np.zeros((2, 4, KEPT, 2, 4, KEPT))
    four[0, :, :, 0] = np.einsum("la,kK->lkaK", cq, kept)
    four[1, :, :, 0] = np.einsum("la,kK->lkaK", sq, kept)
    four[0, :, :, 1] = np.einsum("la,kK->lkaK", -sq, kept)
    four[1, :, :, 1] = np.einsum("la,kK->lkaK", cq, kept)
    four = four.reshape(256, 256)
    return there, there.T.copy(), twist.astype(np.float32), four, four.T.copy()


def right_table(table):
    high, low = halves(table)
    return np.block([[high, low], [high, np.zeros_like(low)]])


def left_table(table):
    return np.ascontiguousarray(right_table(table.T).T)


def split(x):
    high = x.astype(jnp.bfloat16)
    low = (x - high.astype(jnp.float32)).astype(jnp.bfloat16)
    return high, low


def mm(a, b):
    return jnp.dot(a, b, preferred_element_type=jnp.float32)


def from_left_values(table_ref, pairs):
    both = jnp.concatenate([jnp.concatenate(pair, axis=0) for pair in pairs], axis=1)
    total = mm(table_ref[:128, :], both)
    return total + mm(table_ref[128:, :128], both[:128])


def from_left_halves(table_ref, pairs):
    both = jnp.concatenate([jnp.concatenate(pair, axis=0) for pair in pairs], axis=1)
    both = mm(table_ref[...], both)
    return both[:128] + both[128:]


def from_right(tiles, table_ref):
    results = []
    for l, tile in enumerate(tiles):
        both = mm(jnp.concatenate(split(tile), axis=1), table_ref[l])
        results.append(both[:, :128] + both[:, 128:])
    return results


def gather_chunks(tiles):
    lane = lax.broadcasted_iota(jnp.int32, tiles[0].shape, 1)
    odd = lax.bitwise_and(lane, 32) != 0
    upper = lax.bitwise_and(lane, 64) != 0
    tiles = [jnp.where(odd, tiles[(j + 1) % 4], tiles[j]) for j in range(4)]
    tiles = [jnp.where(upper, tiles[(j + 2) % 4], tiles[j]) for j in range(4)]
    return [tiles[-k % 4] for k in range(4)]


def roll_chunks(tile, count):
    return pltpu.roll(tile, 32 * (count % 4), 1) if count % 4 else tile


def slopes_of(bits, low, high):
    at = [jnp.where(bit == 1, high, low) for bit in bits]
    far = [jnp.where(bit == 1, low, high) for bit in bits]

    def slope(corner, axis):
        value = None
        for other in range(3):
            if other != axis:
                factor = at[other] if corner >> other & 1 else far[other]
                value = factor if value is None else value * factor
        return value if corner >> axis & 1 else -value

    return slope


def point_slopes(point):
    low, high = jnp.float32(GAUSS_LOW), jnp.float32(GAUSS_HIGH)
    bits = [lax.bitwise_and(lax.shift_right_logical(point, d), 1) for d in range(3)]
    slope = slopes_of(bits, low, high)
    return [[slope(corner, d) for d in range(3)] for corner in range(8)]


def macro_strain(point, slopes, conn_ref, disp_ref):
    element = lax.shift_right_logical(point, 3)
    grad = [[jnp.float32(0.0)] * 3 for _ in range(3)]
    for corner in range(8):
        node = conn_ref[element, corner]
        for k in range(3):
            u = disp_ref[k, node]
            for d in range(3):
                grad[k][d] = grad[k][d] + slopes[corner][d] * u
    strain = []
    for i, j in TENSOR_PAIRS:
        strain.append(grad[i][i] if i == j else 0.5 * (grad[i][j] + grad[j][i]))
    return strain


def material(elastic, phases, flags):
    hard = phases == 1
    limit = jnp.where(hard, 1.2, 0.3)
    ratio = jnp.where(
        hard,
        3.0 * SHEAR_MODULUS / (3.0 * SHEAR_MODULUS + 10.0),
        3.0 * SHEAR_MODULUS / (3.0 * SHEAR_MODULUS + 2.0),
    )
    active = flags.astype(jnp.float32)
    volume = elastic[0] + elastic[1] + elastic[2]
    third = volume * (1.0 / 3.0)
    trial = [2.0 * SHEAR_MODULUS * (elastic[a] - third) for a in range(3)]
    trial += [2.0 * SHEAR_MODULUS * elastic[a] for a in range(3, 6)]
    normal = trial[0] * trial[0] + trial[1] * trial[1] + trial[2] * trial[2]
    shear = trial[3] * trial[3] + trial[4] * trial[4] + trial[5] * trial[5]
    equivalent = jnp.sqrt(1.5 * (normal + 2.0 * shear))
    bounded = jnp.maximum(equivalent, limit)
    inverse = 1.0 / bounded
    scaled = ratio * active
    softening = 1.0 - scaled * (equivalent - limit) * inverse
    pressure = BULK_MODULUS * volume
    stress = [trial[a] * softening + pressure for a in range(3)]
    stress += [trial[a] * softening for a in range(3, 6)]
    weight = 3.0 * SHEAR_MODULUS * scaled * limit * (inverse * inverse * inverse)
    return stress, trial, softening, weight


def every_fourth(ref, start, plane):
    return ref[pl.ds(start + plane, 32, stride=4), :]


def plane_waves():
    row = lax.broadcasted_iota(jnp.int32, (8, 128), 0)
    lane = lax.broadcasted_iota(jnp.int32, (8, 128), 1)
    inner = lax.bitwise_and(row, 3).astype(jnp.float32)
    depth = lax.bitwise_and(lane, 31).astype(jnp.float32)
    starts = [4.0 * d if d < 8 else 4.0 * d - GRID for d in range(16)]
    wave_y = jnp.concatenate([inner + start for start in starts], axis=0)
    return wave_y, jnp.concatenate([depth] * 16, axis=0)


def forward_planes(stresses, depth, rows, out_ref):
    tiles = gather_chunks(from_right(stresses, depth))
    tiles = [roll_chunks(tile, -s) for s, tile in enumerate(tiles)]
    pairs = [
        split(jnp.concatenate([tile[c * 32 : (c + 1) * 32] for tile in tiles], axis=0))
        for c in range(6)
    ]
    spectrum = from_left_halves(rows, pairs)
    xx, yy, zz, yz, xz, xy = (spectrum[:, c * 128 : (c + 1) * 128] for c in range(6))
    wave_y, wave_z = plane_waves()
    fields = (xx, xy, xz, wave_y * yy + wave_z * yz, wave_y * yz + wave_z * zz)
    for c, field in enumerate(fields):
        out_ref[:, c * 8 : (c + 1) * 8, :] = field.reshape(16, 8, 128)


def backward_planes(in_ref, depth, rows):
    xx, xy, xz, y, z = (
        in_ref[:, c * 8 : (c + 1) * 8, :].reshape(128, 128) for c in range(FIELDS)
    )
    wave_y, wave_z = plane_waves()
    yy, zz = 2.0 * (wave_y * y), 2.0 * (wave_z * z)
    pairs = [split(value) for value in (xx, yy, zz, wave_y * z + wave_z * y, xz, xy)]
    lines = from_left_values(rows, pairs)
    tiles = [
        jnp.concatenate(
            [lines[s * 32 : (s + 1) * 32, c * 128 : (c + 1) * 128] for c in range(6)], axis=0
        )
        for s in range(4)
    ]
    tiles = [roll_chunks(tile, s) for s, tile in enumerate(tiles)]
    return from_right(gather_chunks(tiles), depth)


def basis_of(points, conn_ref):
    shape = (points, 128)
    lane = lax.broadcasted_iota(jnp.int32, shape, 1)
    point = lax.broadcasted_iota(jnp.int32, shape, 0)
    element = lax.shift_right_logical(point, 3)
    bits = [lax.bitwise_and(lax.shift_right_logical(point, d), 1) for d in range(3)]
    slope = slopes_of(bits, GAUSS_LOW, GAUSS_HIGH)
    node = lane // 3
    part = lane - 3 * node
    elements = conn_ref.shape[0]
    grad = [jnp.zeros(shape, jnp.float32) for _ in range(3)]
    for corner in range(8):
        owner = jnp.full(shape, conn_ref[0, corner], jnp.int32)
        for e in range(1, elements):
            owner = jnp.where(element == e, conn_ref[e, corner], owner)
        here = (owner == node) & (lane < 60)
        for d in range(3):
            grad[d] = grad[d] + jnp.where(here, slope(corner, d), 0.0)
    basis = []
    for i, k in TENSOR_PAIRS:
        if i == k:
            basis.append(jnp.where(part == i, grad[i], 0.0))
        else:
            value = jnp.where(part == i, 0.5 * grad[k], 0.0)
            basis.append(value + jnp.where(part == k, 0.5 * grad[i], 0.0))
    return jnp.concatenate(basis, axis=0)


def first_kernel(
    points, conn_hbm, disp_hbm, phase_hbm, flag_hbm, plastic_hbm, depth_hbm, rows_hbm,
    out_ref, macro_ref, basis_ref, turned_ref,
    conn_ref, disp_ref, phase_ref, flag_ref, plastic_ref, depth, rows, sems,
):
    pairs = (
        (conn_hbm, conn_ref), (disp_hbm, disp_ref), (plastic_hbm, plastic_ref),
        (phase_hbm, phase_ref), (flag_hbm.at[pl.ds(0, 128)], flag_ref),
        (depth_hbm, depth), (rows_hbm, rows),
    )
    copies = [pltpu.make_async_copy(a, b, sems.at[i]) for i, (a, b) in enumerate(pairs)]
    for copy in copies:
        copy.start()
    point = lax.axis_index("rve")
    slopes = point_slopes(point)
    for copy in copies[:2]:
        copy.wait()
    macro = macro_strain(point, slopes, conn_ref, disp_ref)
    row = lax.broadcasted_iota(jnp.int32, (8, 128), 0)
    table = jnp.zeros((8, 128), jnp.float32)
    for c in range(6):
        table = jnp.where(row == c, macro[c], table)
    macro_ref[...] = table
    for copy in copies[2:5]:
        copy.wait()
    stresses = []
    for plane in range(PLANES):
        elastic = [macro[c] - every_fourth(plastic_ref, c * 128, plane) for c in range(6)]
        phases = every_fourth(phase_ref, 0, plane)
        flags = every_fourth(flag_ref, 0, plane)
        stress = material(elastic, phases, flags)[0]
        stresses.append(jnp.concatenate(stress, axis=0))
    for copy in copies[5:]:
        copy.wait()
    basis = basis_of(points, conn_ref)
    basis_ref[...] = basis
    high, low = split(jnp.transpose(basis))
    turned_ref[0] = high
    turned_ref[1] = low
    forward_planes(stresses, depth, rows, out_ref)


def middle_kernel(
    macro_ref, phase_ref, flag_ref, plastic_ref, in_ref, back_depth, back_rows, depth, rows,
    out_ref, elastic_ref,
):
    macro = [macro_ref[c : c + 1, :] for c in range(6)]
    correction = backward_planes(in_ref, back_depth, back_rows)
    stresses = []
    for plane in range(PLANES):
        elastic = []
        for c in range(6):
            at = plane * 192 + c * 32
            before = macro[c] - every_fourth(plastic_ref, c * 128, plane)
            after = before - correction[plane][c * 32 : (c + 1) * 32]
            elastic_ref[at : at + 32, :] = after
            elastic.append(after)
        phases = every_fourth(phase_ref, 0, plane)
        flags = every_fourth(flag_ref, 128, plane)
        stress = material(elastic, phases, flags)[0]
        stresses.append(jnp.concatenate(stress, axis=0))
    forward_planes(stresses, depth, rows, out_ref)


def last_kernel(
    phase_ref, flag_ref, elastic_ref, in_ref, back_depth, back_rows, out_ref
):
    correction = backward_planes(in_ref, back_depth, back_rows)
    sums = [None] * 28

    def collect(at, value):
        part = value.reshape(4, 8, 128)
        part = (part[0] + part[1]) + (part[2] + part[3])
        sums[at] = part if sums[at] is None else sums[at] + part

    for plane in range(PLANES):
        elastic = [
            elastic_ref[plane * 192 + c * 32 : plane * 192 + (c + 1) * 32, :]
            - correction[plane][c * 32 : (c + 1) * 32]
            for c in range(6)
        ]
        phases = every_fourth(phase_ref, 0, plane)
        flags = every_fourth(flag_ref, 256, plane)
        stress, trial, softening, weight = material(elastic, phases, flags)
        for c in range(6):
            collect(c, stress[c])
        collect(6, softening)
        at = 7
        for a in range(6):
            scaled = weight * trial[a]
            for b in range(a, 6):
                collect(at, scaled * trial[b])
                at += 1
    row = lax.broadcasted_iota(jnp.int32, (8, 128), 0)
    groups = [jnp.zeros((8, 128), jnp.float32)] * 16
    totals = [jnp.sum(value, axis=0, keepdims=True) for value in sums]

    def place(at, value):
        here = jnp.broadcast_to(value, (8, 128))
        groups[at // 8] = jnp.where(row == at % 8, here, groups[at // 8])

    for c in range(7):
        place(c, totals[c])
    at = 7
    for a in range(6):
        for b in range(a, 6):
            place(OUTER_AT + 6 * a + b, totals[at])
            if a != b:
                place(OUTER_AT + 6 * b + a, totals[at])
            at += 1
    lines = jnp.concatenate(groups, axis=0)
    ones = jnp.ones((SLABS, 128), jnp.float32)
    line = lax.dot_general(
        ones, lines, (((1,), (1,)), ((), ())),
        precision=lax.Precision.HIGHEST, preferred_element_type=jnp.float32,
    )
    out_ref[...] = line.reshape(SLABS, 1, 128)


def column_kernel(in_ref, columns, back_columns, twist_ref, four, back_four, out_ref):
    pairs = [split(in_ref[:, c * 8 : (c + 1) * 8, :].reshape(128, 128)) for c in range(FIELDS)]
    mixed = from_left_values(columns, pairs)
    cosine, sine = twist_ref[0], twist_ref[1]

    def turn(values, table_ref):
        high, low = split(jnp.concatenate(values, axis=0))
        return mm(high, table_ref[...]) + mm(low, table_ref[...])

    values = []
    for c in range(FIELDS):
        lanes = slice(c * 128, (c + 1) * 128)
        real, imag = mixed[:64, lanes], mixed[64:, lanes]
        turned = (real * cosine + imag * sine, imag * cosine - real * sine)
        values.append(jnp.concatenate(turned, axis=1))
    spectrum = turn(values, four)
    xx, xy, xz, y, z = (spectrum[c * 64 : (c + 1) * 64] for c in range(FIELDS))

    shape = (64, 128)
    row = lax.broadcasted_iota(jnp.int32, shape, 0)
    lane = lax.broadcasted_iota(jnp.int32, shape, 1)
    kx = 16 * lax.shift_right_logical(lane, 5) + lax.shift_right_logical(row, 2)
    ky = 4 * lax.axis_index("slab") + lax.bitwise_and(row, 3)
    kz = lax.bitwise_and(lane, 31)
    half = GRID // 2
    keep = (kx != half) & (ky != half) & (kx + ky + kz > 0)
    xi = [
        jnp.where(kx < half, kx, kx - GRID).astype(jnp.float32),
        jnp.where(ky < half, ky, ky - GRID).astype(jnp.float32),
        kz.astype(jnp.float32),
    ]
    length = xi[0] * xi[0] + xi[1] * xi[1] + xi[2] * xi[2]
    inverse = jnp.where(keep, 1.0 / jnp.maximum(length, 1.0), 0.0)
    coupling = (REFERENCE_LAME + REFERENCE_SHEAR) / (
        REFERENCE_SHEAR * (REFERENCE_LAME + 2.0 * REFERENCE_SHEAR)
    )
    xi = [jnp.concatenate([value, value], axis=1) for value in xi]
    inverse = jnp.concatenate([inverse, inverse], axis=1)
    scaled = inverse * (1.0 / (2.0 * REFERENCE_SHEAR))
    traction = [xi[0] * xx + xi[1] * xy + xi[2] * xz, xi[0] * xy + y, xi[0] * xz + z]
    load = xi[0] * traction[0] + xi[1] * traction[1] + xi[2] * traction[2]
    load = load * (inverse * (REFERENCE_SHEAR * coupling))
    field = [scaled * (traction[i] - xi[i] * load) for i in range(3)]
    values = [
        2.0 * (xi[0] * field[0]),
        xi[0] * field[1] + xi[1] * field[0],
        xi[0] * field[2] + xi[2] * field[0],
        field[1],
        field[2],
    ]
    turned = turn(values, back_four)
    for c in range(FIELDS):
        real, imag = turned[c * 64 : (c + 1) * 64, :128], turned[c * 64 : (c + 1) * 64, 128:]
        first, second = real * cosine - imag * sine, real * sine + imag * cosine
        pairs[c] = split(jnp.concatenate([first, second], axis=0))
    result = from_left_values(back_columns, pairs)
    for c in range(FIELDS):
        out_ref[:, c * 8 : (c + 1) * 8, :] = result[:, c * 128 : (c + 1) * 128].reshape(16, 8, 128)


def totals_kernel(in_ref, all_ref):
    line = jnp.sum(in_ref[...].reshape(SLABS, 128), axis=0, keepdims=True)
    all_ref[...] = jnp.broadcast_to(line[None], all_ref.shape)


def own_outputs(line, stress_ref, tangent_ref):
    stress_ref[...] = line[:, :6]
    at = lax.broadcasted_iota(jnp.int32, (1, 128), 1) - OUTER_AT
    a = at // 6
    b = at - 6 * a
    both = (a < 3) & (b < 3)
    shear = jnp.broadcast_to(line[:, 6:7], (1, 128)) * (2.0 * SHEAR_MODULUS)
    fixed = jnp.where(both, BULK_MODULUS - shear * (1.0 / 3.0), 0.0)
    fixed = fixed + jnp.where(a == b, shear, 0.0)
    whole = (fixed - line * jnp.where(b < 3, 1.0, 2.0)) * (1.0 / TANGENT_UNIT)
    for i in range(6):
        tangent_ref[i] = whole[:, OUTER_AT + 6 * i : OUTER_AT + 6 * i + 6]


def assembly_kernel(
    points, basis_ref, turned_ref, in_ref, stress_ref, tangent_ref, stiffness_ref, forces_ref
):
    start = first_of(points)
    own = lax.rem(lax.axis_index("rve") + points - start, points)
    own_outputs(in_ref[own] * (1.0 / VOXELS), stress_ref, tangent_ref)
    shape = (points, 128)
    sums = in_ref[...].reshape(points, 128) * (1.0 / VOXELS)
    sums = jnp.concatenate([sums[points - start :], sums[: points - start]], axis=0)
    basis = [basis_ref[a * points : (a + 1) * points, :] for a in range(6)]
    mean_shear = 2.0 * SHEAR_MODULUS * sums[:, 6:7]

    def column(at):
        return jnp.broadcast_to(sums[:, at : at + 1], shape)

    mean_shear = jnp.broadcast_to(mean_shear, shape)
    on_diagonal = BULK_MODULUS + mean_shear * (2.0 / 3.0)
    off_diagonal = BULK_MODULUS - mean_shear * (1.0 / 3.0)
    answers = []
    force = jnp.zeros(shape, jnp.float32)
    scale = QUADRATURE_WEIGHT / TANGENT_UNIT
    for a in range(6):
        total = jnp.zeros(shape, jnp.float32)
        for b in range(6):
            low, high = min(a, b), max(a, b)
            entry = -PAIR_WEIGHTS[b] * column(OUTER_AT + 6 * low + high)
            if a == b:
                entry = entry + (on_diagonal if a < 3 else mean_shear)
            elif a < 3 and b < 3:
                entry = entry + off_diagonal
            total = total + entry * basis[b]
        answers.append(total * (PAIR_WEIGHTS[a] * scale))
        force = force + basis[a] * (column(a) * (PAIR_WEIGHTS[a] * QUADRATURE_WEIGHT))
    high, low = split(jnp.concatenate(answers, axis=0))
    left_high, left_low = turned_ref[0], turned_ref[1]
    whole = mm(left_high, high) + (mm(left_low, high) + mm(left_high, low))
    stiffness_ref[...] = whole[:60, :60]
    line = jnp.sum(force, axis=0, keepdims=True)
    part8 = lax.broadcasted_iota(jnp.int32, (8, 128), 0)
    lane8 = lax.broadcasted_iota(jnp.int32, (8, 128), 1)
    spread = jnp.where(lane8 % 3 == part8, jnp.broadcast_to(line, (8, 128)), 0.0)
    pick_row = lax.broadcasted_iota(jnp.int32, (128, 128), 0)
    pick_col = lax.broadcasted_iota(jnp.int32, (128, 128), 1)
    pick = (pick_row // 3 == pick_col).astype(jnp.float32)
    forces = jnp.dot(
        spread, pick, precision=lax.Precision.HIGHEST, preferred_element_type=jnp.float32
    )
    forces_ref[...] = forces[:3, :20]


VMEM = pl.BlockSpec(memory_space=pltpu.VMEM)
HBM = pl.BlockSpec(memory_space=pltpu.HBM)
BF16 = jnp.bfloat16
F32 = jnp.float32
LIMIT = 16 * 1024 * 1024


def params():
    return pltpu.CompilerParams(vmem_limit_bytes=LIMIT)


def cost(flops, size):
    return pl.CostEstimate(flops=flops, bytes_accessed=size, transcendentals=0)


def first_of(points):
    return points // 2 + 1 if points > 1 else 0


def exchange(array):
    return lax.all_to_all(array, "slab", split_axis=0, concat_axis=0, tiled=True)


def on_device(phase_ids, yield_flags, plastic_strain, displacements, connectivity):
    points = lax.axis_size("rve")

    def rows(array):
        lead = math.prod(array.shape[:-2])
        array = array.reshape(lead, PLANES, 32, 128)
        return jnp.transpose(array, (0, 2, 1, 3)).reshape(lead * 128, 128)

    phases = rows(phase_ids)
    flags = rows(yield_flags)
    plastic = rows(plastic_strain)

    there, back = depth_tables()
    depth, back_depth = (
        jnp.asarray(np.stack([right_table(np.roll(t, 32 * l, axis)) for l in range(PLANES)]))
        for t, axis in ((there, 1), (back, 0))
    )
    there, back = row_tables()
    line, back_line = jnp.asarray(left_table(there)), jnp.asarray(left_table(back))
    there, back, twist, four, back_four = column_tables()
    column, back_column = jnp.asarray(left_table(there)), jnp.asarray(left_table(back))
    twist = jnp.asarray(twist)
    four = jnp.asarray(four.astype(ml_dtypes.bfloat16))
    back_four = jnp.asarray(back_four.astype(ml_dtypes.bfloat16))

    block = jax.ShapeDtypeStruct((16, 8 * FIELDS, 128), F32)

    first = pl.pallas_call(
        functools.partial(first_kernel, points),
        out_shape=(
            block, jax.ShapeDtypeStruct((8, 128), F32),
            jax.ShapeDtypeStruct((6 * points, 128), F32),
            jax.ShapeDtypeStruct((2, 128, 6 * points), BF16),
        ),
        in_specs=[HBM] * 7, out_specs=(VMEM,) * 4,
        scratch_shapes=[
            pltpu.SMEM(connectivity.shape, jnp.int32), pltpu.SMEM(displacements.shape[::-1], F32),
            pltpu.VMEM((128, 128), jnp.int32), pltpu.VMEM((128, 128), jnp.int32),
            pltpu.VMEM((768, 128), F32), pltpu.VMEM((PLANES, 256, 256), BF16),
            pltpu.VMEM((256, 256), BF16),
            pltpu.SemaphoreType.DMA((7,)),
        ],
        compiler_params=params(), cost_estimate=cost(400_000_000, 2_000_000), name="first",
    )
    columns = pl.pallas_call(
        column_kernel, out_shape=block,
        in_specs=[VMEM] * 6, out_specs=VMEM,
        compiler_params=params(), cost_estimate=cost(400_000_000, 2_000_000), name="columns",
    )
    middle = pl.pallas_call(
        middle_kernel, out_shape=(block, jax.ShapeDtypeStruct((768, 128), F32)),
        in_specs=[VMEM] * 9, out_specs=(VMEM, VMEM),
        compiler_params=params(),
        cost_estimate=cost(800_000_000, 4_000_000), name="middle",
    )
    last = pl.pallas_call(
        last_kernel, out_shape=jax.ShapeDtypeStruct((SLABS, 1, 128), F32),
        in_specs=[VMEM] * 6, out_specs=VMEM,
        compiler_params=params(),
        cost_estimate=cost(400_000_000, 2_000_000), name="last",
    )
    totals = pl.pallas_call(
        totals_kernel, out_shape=jax.ShapeDtypeStruct((points, 1, 128), F32),
        in_specs=[VMEM], out_specs=VMEM, compiler_params=params(),
        cost_estimate=cost(10_000, 50_000), name="totals",
    )
    assembly = pl.pallas_call(
        functools.partial(assembly_kernel, points),
        out_shape=(
            jax.ShapeDtypeStruct((1, 6), F32), jax.ShapeDtypeStruct((6, 1, 6), F32),
            jax.ShapeDtypeStruct((60, 60), F32), jax.ShapeDtypeStruct((3, 20), F32),
        ),
        in_specs=[VMEM] * 3, out_specs=(VMEM,) * 4, compiler_params=params(),
        cost_estimate=cost(10_000_000, 200_000), name="assembly",
    )

    def apply_columns(array):
        return exchange(
            columns(exchange(array), column, back_column, twist, four, back_four)
        )

    operands = (connectivity, displacements.T, phases, flags, plastic, depth, line)
    spectrum, macro, basis, turned_basis = first(
        *(pltpu.with_memory_space_constraint(operand, pltpu.HBM) for operand in operands)
    )
    planes = apply_columns(spectrum)
    spectrum, elastic = middle(
        macro, phases, flags, plastic, planes, back_depth, back_line, depth, line
    )
    planes = apply_columns(spectrum)
    partial = last(phases, flags, elastic, planes, back_depth, back_line)
    everyone = totals(exchange(partial))
    turned = [(g + first_of(points)) % points for g in range(points)]
    everyone = lax.all_to_all(
        everyone, "rve", 0, 0, tiled=True, axis_index_groups=[turned]
    )
    stress, tangent, stiffness, forces = assembly(basis, turned_basis, everyone)
    return (stress, jnp.transpose(tangent, (1, 0, 2)), forces.T, stiffness)


def solution(mesh):
    return jax.shard_map(
        on_device,
        mesh=mesh,
        in_specs=(
            P("slab", None),
            P("rve", None, "slab", None),
            P("rve", None, "slab", None),
            P(),
            P(),
        ),
        out_specs=(P("rve", None), P("rve", None, None), P(), P()),
        check_vma=False,
    )
```

```python
import functools
import math

import jax
import jax.numpy as jnp
import ml_dtypes
import numpy as np
from jax import lax
from jax.experimental import pallas as pl
from jax.experimental.pallas import tpu as pltpu
from jax.sharding import PartitionSpec as P

GRID = 64
ITERS = 2
SLABS = 16
PLANES = GRID // SLABS
KEPT = GRID // 2

SHEAR_MODULUS = 80.0
BULK_MODULUS = 160.0
REFERENCE_SHEAR = 80.0
REFERENCE_LAME = 160.0 - 160.0 / 3.0
TANGENT_UNIT = 100.0
QUADRATURE_WEIGHT = 0.125
PAIR_WEIGHTS = (1.0, 1.0, 1.0, 2.0, 2.0, 2.0)
TENSOR_PAIRS = ((0, 0), (1, 1), (2, 2), (1, 2), (0, 2), (0, 1))
VOXELS = float(GRID**3)
GAUSS_LOW = 0.5 - 0.5 / math.sqrt(3.0)
GAUSS_HIGH = 0.5 + 0.5 / math.sqrt(3.0)
OUTER_AT = 8
FIELDS = 5
FAR = 10


def halves(table):
    high = table.astype(np.float32).astype(ml_dtypes.bfloat16)
    low = (table - high.astype(np.float64)).astype(np.float32).astype(ml_dtypes.bfloat16)
    return high, low


def depth_tables():
    z = np.arange(GRID)
    k = np.arange(KEPT)
    theta = 2.0 * np.pi * np.outer(z, k) / GRID
    forward = np.stack([np.cos(theta), -np.sin(theta)], axis=0)
    weight = np.where(k == 0, 1.0, 2.0) / VOXELS
    inverse = forward * weight[None, None, :]
    pair = np.eye(2)
    there = np.einsum("rR,pzk->rzRpk", pair, forward)
    back = np.einsum("rR,pzk->Rpkrz", pair, inverse)
    return there.reshape(128, 128), back.reshape(128, 128)


def row_tables():
    y = 2 * np.arange(32)[None, :] + np.arange(2)[:, None]
    ky = 4 * np.arange(16)[:, None] + np.arange(4)[None, :]
    theta = 2.0 * np.pi * np.einsum("de,rm->derm", ky, y) / GRID
    c, s = np.cos(theta), np.sin(theta)
    there = np.zeros((16, 2, 4, 2, 2, 32))
    there[:, 0, :, :, 0, :] = c
    there[:, 0, :, :, 1, :] = s
    there[:, 1, :, :, 0, :] = -s
    there[:, 1, :, :, 1, :] = c
    back = np.zeros((2, 2, 32, 16, 2, 4))
    ct, st = np.einsum("derm->rmde", c), np.einsum("derm->rmde", s)
    back[:, 0, :, :, 0, :] = ct
    back[:, 0, :, :, 1, :] = -st
    back[:, 1, :, :, 0, :] = st
    back[:, 1, :, :, 1, :] = ct
    return there.reshape(128, 128), back.reshape(128, 128)


def column_tables():
    d = np.arange(16)
    theta = 2.0 * np.pi * np.outer(d, d) / 16.0
    c, s = np.cos(theta), np.sin(theta)
    same = np.eye(4)
    there = np.zeros((2, 16, 4, 16, 2, 4))
    there[0, :, :, :, 0, :] = np.einsum("bd,ef->bedf", c, same)
    there[0, :, :, :, 1, :] = np.einsum("bd,ef->bedf", s, same)
    there[1, :, :, :, 0, :] = np.einsum("bd,ef->bedf", -s, same)
    there[1, :, :, :, 1, :] = np.einsum("bd,ef->bedf", c, same)
    there = there.reshape(128, 128)
    phi = 2.0 * np.pi * np.outer(np.arange(16), np.arange(4)) / GRID
    twist = np.stack([np.cos(phi), np.sin(phi)])[:, :, None, :, None]
    twist = np.broadcast_to(twist, (2, 16, 4, 4, KEPT)).reshape(2, 64, 128)
    quarter = 2.0 * np.pi * np.outer(np.arange(4), np.arange(4)) / 4.0
    cq, sq = np.rint(np.cos(quarter)), np.rint(np.sin(quarter))
    kept = np.eye(KEPT)
    four = np.zeros((2, 4, KEPT, 2, 4, KEPT))
    four[0, :, :, 0] = np.einsum("la,kK->lkaK", cq, kept)
    four[1, :, :, 0] = np.einsum("la,kK->lkaK", sq, kept)
    four[0, :, :, 1] = np.einsum("la,kK->lkaK", -sq, kept)
    four[1, :, :, 1] = np.einsum("la,kK->lkaK", cq, kept)
    four = four.reshape(256, 256)
    return there, there.T.copy(), twist.astype(np.float32), four, four.T.copy()


def right_table(table):
    high, low = halves(table)
    return np.block([[high, low], [high, np.zeros_like(low)]])


def left_table(table):
    return np.ascontiguousarray(right_table(table.T).T)


def split(x):
    high = x.astype(jnp.bfloat16)
    low = (x - high.astype(jnp.float32)).astype(jnp.bfloat16)
    return high, low


def mm(a, b):
    return jnp.dot(a, b, preferred_element_type=jnp.float32)


def from_left_values(table_ref, pairs):
    both = jnp.concatenate([jnp.concatenate(pair, axis=0) for pair in pairs], axis=1)
    total = mm(table_ref[:128, :], both)
    return total + mm(table_ref[128:, :128], both[:128])


def from_left_halves(table_ref, pairs):
    both = jnp.concatenate([jnp.concatenate(pair, axis=0) for pair in pairs], axis=1)
    both = mm(table_ref[...], both)
    return both[:128] + both[128:]


def from_right(tiles, table_ref):
    results = []
    for l, tile in enumerate(tiles):
        both = mm(jnp.concatenate(split(tile), axis=1), table_ref[l])
        results.append(both[:, :128] + both[:, 128:])
    return results


def gather_chunks(tiles):
    lane = lax.broadcasted_iota(jnp.int32, tiles[0].shape, 1)
    odd = lax.bitwise_and(lane, 32) != 0
    upper = lax.bitwise_and(lane, 64) != 0
    tiles = [jnp.where(odd, tiles[(j + 1) % 4], tiles[j]) for j in range(4)]
    tiles = [jnp.where(upper, tiles[(j + 2) % 4], tiles[j]) for j in range(4)]
    return [tiles[-k % 4] for k in range(4)]


def roll_chunks(tile, count):
    return pltpu.roll(tile, 32 * (count % 4), 1) if count % 4 else tile


def slopes_of(bits, low, high):
    at = [jnp.where(bit == 1, high, low) for bit in bits]
    far = [jnp.where(bit == 1, low, high) for bit in bits]

    def slope(corner, axis):
        value = None
        for other in range(3):
            if other != axis:
                factor = at[other] if corner >> other & 1 else far[other]
                value = factor if value is None else value * factor
        return value if corner >> axis & 1 else -value

    return slope


def point_slopes(point):
    low, high = jnp.float32(GAUSS_LOW), jnp.float32(GAUSS_HIGH)
    bits = [lax.bitwise_and(lax.shift_right_logical(point, d), 1) for d in range(3)]
    slope = slopes_of(bits, low, high)
    return [[slope(corner, d) for d in range(3)] for corner in range(8)]


def macro_strain(point, slopes, conn_ref, disp_ref):
    element = lax.shift_right_logical(point, 3)
    grad = [[jnp.float32(0.0)] * 3 for _ in range(3)]
    for corner in range(8):
        node = conn_ref[element, corner]
        for k in range(3):
            u = disp_ref[k, node]
            for d in range(3):
                grad[k][d] = grad[k][d] + slopes[corner][d] * u
    strain = []
    for i, j in TENSOR_PAIRS:
        strain.append(grad[i][i] if i == j else 0.5 * (grad[i][j] + grad[j][i]))
    return strain


def material(elastic, phases, flags):
    hard = phases == 1
    limit = jnp.where(hard, 1.2, 0.3)
    ratio = jnp.where(
        hard,
        3.0 * SHEAR_MODULUS / (3.0 * SHEAR_MODULUS + 10.0),
        3.0 * SHEAR_MODULUS / (3.0 * SHEAR_MODULUS + 2.0),
    )
    active = flags.astype(jnp.float32)
    volume = elastic[0] + elastic[1] + elastic[2]
    third = volume * (1.0 / 3.0)
    trial = [2.0 * SHEAR_MODULUS * (elastic[a] - third) for a in range(3)]
    trial += [2.0 * SHEAR_MODULUS * elastic[a] for a in range(3, 6)]
    normal = trial[0] * trial[0] + trial[1] * trial[1] + trial[2] * trial[2]
    shear = trial[3] * trial[3] + trial[4] * trial[4] + trial[5] * trial[5]
    equivalent = jnp.sqrt(1.5 * (normal + 2.0 * shear))
    bounded = jnp.maximum(equivalent, limit)
    inverse = 1.0 / bounded
    scaled = ratio * active
    softening = 1.0 - scaled * (equivalent - limit) * inverse
    pressure = BULK_MODULUS * volume
    stress = [trial[a] * softening + pressure for a in range(3)]
    stress += [trial[a] * softening for a in range(3, 6)]
    weight = 3.0 * SHEAR_MODULUS * scaled * limit * (inverse * inverse * inverse)
    return stress, trial, softening, weight


def every_fourth(ref, start, plane):
    return ref[pl.ds(start + plane, 32, stride=4), :]


def plane_waves():
    row = lax.broadcasted_iota(jnp.int32, (8, 128), 0)
    lane = lax.broadcasted_iota(jnp.int32, (8, 128), 1)
    inner = lax.bitwise_and(row, 3).astype(jnp.float32)
    depth = lax.bitwise_and(lane, 31).astype(jnp.float32)
    starts = [4.0 * d if d < 8 else 4.0 * d - GRID for d in range(16)]
    wave_y = jnp.concatenate([inner + start for start in starts], axis=0)
    return wave_y, jnp.concatenate([depth] * 16, axis=0)


def forward_planes(stresses, depth, rows, out_ref):
    tiles = gather_chunks(from_right(stresses, depth))
    tiles = [roll_chunks(tile, -s) for s, tile in enumerate(tiles)]
    pairs = [
        split(jnp.concatenate([tile[c * 32 : (c + 1) * 32] for tile in tiles], axis=0))
        for c in range(6)
    ]
    spectrum = from_left_halves(rows, pairs)
    xx, yy, zz, yz, xz, xy = (spectrum[:, c * 128 : (c + 1) * 128] for c in range(6))
    wave_y, wave_z = plane_waves()
    fields = (xx, xy, xz, wave_y * yy + wave_z * yz, wave_y * yz + wave_z * zz)
    for c, field in enumerate(fields):
        out_ref[:, c * 8 : (c + 1) * 8, :] = field.reshape(16, 8, 128)


def backward_planes(in_ref, depth, rows):
    xx, xy, xz, y, z = (
        in_ref[:, c * 8 : (c + 1) * 8, :].reshape(128, 128) for c in range(FIELDS)
    )
    wave_y, wave_z = plane_waves()
    yy, zz = 2.0 * (wave_y * y), 2.0 * (wave_z * z)
    pairs = [split(value) for value in (xx, yy, zz, wave_y * z + wave_z * y, xz, xy)]
    lines = from_left_values(rows, pairs)
    tiles = [
        jnp.concatenate(
            [lines[s * 32 : (s + 1) * 32, c * 128 : (c + 1) * 128] for c in range(6)], axis=0
        )
        for s in range(4)
    ]
    tiles = [roll_chunks(tile, s) for s, tile in enumerate(tiles)]
    return from_right(gather_chunks(tiles), depth)


def basis_of(points, conn_ref):
    shape = (points, 128)
    lane = lax.broadcasted_iota(jnp.int32, shape, 1)
    point = lax.broadcasted_iota(jnp.int32, shape, 0)
    element = lax.shift_right_logical(point, 3)
    bits = [lax.bitwise_and(lax.shift_right_logical(point, d), 1) for d in range(3)]
    slope = slopes_of(bits, GAUSS_LOW, GAUSS_HIGH)
    node = lane // 3
    part = lane - 3 * node
    elements = conn_ref.shape[0]
    grad = [jnp.zeros(shape, jnp.float32) for _ in range(3)]
    for corner in range(8):
        owner = jnp.full(shape, conn_ref[0, corner], jnp.int32)
        for e in range(1, elements):
            owner = jnp.where(element == e, conn_ref[e, corner], owner)
        here = (owner == node) & (lane < 60)
        for d in range(3):
            grad[d] = grad[d] + jnp.where(here, slope(corner, d), 0.0)
    basis = []
    for i, k in TENSOR_PAIRS:
        if i == k:
            basis.append(jnp.where(part == i, grad[i], 0.0))
        else:
            value = jnp.where(part == i, 0.5 * grad[k], 0.0)
            basis.append(value + jnp.where(part == k, 0.5 * grad[i], 0.0))
    return jnp.concatenate(basis, axis=0)


def first_kernel(
    points, conn_hbm, disp_hbm, phase_hbm, flag_hbm, plastic_hbm, depth_hbm, rows_hbm,
    out_ref, macro_ref, basis_ref, turned_ref,
    conn_ref, disp_ref, phase_ref, flag_ref, plastic_ref, depth, rows, sems,
):
    pairs = (
        (conn_hbm, conn_ref), (disp_hbm, disp_ref), (plastic_hbm, plastic_ref),
        (phase_hbm, phase_ref), (flag_hbm.at[pl.ds(0, 128)], flag_ref),
        (depth_hbm, depth), (rows_hbm, rows),
    )
    copies = [pltpu.make_async_copy(a, b, sems.at[i]) for i, (a, b) in enumerate(pairs)]
    for copy in copies:
        copy.start()
    point = lax.axis_index("rve")
    slopes = point_slopes(point)
    for copy in copies[:2]:
        copy.wait()
    macro = macro_strain(point, slopes, conn_ref, disp_ref)
    row = lax.broadcasted_iota(jnp.int32, (8, 128), 0)
    table = jnp.zeros((8, 128), jnp.float32)
    for c in range(6):
        table = jnp.where(row == c, macro[c], table)
    macro_ref[...] = table
    for copy in copies[2:5]:
        copy.wait()
    stresses = []
    for plane in range(PLANES):
        elastic = [macro[c] - every_fourth(plastic_ref, c * 128, plane) for c in range(6)]
        phases = every_fourth(phase_ref, 0, plane)
        flags = every_fourth(flag_ref, 0, plane)
        stress = material(elastic, phases, flags)[0]
        stresses.append(jnp.concatenate(stress, axis=0))
    for copy in copies[5:]:
        copy.wait()
    basis = basis_of(points, conn_ref)
    basis_ref[...] = basis
    high, low = split(jnp.transpose(basis))
    turned_ref[0] = high
    turned_ref[1] = low
    forward_planes(stresses, depth, rows, out_ref)


def middle_kernel(
    macro_ref, phase_ref, flag_ref, plastic_ref, in_ref, back_depth, back_rows, depth, rows,
    out_ref, elastic_ref,
):
    macro = [macro_ref[c : c + 1, :] for c in range(6)]
    correction = backward_planes(in_ref, back_depth, back_rows)
    stresses = []
    for plane in range(PLANES):
        elastic = []
        for c in range(6):
            at = plane * 192 + c * 32
            before = macro[c] - every_fourth(plastic_ref, c * 128, plane)
            after = before - correction[plane][c * 32 : (c + 1) * 32]
            elastic_ref[at : at + 32, :] = after
            elastic.append(after)
        phases = every_fourth(phase_ref, 0, plane)
        flags = every_fourth(flag_ref, 128, plane)
        stress = material(elastic, phases, flags)[0]
        stresses.append(jnp.concatenate(stress, axis=0))
    forward_planes(stresses, depth, rows, out_ref)


def last_kernel(
    phase_ref, flag_ref, elastic_ref, in_ref, back_depth, back_rows, out_ref
):
    correction = backward_planes(in_ref, back_depth, back_rows)
    sums = [None] * 28

    def collect(at, value):
        part = value.reshape(4, 8, 128)
        part = (part[0] + part[1]) + (part[2] + part[3])
        sums[at] = part if sums[at] is None else sums[at] + part

    for plane in range(PLANES):
        elastic = [
            elastic_ref[plane * 192 + c * 32 : plane * 192 + (c + 1) * 32, :]
            - correction[plane][c * 32 : (c + 1) * 32]
            for c in range(6)
        ]
        phases = every_fourth(phase_ref, 0, plane)
        flags = every_fourth(flag_ref, 256, plane)
        stress, trial, softening, weight = material(elastic, phases, flags)
        for c in range(6):
            collect(c, stress[c])
        collect(6, softening)
        at = 7
        for a in range(6):
            scaled = weight * trial[a]
            for b in range(a, 6):
                collect(at, scaled * trial[b])
                at += 1
    row = lax.broadcasted_iota(jnp.int32, (8, 128), 0)
    groups = [jnp.zeros((8, 128), jnp.float32)] * 16
    totals = [jnp.sum(value, axis=0, keepdims=True) for value in sums]

    def place(at, value):
        here = jnp.broadcast_to(value, (8, 128))
        groups[at // 8] = jnp.where(row == at % 8, here, groups[at // 8])

    for c in range(7):
        place(c, totals[c])
    at = 7
    for a in range(6):
        for b in range(a, 6):
            place(OUTER_AT + 6 * a + b, totals[at])
            if a != b:
                place(OUTER_AT + 6 * b + a, totals[at])
            at += 1
    lines = jnp.concatenate(groups, axis=0)
    ones = jnp.ones((SLABS, 128), jnp.float32)
    line = lax.dot_general(
        ones, lines, (((1,), (1,)), ((), ())),
        precision=lax.Precision.HIGHEST, preferred_element_type=jnp.float32,
    )
    out_ref[...] = line.reshape(SLABS, 1, 128)


def column_kernel(in_ref, columns, back_columns, twist_ref, four, back_four, out_ref):
    pairs = [split(in_ref[:, c * 8 : (c + 1) * 8, :].reshape(128, 128)) for c in range(FIELDS)]
    mixed = from_left_values(columns, pairs)
    cosine, sine = twist_ref[0], twist_ref[1]

    def turn(values, table_ref):
        high, low = split(jnp.concatenate(values, axis=0))
        return mm(high, table_ref[...]) + mm(low, table_ref[...])

    values = []
    for c in range(FIELDS):
        lanes = slice(c * 128, (c + 1) * 128)
        real, imag = mixed[:64, lanes], mixed[64:, lanes]
        turned = (real * cosine + imag * sine, imag * cosine - real * sine)
        values.append(jnp.concatenate(turned, axis=1))
    spectrum = turn(values, four)
    xx, xy, xz, y, z = (spectrum[c * 64 : (c + 1) * 64] for c in range(FIELDS))

    shape = (64, 128)
    row = lax.broadcasted_iota(jnp.int32, shape, 0)
    lane = lax.broadcasted_iota(jnp.int32, shape, 1)
    kx = 16 * lax.shift_right_logical(lane, 5) + lax.shift_right_logical(row, 2)
    ky = 4 * lax.axis_index("slab") + lax.bitwise_and(row, 3)
    kz = lax.bitwise_and(lane, 31)
    half = GRID // 2
    keep = (kx != half) & (ky != half) & (kx + ky + kz > 0)
    xi = [
        jnp.where(kx < half, kx, kx - GRID).astype(jnp.float32),
        jnp.where(ky < half, ky, ky - GRID).astype(jnp.float32),
        kz.astype(jnp.float32),
    ]
    length = xi[0] * xi[0] + xi[1] * xi[1] + xi[2] * xi[2]
    inverse = jnp.where(keep, 1.0 / jnp.maximum(length, 1.0), 0.0)
    coupling = (REFERENCE_LAME + REFERENCE_SHEAR) / (
        REFERENCE_SHEAR * (REFERENCE_LAME + 2.0 * REFERENCE_SHEAR)
    )
    xi = [jnp.concatenate([value, value], axis=1) for value in xi]
    inverse = jnp.concatenate([inverse, inverse], axis=1)
    scaled = inverse * (1.0 / (2.0 * REFERENCE_SHEAR))
    traction = [xi[0] * xx + xi[1] * xy + xi[2] * xz, xi[0] * xy + y, xi[0] * xz + z]
    load = xi[0] * traction[0] + xi[1] * traction[1] + xi[2] * traction[2]
    load = load * (inverse * (REFERENCE_SHEAR * coupling))
    field = [scaled * (traction[i] - xi[i] * load) for i in range(3)]
    values = [
        2.0 * (xi[0] * field[0]),
        xi[0] * field[1] + xi[1] * field[0],
        xi[0] * field[2] + xi[2] * field[0],
        field[1],
        field[2],
    ]
    turned = turn(values, back_four)
    for c in range(FIELDS):
        real, imag = turned[c * 64 : (c + 1) * 64, :128], turned[c * 64 : (c + 1) * 64, 128:]
        first, second = real * cosine - imag * sine, real * sine + imag * cosine
        pairs[c] = split(jnp.concatenate([first, second], axis=0))
    result = from_left_values(back_columns, pairs)
    for c in range(FIELDS):
        out_ref[:, c * 8 : (c + 1) * 8, :] = result[:, c * 128 : (c + 1) * 128].reshape(16, 8, 128)


def totals_kernel(in_ref, all_ref):
    line = jnp.sum(in_ref[...].reshape(SLABS, 128), axis=0, keepdims=True)
    all_ref[...] = jnp.broadcast_to(line[None], all_ref.shape)


def own_outputs(line, stress_ref, tangent_ref):
    stress_ref[...] = line[:, :6]
    at = lax.broadcasted_iota(jnp.int32, (1, 128), 1) - OUTER_AT
    a = at // 6
    b = at - 6 * a
    both = (a < 3) & (b < 3)
    shear = jnp.broadcast_to(line[:, 6:7], (1, 128)) * (2.0 * SHEAR_MODULUS)
    fixed = jnp.where(both, BULK_MODULUS - shear * (1.0 / 3.0), 0.0)
    fixed = fixed + jnp.where(a == b, shear, 0.0)
    whole = (fixed - line * jnp.where(b < 3, 1.0, 2.0)) * (1.0 / TANGENT_UNIT)
    for i in range(6):
        tangent_ref[i] = whole[:, OUTER_AT + 6 * i : OUTER_AT + 6 * i + 6]


def assembly_kernel(
    points, basis_ref, turned_ref, in_ref, stress_ref, tangent_ref, stiffness_ref, forces_ref
):
    start = first_of(points)
    own = lax.rem(lax.axis_index("rve") + points - start, points)
    own_outputs(in_ref[own] * (1.0 / VOXELS), stress_ref, tangent_ref)
    shape = (points, 128)
    sums = in_ref[...].reshape(points, 128) * (1.0 / VOXELS)
    sums = jnp.concatenate([sums[points - start :], sums[: points - start]], axis=0)
    basis = [basis_ref[a * points : (a + 1) * points, :] for a in range(6)]
    mean_shear = 2.0 * SHEAR_MODULUS * sums[:, 6:7]

    def column(at):
        return jnp.broadcast_to(sums[:, at : at + 1], shape)

    mean_shear = jnp.broadcast_to(mean_shear, shape)
    on_diagonal = BULK_MODULUS + mean_shear * (2.0 / 3.0)
    off_diagonal = BULK_MODULUS - mean_shear * (1.0 / 3.0)
    answers = []
    force = jnp.zeros(shape, jnp.float32)
    scale = QUADRATURE_WEIGHT / TANGENT_UNIT
    for a in range(6):
        total = jnp.zeros(shape, jnp.float32)
        for b in range(6):
            low, high = min(a, b), max(a, b)
            entry = -PAIR_WEIGHTS[b] * column(OUTER_AT + 6 * low + high)
            if a == b:
                entry = entry + (on_diagonal if a < 3 else mean_shear)
            elif a < 3 and b < 3:
                entry = entry + off_diagonal
            total = total + entry * basis[b]
        answers.append(total * (PAIR_WEIGHTS[a] * scale))
        force = force + basis[a] * (column(a) * (PAIR_WEIGHTS[a] * QUADRATURE_WEIGHT))
    high, low = split(jnp.concatenate(answers, axis=0))
    left_high, left_low = turned_ref[0], turned_ref[1]
    whole = mm(left_high, high) + (mm(left_low, high) + mm(left_high, low))
    stiffness_ref[...] = whole[:60, :60]
    line = jnp.sum(force, axis=0, keepdims=True)
    part8 = lax.broadcasted_iota(jnp.int32, (8, 128), 0)
    lane8 = lax.broadcasted_iota(jnp.int32, (8, 128), 1)
    spread = jnp.where(lane8 % 3 == part8, jnp.broadcast_to(line, (8, 128)), 0.0)
    pick_row = lax.broadcasted_iota(jnp.int32, (128, 128), 0)
    pick_col = lax.broadcasted_iota(jnp.int32, (128, 128), 1)
    pick = (pick_row // 3 == pick_col).astype(jnp.float32)
    forces = jnp.dot(
        spread, pick, precision=lax.Precision.HIGHEST, preferred_element_type=jnp.float32
    )
    forces_ref[...] = forces[:3, :20]


VMEM = pl.BlockSpec(memory_space=pltpu.VMEM)
HBM = pl.BlockSpec(memory_space=pltpu.HBM)
BF16 = jnp.bfloat16
F32 = jnp.float32
LIMIT = 16 * 1024 * 1024


def params():
    return pltpu.CompilerParams(vmem_limit_bytes=LIMIT)


def cost(flops, size):
    return pl.CostEstimate(flops=flops, bytes_accessed=size, transcendentals=0)


def first_of(points):
    return points // 2 + 1 if points > 1 else 0


def exchange(array, turn=0):
    groups = [[(d + turn) % SLABS for d in range(SLABS)]] if turn else None
    return lax.all_to_all(
        array, "slab", split_axis=0, concat_axis=0, tiled=True, axis_index_groups=groups
    )


def on_device(phase_ids, yield_flags, plastic_strain, displacements, connectivity):
    points = lax.axis_size("rve")

    def rows(array):
        lead = math.prod(array.shape[:-2])
        array = array.reshape(lead, PLANES, 32, 128)
        return jnp.transpose(array, (0, 2, 1, 3)).reshape(lead * 128, 128)

    phases = rows(phase_ids)
    flags = rows(yield_flags)
    plastic = rows(plastic_strain)

    there, back = depth_tables()
    depth, back_depth = (
        jnp.asarray(np.stack([right_table(np.roll(t, 32 * l, axis)) for l in range(PLANES)]))
        for t, axis in ((there, 1), (back, 0))
    )
    there, back = row_tables()
    line, back_line = jnp.asarray(left_table(there)), jnp.asarray(left_table(back))
    there, back, twist, four, back_four = column_tables()
    column, back_column = jnp.asarray(left_table(there)), jnp.asarray(left_table(back))
    twist = jnp.asarray(twist)
    four = jnp.asarray(four.astype(ml_dtypes.bfloat16))
    back_four = jnp.asarray(back_four.astype(ml_dtypes.bfloat16))

    block = jax.ShapeDtypeStruct((16, 8 * FIELDS, 128), F32)

    first = pl.pallas_call(
        functools.partial(first_kernel, points),
        out_shape=(
            block, jax.ShapeDtypeStruct((8, 128), F32),
            jax.ShapeDtypeStruct((6 * points, 128), F32),
            jax.ShapeDtypeStruct((2, 128, 6 * points), BF16),
        ),
        in_specs=[HBM] * 7, out_specs=(VMEM,) * 4,
        scratch_shapes=[
            pltpu.SMEM(connectivity.shape, jnp.int32), pltpu.SMEM(displacements.shape[::-1], F32),
            pltpu.VMEM((128, 128), jnp.int32), pltpu.VMEM((128, 128), jnp.int32),
            pltpu.VMEM((768, 128), F32), pltpu.VMEM((PLANES, 256, 256), BF16),
            pltpu.VMEM((256, 256), BF16),
            pltpu.SemaphoreType.DMA((7,)),
        ],
        compiler_params=params(), cost_estimate=cost(400_000_000, 2_000_000), name="first",
    )
    columns = pl.pallas_call(
        column_kernel, out_shape=block,
        in_specs=[VMEM] * 6, out_specs=VMEM,
        compiler_params=params(), cost_estimate=cost(400_000_000, 2_000_000), name="columns",
    )
    middle = pl.pallas_call(
        middle_kernel, out_shape=(block, jax.ShapeDtypeStruct((768, 128), F32)),
        in_specs=[VMEM] * 9, out_specs=(VMEM, VMEM),
        compiler_params=params(),
        cost_estimate=cost(800_000_000, 4_000_000), name="middle",
    )
    last = pl.pallas_call(
        last_kernel, out_shape=jax.ShapeDtypeStruct((SLABS, 1, 128), F32),
        in_specs=[VMEM] * 6, out_specs=VMEM,
        compiler_params=params(),
        cost_estimate=cost(400_000_000, 2_000_000), name="last",
    )
    totals = pl.pallas_call(
        totals_kernel, out_shape=jax.ShapeDtypeStruct((points, 1, 128), F32),
        in_specs=[VMEM], out_specs=VMEM, compiler_params=params(),
        cost_estimate=cost(10_000, 50_000), name="totals",
    )
    assembly = pl.pallas_call(
        functools.partial(assembly_kernel, points),
        out_shape=(
            jax.ShapeDtypeStruct((1, 6), F32), jax.ShapeDtypeStruct((6, 1, 6), F32),
            jax.ShapeDtypeStruct((60, 60), F32), jax.ShapeDtypeStruct((3, 20), F32),
        ),
        in_specs=[VMEM] * 3, out_specs=(VMEM,) * 4, compiler_params=params(),
        cost_estimate=cost(10_000_000, 200_000), name="assembly",
    )

    def apply_columns(array):
        return exchange(
            columns(exchange(array), column, back_column, twist, four, back_four)
        )

    operands = (connectivity, displacements.T, phases, flags, plastic, depth, line)
    spectrum, macro, basis, turned_basis = first(
        *(pltpu.with_memory_space_constraint(operand, pltpu.HBM) for operand in operands)
    )
    planes = apply_columns(spectrum)
    spectrum, elastic = middle(
        macro, phases, flags, plastic, planes, back_depth, back_line, depth, line
    )
    planes = apply_columns(spectrum)
    partial = last(phases, flags, elastic, planes, back_depth, back_line)
    everyone = totals(exchange(partial, FAR))
    turned = [(g + first_of(points)) % points for g in range(points)]
    everyone = lax.all_to_all(
        everyone, "rve", 0, 0, tiled=True, axis_index_groups=[turned]
    )
    stress, tangent, stiffness, forces = assembly(basis, turned_basis, everyone)
    return (stress, jnp.transpose(tangent, (1, 0, 2)), forces.T, stiffness)


def solution(mesh):
    return jax.shard_map(
        on_device,
        mesh=mesh,
        in_specs=(
            P("slab", None),
            P("rve", None, "slab", None),
            P("rve", None, "slab", None),
            P(),
            P(),
        ),
        out_specs=(P("rve", None), P("rve", None, None), P(), P()),
        check_vma=False,
    )
```

```python
import functools
import math

import jax
import jax.numpy as jnp
import ml_dtypes
import numpy as np
from jax import lax
from jax.experimental import pallas as pl
from jax.experimental.pallas import tpu as pltpu
from jax.sharding import PartitionSpec as P

GRID = 64
ITERS = 2
SLABS = 16
PLANES = GRID // SLABS
KEPT = GRID // 2

SHEAR_MODULUS = 80.0
BULK_MODULUS = 160.0
REFERENCE_SHEAR = 80.0
REFERENCE_LAME = 160.0 - 160.0 / 3.0
TANGENT_UNIT = 100.0
QUADRATURE_WEIGHT = 0.125
PAIR_WEIGHTS = (1.0, 1.0, 1.0, 2.0, 2.0, 2.0)
TENSOR_PAIRS = ((0, 0), (1, 1), (2, 2), (1, 2), (0, 2), (0, 1))
VOXELS = float(GRID**3)
GAUSS_LOW = 0.5 - 0.5 / math.sqrt(3.0)
GAUSS_HIGH = 0.5 + 0.5 / math.sqrt(3.0)
OUTER_AT = 8
FIELDS = 5
FAR = 10


def halves(table):
    high = table.astype(np.float32).astype(ml_dtypes.bfloat16)
    low = (table - high.astype(np.float64)).astype(np.float32).astype(ml_dtypes.bfloat16)
    return high, low


def depth_tables():
    z = np.arange(GRID)
    k = np.arange(KEPT)
    theta = 2.0 * np.pi * np.outer(z, k) / GRID
    forward = np.stack([np.cos(theta), -np.sin(theta)], axis=0)
    weight = np.where(k == 0, 1.0, 2.0) / VOXELS
    inverse = forward * weight[None, None, :]
    pair = np.eye(2)
    there = np.einsum("rR,pzk->rzRpk", pair, forward)
    back = np.einsum("rR,pzk->Rpkrz", pair, inverse)
    return there.reshape(128, 128), back.reshape(128, 128)


def row_tables():
    y = 2 * np.arange(32)[None, :] + np.arange(2)[:, None]
    ky = 4 * np.arange(16)[:, None] + np.arange(4)[None, :]
    theta = 2.0 * np.pi * np.einsum("de,rm->derm", ky, y) / GRID
    c, s = np.cos(theta), np.sin(theta)
    there = np.zeros((16, 2, 4, 2, 2, 32))
    there[:, 0, :, :, 0, :] = c
    there[:, 0, :, :, 1, :] = s
    there[:, 1, :, :, 0, :] = -s
    there[:, 1, :, :, 1, :] = c
    back = np.zeros((2, 2, 32, 16, 2, 4))
    ct, st = np.einsum("derm->rmde", c), np.einsum("derm->rmde", s)
    back[:, 0, :, :, 0, :] = ct
    back[:, 0, :, :, 1, :] = -st
    back[:, 1, :, :, 0, :] = st
    back[:, 1, :, :, 1, :] = ct
    return there.reshape(128, 128), back.reshape(128, 128)


def column_tables():
    d = np.arange(16)
    theta = 2.0 * np.pi * np.outer(d, d) / 16.0
    c, s = np.cos(theta), np.sin(theta)
    same = np.eye(4)
    there = np.zeros((2, 16, 4, 16, 2, 4))
    there[0, :, :, :, 0, :] = np.einsum("bd,ef->bedf", c, same)
    there[0, :, :, :, 1, :] = np.einsum("bd,ef->bedf", s, same)
    there[1, :, :, :, 0, :] = np.einsum("bd,ef->bedf", -s, same)
    there[1, :, :, :, 1, :] = np.einsum("bd,ef->bedf", c, same)
    there = there.reshape(128, 128)
    phi = 2.0 * np.pi * np.outer(np.arange(16), np.arange(4)) / GRID
    twist = np.stack([np.cos(phi), np.sin(phi)])[:, :, None, :, None]
    twist = np.broadcast_to(twist, (2, 16, 4, 4, KEPT)).reshape(2, 64, 128)
    quarter = 2.0 * np.pi * np.outer(np.arange(4), np.arange(4)) / 4.0
    cq, sq = np.rint(np.cos(quarter)), np.rint(np.sin(quarter))
    kept = np.eye(KEPT)
    four = np.zeros((2, 4, KEPT, 2, 4, KEPT))
    four[0, :, :, 0] = np.einsum("la,kK->lkaK", cq, kept)
    four[1, :, :, 0] = np.einsum("la,kK->lkaK", sq, kept)
    four[0, :, :, 1] = np.einsum("la,kK->lkaK", -sq, kept)
    four[1, :, :, 1] = np.einsum("la,kK->lkaK", cq, kept)
    four = four.reshape(256, 256)
    return there, there.T.copy(), twist.astype(np.float32), four, four.T.copy()


def right_table(table):
    high, low = halves(table)
    return np.block([[high, low], [high, np.zeros_like(low)]])


def left_table(table):
    return np.ascontiguousarray(right_table(table.T).T)


def split(x):
    high = x.astype(jnp.bfloat16)
    low = (x - high.astype(jnp.float32)).astype(jnp.bfloat16)
    return high, low


def mm(a, b):
    return jnp.dot(a, b, preferred_element_type=jnp.float32)


def from_left_values(table_ref, pairs):
    both = jnp.concatenate([jnp.concatenate(pair, axis=0) for pair in pairs], axis=1)
    total = mm(table_ref[:128, :], both)
    return total + mm(table_ref[128:, :128], both[:128])


def from_left_halves(table_ref, pairs):
    both = jnp.concatenate([jnp.concatenate(pair, axis=0) for pair in pairs], axis=1)
    both = mm(table_ref[...], both)
    return both[:128] + both[128:]


def from_right(tiles, table_ref):
    results = []
    for l, tile in enumerate(tiles):
        both = mm(jnp.concatenate(split(tile), axis=1), table_ref[l])
        results.append(both[:, :128] + both[:, 128:])
    return results


def gather_chunks(tiles):
    lane = lax.broadcasted_iota(jnp.int32, tiles[0].shape, 1)
    odd = lax.bitwise_and(lane, 32) != 0
    upper = lax.bitwise_and(lane, 64) != 0
    tiles = [jnp.where(odd, tiles[(j + 1) % 4], tiles[j]) for j in range(4)]
    tiles = [jnp.where(upper, tiles[(j + 2) % 4], tiles[j]) for j in range(4)]
    return [tiles[-k % 4] for k in range(4)]


def roll_chunks(tile, count):
    return pltpu.roll(tile, 32 * (count % 4), 1) if count % 4 else tile


def slopes_of(bits, low, high):
    at = [jnp.where(bit == 1, high, low) for bit in bits]
    far = [jnp.where(bit == 1, low, high) for bit in bits]

    def slope(corner, axis):
        value = None
        for other in range(3):
            if other != axis:
                factor = at[other] if corner >> other & 1 else far[other]
                value = factor if value is None else value * factor
        return value if corner >> axis & 1 else -value

    return slope


def point_slopes(point):
    low, high = jnp.float32(GAUSS_LOW), jnp.float32(GAUSS_HIGH)
    bits = [lax.bitwise_and(lax.shift_right_logical(point, d), 1) for d in range(3)]
    slope = slopes_of(bits, low, high)
    return [[slope(corner, d) for d in range(3)] for corner in range(8)]


def macro_strain(point, slopes, conn_ref, disp_ref):
    element = lax.shift_right_logical(point, 3)
    grad = [[jnp.float32(0.0)] * 3 for _ in range(3)]
    for corner in range(8):
        node = conn_ref[element, corner]
        for k in range(3):
            u = disp_ref[k, node]
            for d in range(3):
                grad[k][d] = grad[k][d] + slopes[corner][d] * u
    strain = []
    for i, j in TENSOR_PAIRS:
        strain.append(grad[i][i] if i == j else 0.5 * (grad[i][j] + grad[j][i]))
    return strain


def material(elastic, phases, flags):
    hard = phases == 1
    limit = jnp.where(hard, 1.2, 0.3)
    ratio = jnp.where(
        hard,
        3.0 * SHEAR_MODULUS / (3.0 * SHEAR_MODULUS + 10.0),
        3.0 * SHEAR_MODULUS / (3.0 * SHEAR_MODULUS + 2.0),
    )
    active = flags.astype(jnp.float32)
    volume = elastic[0] + elastic[1] + elastic[2]
    third = volume * (1.0 / 3.0)
    trial = [2.0 * SHEAR_MODULUS * (elastic[a] - third) for a in range(3)]
    trial += [2.0 * SHEAR_MODULUS * elastic[a] for a in range(3, 6)]
    normal = trial[0] * trial[0] + trial[1] * trial[1] + trial[2] * trial[2]
    shear = trial[3] * trial[3] + trial[4] * trial[4] + trial[5] * trial[5]
    equivalent = jnp.sqrt(1.5 * (normal + 2.0 * shear))
    bounded = jnp.maximum(equivalent, limit)
    inverse = 1.0 / bounded
    scaled = ratio * active
    softening = 1.0 - scaled * (equivalent - limit) * inverse
    pressure = BULK_MODULUS * volume
    stress = [trial[a] * softening + pressure for a in range(3)]
    stress += [trial[a] * softening for a in range(3, 6)]
    weight = 3.0 * SHEAR_MODULUS * scaled * limit * (inverse * inverse * inverse)
    return stress, trial, softening, weight


def every_fourth(ref, start, plane):
    return ref[pl.ds(start + plane, 32, stride=4), :]


def plane_waves():
    row = lax.broadcasted_iota(jnp.int32, (8, 128), 0)
    lane = lax.broadcasted_iota(jnp.int32, (8, 128), 1)
    inner = lax.bitwise_and(row, 3).astype(jnp.float32)
    depth = lax.bitwise_and(lane, 31).astype(jnp.float32)
    starts = [4.0 * d if d < 8 else 4.0 * d - GRID for d in range(16)]
    wave_y = jnp.concatenate([inner + start for start in starts], axis=0)
    return wave_y, jnp.concatenate([depth] * 16, axis=0)


def forward_planes(stresses, depth, rows, out_ref, turn=0):
    tiles = gather_chunks(from_right(stresses, depth))
    tiles = [roll_chunks(tile, -s) for s, tile in enumerate(tiles)]
    pairs = [
        split(jnp.concatenate([tile[c * 32 : (c + 1) * 32] for tile in tiles], axis=0))
        for c in range(6)
    ]
    spectrum = from_left_halves(rows, pairs)
    xx, yy, zz, yz, xz, xy = (spectrum[:, c * 128 : (c + 1) * 128] for c in range(6))
    wave_y, wave_z = plane_waves()
    fields = (xx, xy, xz, wave_y * yy + wave_z * yz, wave_y * yz + wave_z * zz)
    for c, field in enumerate(fields):
        block = field.reshape(16, 8, 128)
        out_ref[: 16 - turn, c * 8 : (c + 1) * 8, :] = block[turn:]
        if turn:
            out_ref[16 - turn :, c * 8 : (c + 1) * 8, :] = block[:turn]


def backward_planes(in_ref, depth, rows):
    xx, xy, xz, y, z = (
        in_ref[:, c * 8 : (c + 1) * 8, :].reshape(128, 128) for c in range(FIELDS)
    )
    wave_y, wave_z = plane_waves()
    yy, zz = 2.0 * (wave_y * y), 2.0 * (wave_z * z)
    pairs = [split(value) for value in (xx, yy, zz, wave_y * z + wave_z * y, xz, xy)]
    lines = from_left_values(rows, pairs)
    tiles = [
        jnp.concatenate(
            [lines[s * 32 : (s + 1) * 32, c * 128 : (c + 1) * 128] for c in range(6)], axis=0
        )
        for s in range(4)
    ]
    tiles = [roll_chunks(tile, s) for s, tile in enumerate(tiles)]
    return from_right(gather_chunks(tiles), depth)


def basis_of(points, conn_ref):
    shape = (points, 128)
    lane = lax.broadcasted_iota(jnp.int32, shape, 1)
    point = lax.broadcasted_iota(jnp.int32, shape, 0)
    element = lax.shift_right_logical(point, 3)
    bits = [lax.bitwise_and(lax.shift_right_logical(point, d), 1) for d in range(3)]
    slope = slopes_of(bits, GAUSS_LOW, GAUSS_HIGH)
    node = lane // 3
    part = lane - 3 * node
    elements = conn_ref.shape[0]
    grad = [jnp.zeros(shape, jnp.float32) for _ in range(3)]
    for corner in range(8):
        owner = jnp.full(shape, conn_ref[0, corner], jnp.int32)
        for e in range(1, elements):
            owner = jnp.where(element == e, conn_ref[e, corner], owner)
        here = (owner == node) & (lane < 60)
        for d in range(3):
            grad[d] = grad[d] + jnp.where(here, slope(corner, d), 0.0)
    basis = []
    for i, k in TENSOR_PAIRS:
        if i == k:
            basis.append(jnp.where(part == i, grad[i], 0.0))
        else:
            value = jnp.where(part == i, 0.5 * grad[k], 0.0)
            basis.append(value + jnp.where(part == k, 0.5 * grad[i], 0.0))
    return jnp.concatenate(basis, axis=0)


def first_kernel(
    points, conn_hbm, disp_hbm, phase_hbm, flag_hbm, plastic_hbm, depth_hbm, rows_hbm,
    out_ref, macro_ref, basis_ref, turned_ref,
    conn_ref, disp_ref, phase_ref, flag_ref, plastic_ref, depth, rows, sems,
):
    pairs = (
        (conn_hbm, conn_ref), (disp_hbm, disp_ref), (plastic_hbm, plastic_ref),
        (phase_hbm, phase_ref), (flag_hbm.at[pl.ds(0, 128)], flag_ref),
        (depth_hbm, depth), (rows_hbm, rows),
    )
    copies = [pltpu.make_async_copy(a, b, sems.at[i]) for i, (a, b) in enumerate(pairs)]
    for copy in copies:
        copy.start()
    point = lax.axis_index("rve")
    slopes = point_slopes(point)
    for copy in copies[:2]:
        copy.wait()
    macro = macro_strain(point, slopes, conn_ref, disp_ref)
    row = lax.broadcasted_iota(jnp.int32, (8, 128), 0)
    table = jnp.zeros((8, 128), jnp.float32)
    for c in range(6):
        table = jnp.where(row == c, macro[c], table)
    macro_ref[...] = table
    for copy in copies[2:5]:
        copy.wait()
    stresses = []
    for plane in range(PLANES):
        elastic = [macro[c] - every_fourth(plastic_ref, c * 128, plane) for c in range(6)]
        phases = every_fourth(phase_ref, 0, plane)
        flags = every_fourth(flag_ref, 0, plane)
        stress = material(elastic, phases, flags)[0]
        stresses.append(jnp.concatenate(stress, axis=0))
    for copy in copies[5:]:
        copy.wait()
    basis = basis_of(points, conn_ref)
    basis_ref[...] = basis
    high, low = split(jnp.transpose(basis))
    turned_ref[0] = high
    turned_ref[1] = low
    forward_planes(stresses, depth, rows, out_ref, FAR)


def middle_kernel(
    macro_ref, phase_ref, flag_ref, plastic_ref, in_ref, back_depth, back_rows, depth, rows,
    out_ref, elastic_ref,
):
    macro = [macro_ref[c : c + 1, :] for c in range(6)]
    correction = backward_planes(in_ref, back_depth, back_rows)
    stresses = []
    for plane in range(PLANES):
        elastic = []
        for c in range(6):
            at = plane * 192 + c * 32
            before = macro[c] - every_fourth(plastic_ref, c * 128, plane)
            after = before - correction[plane][c * 32 : (c + 1) * 32]
            elastic_ref[at : at + 32, :] = after
            elastic.append(after)
        phases = every_fourth(phase_ref, 0, plane)
        flags = every_fourth(flag_ref, 128, plane)
        stress = material(elastic, phases, flags)[0]
        stresses.append(jnp.concatenate(stress, axis=0))
    forward_planes(stresses, depth, rows, out_ref)


def last_kernel(
    phase_ref, flag_ref, elastic_ref, in_ref, back_depth, back_rows, out_ref
):
    correction = backward_planes(in_ref, back_depth, back_rows)
    sums = [None] * 28

    def collect(at, value):
        part = value.reshape(4, 8, 128)
        part = (part[0] + part[1]) + (part[2] + part[3])
        sums[at] = part if sums[at] is None else sums[at] + part

    for plane in range(PLANES):
        elastic = [
            elastic_ref[plane * 192 + c * 32 : plane * 192 + (c + 1) * 32, :]
            - correction[plane][c * 32 : (c + 1) * 32]
            for c in range(6)
        ]
        phases = every_fourth(phase_ref, 0, plane)
        flags = every_fourth(flag_ref, 256, plane)
        stress, trial, softening, weight = material(elastic, phases, flags)
        for c in range(6):
            collect(c, stress[c])
        collect(6, softening)
        at = 7
        for a in range(6):
            scaled = weight * trial[a]
            for b in range(a, 6):
                collect(at, scaled * trial[b])
                at += 1
    row = lax.broadcasted_iota(jnp.int32, (8, 128), 0)
    groups = [jnp.zeros((8, 128), jnp.float32)] * 16
    totals = [jnp.sum(value, axis=0, keepdims=True) for value in sums]

    def place(at, value):
        here = jnp.broadcast_to(value, (8, 128))
        groups[at // 8] = jnp.where(row == at % 8, here, groups[at // 8])

    for c in range(7):
        place(c, totals[c])
    at = 7
    for a in range(6):
        for b in range(a, 6):
            place(OUTER_AT + 6 * a + b, totals[at])
            if a != b:
                place(OUTER_AT + 6 * b + a, totals[at])
            at += 1
    lines = jnp.concatenate(groups, axis=0)
    ones = jnp.ones((SLABS, 128), jnp.float32)
    line = lax.dot_general(
        ones, lines, (((1,), (1,)), ((), ())),
        precision=lax.Precision.HIGHEST, preferred_element_type=jnp.float32,
    )
    out_ref[...] = line.reshape(SLABS, 1, 128)


def column_kernel(turn, in_ref, columns, back_columns, twist_ref, four, back_four, out_ref):
    pairs = []
    for c in range(FIELDS):
        block = in_ref[:, c * 8 : (c + 1) * 8, :]
        if turn:
            block = jnp.concatenate([block[16 - turn :], block[: 16 - turn]], axis=0)
        pairs.append(split(block.reshape(128, 128)))
    mixed = from_left_values(columns, pairs)
    cosine, sine = twist_ref[0], twist_ref[1]

    def turn(values, table_ref):
        high, low = split(jnp.concatenate(values, axis=0))
        return mm(high, table_ref[...]) + mm(low, table_ref[...])

    values = []
    for c in range(FIELDS):
        lanes = slice(c * 128, (c + 1) * 128)
        real, imag = mixed[:64, lanes], mixed[64:, lanes]
        turned = (real * cosine + imag * sine, imag * cosine - real * sine)
        values.append(jnp.concatenate(turned, axis=1))
    spectrum = turn(values, four)
    xx, xy, xz, y, z = (spectrum[c * 64 : (c + 1) * 64] for c in range(FIELDS))

    shape = (64, 128)
    row = lax.broadcasted_iota(jnp.int32, shape, 0)
    lane = lax.broadcasted_iota(jnp.int32, shape, 1)
    kx = 16 * lax.shift_right_logical(lane, 5) + lax.shift_right_logical(row, 2)
    ky = 4 * lax.axis_index("slab") + lax.bitwise_and(row, 3)
    kz = lax.bitwise_and(lane, 31)
    half = GRID // 2
    keep = (kx != half) & (ky != half) & (kx + ky + kz > 0)
    xi = [
        jnp.where(kx < half, kx, kx - GRID).astype(jnp.float32),
        jnp.where(ky < half, ky, ky - GRID).astype(jnp.float32),
        kz.astype(jnp.float32),
    ]
    length = xi[0] * xi[0] + xi[1] * xi[1] + xi[2] * xi[2]
    inverse = jnp.where(keep, 1.0 / jnp.maximum(length, 1.0), 0.0)
    coupling = (REFERENCE_LAME + REFERENCE_SHEAR) / (
        REFERENCE_SHEAR * (REFERENCE_LAME + 2.0 * REFERENCE_SHEAR)
    )
    xi = [jnp.concatenate([value, value], axis=1) for value in xi]
    inverse = jnp.concatenate([inverse, inverse], axis=1)
    scaled = inverse * (1.0 / (2.0 * REFERENCE_SHEAR))
    traction = [xi[0] * xx + xi[1] * xy + xi[2] * xz, xi[0] * xy + y, xi[0] * xz + z]
    load = xi[0] * traction[0] + xi[1] * traction[1] + xi[2] * traction[2]
    load = load * (inverse * (REFERENCE_SHEAR * coupling))
    field = [scaled * (traction[i] - xi[i] * load) for i in range(3)]
    values = [
        2.0 * (xi[0] * field[0]),
        xi[0] * field[1] + xi[1] * field[0],
        xi[0] * field[2] + xi[2] * field[0],
        field[1],
        field[2],
    ]
    turned = turn(values, back_four)
    for c in range(FIELDS):
        real, imag = turned[c * 64 : (c + 1) * 64, :128], turned[c * 64 : (c + 1) * 64, 128:]
        first, second = real * cosine - imag * sine, real * sine + imag * cosine
        pairs[c] = split(jnp.concatenate([first, second], axis=0))
    result = from_left_values(back_columns, pairs)
    for c in range(FIELDS):
        out_ref[:, c * 8 : (c + 1) * 8, :] = result[:, c * 128 : (c + 1) * 128].reshape(16, 8, 128)


def totals_kernel(in_ref, all_ref):
    line = jnp.sum(in_ref[...].reshape(SLABS, 128), axis=0, keepdims=True)
    all_ref[...] = jnp.broadcast_to(line[None], all_ref.shape)


def own_outputs(line, stress_ref, tangent_ref):
    stress_ref[...] = line[:, :6]
    at = lax.broadcasted_iota(jnp.int32, (1, 128), 1) - OUTER_AT
    a = at // 6
    b = at - 6 * a
    both = (a < 3) & (b < 3)
    shear = jnp.broadcast_to(line[:, 6:7], (1, 128)) * (2.0 * SHEAR_MODULUS)
    fixed = jnp.where(both, BULK_MODULUS - shear * (1.0 / 3.0), 0.0)
    fixed = fixed + jnp.where(a == b, shear, 0.0)
    whole = (fixed - line * jnp.where(b < 3, 1.0, 2.0)) * (1.0 / TANGENT_UNIT)
    for i in range(6):
        tangent_ref[i] = whole[:, OUTER_AT + 6 * i : OUTER_AT + 6 * i + 6]


def assembly_kernel(
    points, basis_ref, turned_ref, in_ref, stress_ref, tangent_ref, stiffness_ref, forces_ref
):
    start = first_of(points)
    own = lax.rem(lax.axis_index("rve") + points - start, points)
    own_outputs(in_ref[own] * (1.0 / VOXELS), stress_ref, tangent_ref)
    shape = (points, 128)
    sums = in_ref[...].reshape(points, 128) * (1.0 / VOXELS)
    sums = jnp.concatenate([sums[points - start :], sums[: points - start]], axis=0)
    basis = [basis_ref[a * points : (a + 1) * points, :] for a in range(6)]
    mean_shear = 2.0 * SHEAR_MODULUS * sums[:, 6:7]

    def column(at):
        return jnp.broadcast_to(sums[:, at : at + 1], shape)

    mean_shear = jnp.broadcast_to(mean_shear, shape)
    on_diagonal = BULK_MODULUS + mean_shear * (2.0 / 3.0)
    off_diagonal = BULK_MODULUS - mean_shear * (1.0 / 3.0)
    answers = []
    force = jnp.zeros(shape, jnp.float32)
    scale = QUADRATURE_WEIGHT / TANGENT_UNIT
    for a in range(6):
        total = jnp.zeros(shape, jnp.float32)
        for b in range(6):
            low, high = min(a, b), max(a, b)
            entry = -PAIR_WEIGHTS[b] * column(OUTER_AT + 6 * low + high)
            if a == b:
                entry = entry + (on_diagonal if a < 3 else mean_shear)
            elif a < 3 and b < 3:
                entry = entry + off_diagonal
            total = total + entry * basis[b]
        answers.append(total * (PAIR_WEIGHTS[a] * scale))
        force = force + basis[a] * (column(a) * (PAIR_WEIGHTS[a] * QUADRATURE_WEIGHT))
    high, low = split(jnp.concatenate(answers, axis=0))
    left_high, left_low = turned_ref[0], turned_ref[1]
    whole = mm(left_high, high) + (mm(left_low, high) + mm(left_high, low))
    stiffness_ref[...] = whole[:60, :60]
    line = jnp.sum(force, axis=0, keepdims=True)
    part8 = lax.broadcasted_iota(jnp.int32, (8, 128), 0)
    lane8 = lax.broadcasted_iota(jnp.int32, (8, 128), 1)
    spread = jnp.where(lane8 % 3 == part8, jnp.broadcast_to(line, (8, 128)), 0.0)
    pick_row = lax.broadcasted_iota(jnp.int32, (128, 128), 0)
    pick_col = lax.broadcasted_iota(jnp.int32, (128, 128), 1)
    pick = (pick_row // 3 == pick_col).astype(jnp.float32)
    forces = jnp.dot(
        spread, pick, precision=lax.Precision.HIGHEST, preferred_element_type=jnp.float32
    )
    forces_ref[...] = forces[:3, :20]


VMEM = pl.BlockSpec(memory_space=pltpu.VMEM)
HBM = pl.BlockSpec(memory_space=pltpu.HBM)
BF16 = jnp.bfloat16
F32 = jnp.float32
LIMIT = 16 * 1024 * 1024


def params():
    return pltpu.CompilerParams(vmem_limit_bytes=LIMIT)


def cost(flops, size):
    return pl.CostEstimate(flops=flops, bytes_accessed=size, transcendentals=0)


def first_of(points):
    return points // 2 + 1 if points > 1 else 0


def exchange(array, turn=0):
    groups = [[(d + turn) % SLABS for d in range(SLABS)]] if turn else None
    return lax.all_to_all(
        array, "slab", split_axis=0, concat_axis=0, tiled=True, axis_index_groups=groups
    )


def on_device(phase_ids, yield_flags, plastic_strain, displacements, connectivity):
    points = lax.axis_size("rve")

    def rows(array):
        lead = math.prod(array.shape[:-2])
        array = array.reshape(lead, PLANES, 32, 128)
        return jnp.transpose(array, (0, 2, 1, 3)).reshape(lead * 128, 128)

    phases = rows(phase_ids)
    flags = rows(yield_flags)
    plastic = rows(plastic_strain)

    there, back = depth_tables()
    depth, back_depth = (
        jnp.asarray(np.stack([right_table(np.roll(t, 32 * l, axis)) for l in range(PLANES)]))
        for t, axis in ((there, 1), (back, 0))
    )
    there, back = row_tables()
    line, back_line = jnp.asarray(left_table(there)), jnp.asarray(left_table(back))
    there, back, twist, four, back_four = column_tables()
    column, back_column = jnp.asarray(left_table(there)), jnp.asarray(left_table(back))
    twist = jnp.asarray(twist)
    four = jnp.asarray(four.astype(ml_dtypes.bfloat16))
    back_four = jnp.asarray(back_four.astype(ml_dtypes.bfloat16))

    block = jax.ShapeDtypeStruct((16, 8 * FIELDS, 128), F32)

    first = pl.pallas_call(
        functools.partial(first_kernel, points),
        out_shape=(
            block, jax.ShapeDtypeStruct((8, 128), F32),
            jax.ShapeDtypeStruct((6 * points, 128), F32),
            jax.ShapeDtypeStruct((2, 128, 6 * points), BF16),
        ),
        in_specs=[HBM] * 7, out_specs=(VMEM,) * 4,
        scratch_shapes=[
            pltpu.SMEM(connectivity.shape, jnp.int32), pltpu.SMEM(displacements.shape[::-1], F32),
            pltpu.VMEM((128, 128), jnp.int32), pltpu.VMEM((128, 128), jnp.int32),
            pltpu.VMEM((768, 128), F32), pltpu.VMEM((PLANES, 256, 256), BF16),
            pltpu.VMEM((256, 256), BF16),
            pltpu.SemaphoreType.DMA((7,)),
        ],
        compiler_params=params(), cost_estimate=cost(400_000_000, 2_000_000), name="first",
    )
    def columns(turn):
        return pl.pallas_call(
            functools.partial(column_kernel, turn), out_shape=block,
            in_specs=[VMEM] * 6, out_specs=VMEM, compiler_params=params(),
            cost_estimate=cost(400_000_000, 2_000_000), name="columns",
        )

    middle = pl.pallas_call(
        middle_kernel, out_shape=(block, jax.ShapeDtypeStruct((768, 128), F32)),
        in_specs=[VMEM] * 9, out_specs=(VMEM, VMEM),
        compiler_params=params(),
        cost_estimate=cost(800_000_000, 4_000_000), name="middle",
    )
    last = pl.pallas_call(
        last_kernel, out_shape=jax.ShapeDtypeStruct((SLABS, 1, 128), F32),
        in_specs=[VMEM] * 6, out_specs=VMEM,
        compiler_params=params(),
        cost_estimate=cost(400_000_000, 2_000_000), name="last",
    )
    totals = pl.pallas_call(
        totals_kernel, out_shape=jax.ShapeDtypeStruct((points, 1, 128), F32),
        in_specs=[VMEM], out_specs=VMEM, compiler_params=params(),
        cost_estimate=cost(10_000, 50_000), name="totals",
    )
    assembly = pl.pallas_call(
        functools.partial(assembly_kernel, points),
        out_shape=(
            jax.ShapeDtypeStruct((1, 6), F32), jax.ShapeDtypeStruct((6, 1, 6), F32),
            jax.ShapeDtypeStruct((60, 60), F32), jax.ShapeDtypeStruct((3, 20), F32),
        ),
        in_specs=[VMEM] * 3, out_specs=(VMEM,) * 4, compiler_params=params(),
        cost_estimate=cost(10_000_000, 200_000), name="assembly",
    )

    def apply_columns(array, turn):
        return exchange(
            columns(turn)(exchange(array, turn), column, back_column, twist, four, back_four)
        )

    operands = (connectivity, displacements.T, phases, flags, plastic, depth, line)
    spectrum, macro, basis, turned_basis = first(
        *(pltpu.with_memory_space_constraint(operand, pltpu.HBM) for operand in operands)
    )
    planes = apply_columns(spectrum, FAR)
    spectrum, elastic = middle(
        macro, phases, flags, plastic, planes, back_depth, back_line, depth, line
    )
    planes = apply_columns(spectrum, 0)
    partial = last(phases, flags, elastic, planes, back_depth, back_line)
    everyone = totals(exchange(partial, FAR))
    turned = [(g + first_of(points)) % points for g in range(points)]
    everyone = lax.all_to_all(
        everyone, "rve", 0, 0, tiled=True, axis_index_groups=[turned]
    )
    stress, tangent, stiffness, forces = assembly(basis, turned_basis, everyone)
    return (stress, jnp.transpose(tangent, (1, 0, 2)), forces.T, stiffness)


def solution(mesh):
    return jax.shard_map(
        on_device,
        mesh=mesh,
        in_specs=(
            P("slab", None),
            P("rve", None, "slab", None),
            P("rve", None, "slab", None),
            P(),
            P(),
        ),
        out_specs=(P("rve", None), P("rve", None, None), P(), P()),
        check_vma=False,
    )
```

```python
import functools
import math

import jax
import jax.numpy as jnp
import ml_dtypes
import numpy as np
from jax import lax
from jax.experimental import pallas as pl
from jax.experimental.pallas import tpu as pltpu
from jax.sharding import PartitionSpec as P

GRID = 64
ITERS = 2
SLABS = 16
PLANES = GRID // SLABS
KEPT = GRID // 2

SHEAR_MODULUS = 80.0
BULK_MODULUS = 160.0
REFERENCE_SHEAR = 80.0
REFERENCE_LAME = 160.0 - 160.0 / 3.0
TANGENT_UNIT = 100.0
QUADRATURE_WEIGHT = 0.125
PAIR_WEIGHTS = (1.0, 1.0, 1.0, 2.0, 2.0, 2.0)
TENSOR_PAIRS = ((0, 0), (1, 1), (2, 2), (1, 2), (0, 2), (0, 1))
VOXELS = float(GRID**3)
GAUSS_LOW = 0.5 - 0.5 / math.sqrt(3.0)
GAUSS_HIGH = 0.5 + 0.5 / math.sqrt(3.0)
OUTER_AT = 8
FIELDS = 5
FAR = 10


def halves(table):
    high = table.astype(np.float32).astype(ml_dtypes.bfloat16)
    low = (table - high.astype(np.float64)).astype(np.float32).astype(ml_dtypes.bfloat16)
    return high, low


def depth_tables():
    z = np.arange(GRID)
    k = np.arange(KEPT)
    theta = 2.0 * np.pi * np.outer(z, k) / GRID
    forward = np.stack([np.cos(theta), -np.sin(theta)], axis=0)
    weight = np.where(k == 0, 1.0, 2.0) / VOXELS
    inverse = forward * weight[None, None, :]
    pair = np.eye(2)
    there = np.einsum("rR,pzk->rzRpk", pair, forward)
    back = np.einsum("rR,pzk->Rpkrz", pair, inverse)
    return there.reshape(128, 128), back.reshape(128, 128)


def row_tables():
    y = 2 * np.arange(32)[None, :] + np.arange(2)[:, None]
    ky = 4 * np.arange(16)[:, None] + np.arange(4)[None, :]
    theta = 2.0 * np.pi * np.einsum("de,rm->derm", ky, y) / GRID
    c, s = np.cos(theta), np.sin(theta)
    there = np.zeros((16, 2, 4, 2, 2, 32))
    there[:, 0, :, :, 0, :] = c
    there[:, 0, :, :, 1, :] = s
    there[:, 1, :, :, 0, :] = -s
    there[:, 1, :, :, 1, :] = c
    back = np.zeros((2, 2, 32, 16, 2, 4))
    ct, st = np.einsum("derm->rmde", c), np.einsum("derm->rmde", s)
    back[:, 0, :, :, 0, :] = ct
    back[:, 0, :, :, 1, :] = -st
    back[:, 1, :, :, 0, :] = st
    back[:, 1, :, :, 1, :] = ct
    return there.reshape(128, 128), back.reshape(128, 128)


def column_tables():
    d = np.arange(16)
    theta = 2.0 * np.pi * np.outer(d, d) / 16.0
    c, s = np.cos(theta), np.sin(theta)
    same = np.eye(4)
    there = np.zeros((2, 16, 4, 16, 2, 4))
    there[0, :, :, :, 0, :] = np.einsum("bd,ef->bedf", c, same)
    there[0, :, :, :, 1, :] = np.einsum("bd,ef->bedf", s, same)
    there[1, :, :, :, 0, :] = np.einsum("bd,ef->bedf", -s, same)
    there[1, :, :, :, 1, :] = np.einsum("bd,ef->bedf", c, same)
    there = there.reshape(128, 128)
    phi = 2.0 * np.pi * np.outer(np.arange(16), np.arange(4)) / GRID
    twist = np.stack([np.cos(phi), np.sin(phi)])[:, :, None, :, None]
    twist = np.broadcast_to(twist, (2, 16, 4, 4, KEPT)).reshape(2, 64, 128)
    quarter = 2.0 * np.pi * np.outer(np.arange(4), np.arange(4)) / 4.0
    cq, sq = np.rint(np.cos(quarter)), np.rint(np.sin(quarter))
    kept = np.eye(KEPT)
    four = np.zeros((2, 4, KEPT, 2, 4, KEPT))
    four[0, :, :, 0] = np.einsum("la,kK->lkaK", cq, kept)
    four[1, :, :, 0] = np.einsum("la,kK->lkaK", sq, kept)
    four[0, :, :, 1] = np.einsum("la,kK->lkaK", -sq, kept)
    four[1, :, :, 1] = np.einsum("la,kK->lkaK", cq, kept)
    four = four.reshape(256, 256)
    return there, there.T.copy(), twist.astype(np.float32), four, four.T.copy()


def right_table(table):
    high, low = halves(table)
    return np.block([[high, low], [high, np.zeros_like(low)]])


def left_table(table):
    return np.ascontiguousarray(right_table(table.T).T)


def split(x):
    high = x.astype(jnp.bfloat16)
    low = (x - high.astype(jnp.float32)).astype(jnp.bfloat16)
    return high, low


def mm(a, b):
    return jnp.dot(a, b, preferred_element_type=jnp.float32)


def from_left_values(table_ref, pairs):
    both = jnp.concatenate([jnp.concatenate(pair, axis=0) for pair in pairs], axis=1)
    total = mm(table_ref[:128, :], both)
    return total + mm(table_ref[128:, :128], both[:128])


def from_left_halves(table_ref, pairs):
    both = jnp.concatenate([jnp.concatenate(pair, axis=0) for pair in pairs], axis=1)
    both = mm(table_ref[...], both)
    return both[:128] + both[128:]


def from_right(tiles, table_ref):
    results = []
    for l, tile in enumerate(tiles):
        both = mm(jnp.concatenate(split(tile), axis=1), table_ref[l])
        results.append(both[:, :128] + both[:, 128:])
    return results


def gather_chunks(tiles):
    lane = lax.broadcasted_iota(jnp.int32, tiles[0].shape, 1)
    odd = lax.bitwise_and(lane, 32) != 0
    upper = lax.bitwise_and(lane, 64) != 0
    tiles = [jnp.where(odd, tiles[(j + 1) % 4], tiles[j]) for j in range(4)]
    tiles = [jnp.where(upper, tiles[(j + 2) % 4], tiles[j]) for j in range(4)]
    return [tiles[-k % 4] for k in range(4)]


def roll_chunks(tile, count):
    return pltpu.roll(tile, 32 * (count % 4), 1) if count % 4 else tile


def slopes_of(bits, low, high):
    at = [jnp.where(bit == 1, high, low) for bit in bits]
    far = [jnp.where(bit == 1, low, high) for bit in bits]

    def slope(corner, axis):
        value = None
        for other in range(3):
            if other != axis:
                factor = at[other] if corner >> other & 1 else far[other]
                value = factor if value is None else value * factor
        return value if corner >> axis & 1 else -value

    return slope


def point_slopes(point):
    low, high = jnp.float32(GAUSS_LOW), jnp.float32(GAUSS_HIGH)
    bits = [lax.bitwise_and(lax.shift_right_logical(point, d), 1) for d in range(3)]
    slope = slopes_of(bits, low, high)
    return [[slope(corner, d) for d in range(3)] for corner in range(8)]


def macro_strain(point, slopes, conn_ref, disp_ref):
    element = lax.shift_right_logical(point, 3)
    grad = [[jnp.float32(0.0)] * 3 for _ in range(3)]
    for corner in range(8):
        node = conn_ref[element, corner]
        for k in range(3):
            u = disp_ref[k, node]
            for d in range(3):
                grad[k][d] = grad[k][d] + slopes[corner][d] * u
    strain = []
    for i, j in TENSOR_PAIRS:
        strain.append(grad[i][i] if i == j else 0.5 * (grad[i][j] + grad[j][i]))
    return strain


def material(elastic, phases, flags):
    hard = phases == 1
    limit = jnp.where(hard, 1.2, 0.3)
    ratio = jnp.where(
        hard,
        3.0 * SHEAR_MODULUS / (3.0 * SHEAR_MODULUS + 10.0),
        3.0 * SHEAR_MODULUS / (3.0 * SHEAR_MODULUS + 2.0),
    )
    active = flags.astype(jnp.float32)
    volume = elastic[0] + elastic[1] + elastic[2]
    third = volume * (1.0 / 3.0)
    trial = [2.0 * SHEAR_MODULUS * (elastic[a] - third) for a in range(3)]
    trial += [2.0 * SHEAR_MODULUS * elastic[a] for a in range(3, 6)]
    normal = trial[0] * trial[0] + trial[1] * trial[1] + trial[2] * trial[2]
    shear = trial[3] * trial[3] + trial[4] * trial[4] + trial[5] * trial[5]
    equivalent = jnp.sqrt(1.5 * (normal + 2.0 * shear))
    bounded = jnp.maximum(equivalent, limit)
    inverse = 1.0 / bounded
    scaled = ratio * active
    softening = 1.0 - scaled * (equivalent - limit) * inverse
    pressure = BULK_MODULUS * volume
    stress = [trial[a] * softening + pressure for a in range(3)]
    stress += [trial[a] * softening for a in range(3, 6)]
    weight = 3.0 * SHEAR_MODULUS * scaled * limit * (inverse * inverse * inverse)
    return stress, trial, softening, weight


def every_fourth(ref, start, plane):
    return ref[pl.ds(start + plane, 32, stride=4), :]


def plane_waves():
    row = lax.broadcasted_iota(jnp.int32, (8, 128), 0)
    lane = lax.broadcasted_iota(jnp.int32, (8, 128), 1)
    inner = lax.bitwise_and(row, 3).astype(jnp.float32)
    depth = lax.bitwise_and(lane, 31).astype(jnp.float32)
    starts = [4.0 * d if d < 8 else 4.0 * d - GRID for d in range(16)]
    wave_y = jnp.concatenate([inner + start for start in starts], axis=0)
    return wave_y, jnp.concatenate([depth] * 16, axis=0)


def forward_planes(stresses, depth, rows, out_ref, turn=0):
    tiles = gather_chunks(from_right(stresses, depth))
    tiles = [roll_chunks(tile, -s) for s, tile in enumerate(tiles)]
    pairs = [
        split(jnp.concatenate([tile[c * 32 : (c + 1) * 32] for tile in tiles], axis=0))
        for c in range(6)
    ]
    spectrum = from_left_halves(rows, pairs)
    xx, yy, zz, yz, xz, xy = (spectrum[:, c * 128 : (c + 1) * 128] for c in range(6))
    wave_y, wave_z = plane_waves()
    fields = (xx, xy, xz, wave_y * yy + wave_z * yz, wave_y * yz + wave_z * zz)
    for c, field in enumerate(fields):
        block = field.reshape(16, 8, 128)
        out_ref[: 16 - turn, c * 8 : (c + 1) * 8, :] = block[turn:]
        if turn:
            out_ref[16 - turn :, c * 8 : (c + 1) * 8, :] = block[:turn]


def backward_planes(in_ref, depth, rows):
    xx, xy, xz, y, z = (
        in_ref[:, c * 8 : (c + 1) * 8, :].reshape(128, 128) for c in range(FIELDS)
    )
    wave_y, wave_z = plane_waves()
    yy, zz = 2.0 * (wave_y * y), 2.0 * (wave_z * z)
    pairs = [split(value) for value in (xx, yy, zz, wave_y * z + wave_z * y, xz, xy)]
    lines = from_left_values(rows, pairs)
    tiles = [
        jnp.concatenate(
            [lines[s * 32 : (s + 1) * 32, c * 128 : (c + 1) * 128] for c in range(6)], axis=0
        )
        for s in range(4)
    ]
    tiles = [roll_chunks(tile, s) for s, tile in enumerate(tiles)]
    return from_right(gather_chunks(tiles), depth)


def basis_of(points, conn_ref):
    shape = (points, 128)
    lane = lax.broadcasted_iota(jnp.int32, shape, 1)
    point = lax.broadcasted_iota(jnp.int32, shape, 0)
    element = lax.shift_right_logical(point, 3)
    bits = [lax.bitwise_and(lax.shift_right_logical(point, d), 1) for d in range(3)]
    slope = slopes_of(bits, GAUSS_LOW, GAUSS_HIGH)
    node = lane // 3
    part = lane - 3 * node
    elements = conn_ref.shape[0]
    grad = [jnp.zeros(shape, jnp.float32) for _ in range(3)]
    for corner in range(8):
        owner = jnp.full(shape, conn_ref[0, corner], jnp.int32)
        for e in range(1, elements):
            owner = jnp.where(element == e, conn_ref[e, corner], owner)
        here = (owner == node) & (lane < 60)
        for d in range(3):
            grad[d] = grad[d] + jnp.where(here, slope(corner, d), 0.0)
    basis = []
    for i, k in TENSOR_PAIRS:
        if i == k:
            basis.append(jnp.where(part == i, grad[i], 0.0))
        else:
            value = jnp.where(part == i, 0.5 * grad[k], 0.0)
            basis.append(value + jnp.where(part == k, 0.5 * grad[i], 0.0))
    return jnp.concatenate(basis, axis=0)


def first_kernel(
    points, conn_hbm, disp_hbm, phase_hbm, flag_hbm, plastic_hbm, depth_hbm, rows_hbm,
    out_ref, macro_ref, basis_ref, turned_ref,
    conn_ref, disp_ref, phase_ref, flag_ref, plastic_ref, depth, rows, sems,
):
    pairs = (
        (conn_hbm, conn_ref), (disp_hbm, disp_ref), (plastic_hbm, plastic_ref),
        (phase_hbm, phase_ref), (flag_hbm.at[pl.ds(0, 128)], flag_ref),
        (depth_hbm, depth), (rows_hbm, rows),
    )
    copies = [pltpu.make_async_copy(a, b, sems.at[i]) for i, (a, b) in enumerate(pairs)]
    for copy in copies:
        copy.start()
    point = lax.axis_index("rve")
    slopes = point_slopes(point)
    for copy in copies[:2]:
        copy.wait()
    macro = macro_strain(point, slopes, conn_ref, disp_ref)
    row = lax.broadcasted_iota(jnp.int32, (8, 128), 0)
    table = jnp.zeros((8, 128), jnp.float32)
    for c in range(6):
        table = jnp.where(row == c, macro[c], table)
    macro_ref[...] = table
    for copy in copies[2:5]:
        copy.wait()
    stresses = []
    for plane in range(PLANES):
        elastic = [macro[c] - every_fourth(plastic_ref, c * 128, plane) for c in range(6)]
        phases = every_fourth(phase_ref, 0, plane)
        flags = every_fourth(flag_ref, 0, plane)
        stress = material(elastic, phases, flags)[0]
        stresses.append(jnp.concatenate(stress, axis=0))
    for copy in copies[5:]:
        copy.wait()
    basis = basis_of(points, conn_ref)
    basis_ref[...] = basis
    high, low = split(jnp.transpose(basis))
    turned_ref[0] = high
    turned_ref[1] = low
    forward_planes(stresses, depth, rows, out_ref, FAR)


def middle_kernel(
    macro_ref, phase_ref, flag_ref, plastic_ref, in_ref, back_depth, back_rows, depth, rows,
    out_ref, elastic_ref,
):
    macro = [macro_ref[c : c + 1, :] for c in range(6)]
    correction = backward_planes(in_ref, back_depth, back_rows)
    stresses = []
    for plane in range(PLANES):
        elastic = []
        for c in range(6):
            at = plane * 192 + c * 32
            before = macro[c] - every_fourth(plastic_ref, c * 128, plane)
            after = before - correction[plane][c * 32 : (c + 1) * 32]
            elastic_ref[at : at + 32, :] = after
            elastic.append(after)
        phases = every_fourth(phase_ref, 0, plane)
        flags = every_fourth(flag_ref, 128, plane)
        stress = material(elastic, phases, flags)[0]
        stresses.append(jnp.concatenate(stress, axis=0))
    forward_planes(stresses, depth, rows, out_ref, FAR)


def last_kernel(
    phase_ref, flag_ref, elastic_ref, in_ref, back_depth, back_rows, out_ref
):
    correction = backward_planes(in_ref, back_depth, back_rows)
    sums = [None] * 28

    def collect(at, value):
        part = value.reshape(4, 8, 128)
        part = (part[0] + part[1]) + (part[2] + part[3])
        sums[at] = part if sums[at] is None else sums[at] + part

    for plane in range(PLANES):
        elastic = [
            elastic_ref[plane * 192 + c * 32 : plane * 192 + (c + 1) * 32, :]
            - correction[plane][c * 32 : (c + 1) * 32]
            for c in range(6)
        ]
        phases = every_fourth(phase_ref, 0, plane)
        flags = every_fourth(flag_ref, 256, plane)
        stress, trial, softening, weight = material(elastic, phases, flags)
        for c in range(6):
            collect(c, stress[c])
        collect(6, softening)
        at = 7
        for a in range(6):
            scaled = weight * trial[a]
            for b in range(a, 6):
                collect(at, scaled * trial[b])
                at += 1
    row = lax.broadcasted_iota(jnp.int32, (8, 128), 0)
    groups = [jnp.zeros((8, 128), jnp.float32)] * 16
    totals = [jnp.sum(value, axis=0, keepdims=True) for value in sums]

    def place(at, value):
        here = jnp.broadcast_to(value, (8, 128))
        groups[at // 8] = jnp.where(row == at % 8, here, groups[at // 8])

    for c in range(7):
        place(c, totals[c])
    at = 7
    for a in range(6):
        for b in range(a, 6):
            place(OUTER_AT + 6 * a + b, totals[at])
            if a != b:
                place(OUTER_AT + 6 * b + a, totals[at])
            at += 1
    lines = jnp.concatenate(groups, axis=0)
    ones = jnp.ones((SLABS, 128), jnp.float32)
    line = lax.dot_general(
        ones, lines, (((1,), (1,)), ((), ())),
        precision=lax.Precision.HIGHEST, preferred_element_type=jnp.float32,
    )
    out_ref[...] = line.reshape(SLABS, 1, 128)


def column_kernel(turn, in_ref, columns, back_columns, twist_ref, four, back_four, out_ref):
    pairs = []
    for c in range(FIELDS):
        block = in_ref[:, c * 8 : (c + 1) * 8, :]
        if turn:
            block = jnp.concatenate([block[16 - turn :], block[: 16 - turn]], axis=0)
        pairs.append(split(block.reshape(128, 128)))
    mixed = from_left_values(columns, pairs)
    cosine, sine = twist_ref[0], twist_ref[1]

    def turn(values, table_ref):
        high, low = split(jnp.concatenate(values, axis=0))
        return mm(high, table_ref[...]) + mm(low, table_ref[...])

    values = []
    for c in range(FIELDS):
        lanes = slice(c * 128, (c + 1) * 128)
        real, imag = mixed[:64, lanes], mixed[64:, lanes]
        turned = (real * cosine + imag * sine, imag * cosine - real * sine)
        values.append(jnp.concatenate(turned, axis=1))
    spectrum = turn(values, four)
    xx, xy, xz, y, z = (spectrum[c * 64 : (c + 1) * 64] for c in range(FIELDS))

    shape = (64, 128)
    row = lax.broadcasted_iota(jnp.int32, shape, 0)
    lane = lax.broadcasted_iota(jnp.int32, shape, 1)
    kx = 16 * lax.shift_right_logical(lane, 5) + lax.shift_right_logical(row, 2)
    ky = 4 * lax.axis_index("slab") + lax.bitwise_and(row, 3)
    kz = lax.bitwise_and(lane, 31)
    half = GRID // 2
    keep = (kx != half) & (ky != half) & (kx + ky + kz > 0)
    xi = [
        jnp.where(kx < half, kx, kx - GRID).astype(jnp.float32),
        jnp.where(ky < half, ky, ky - GRID).astype(jnp.float32),
        kz.astype(jnp.float32),
    ]
    length = xi[0] * xi[0] + xi[1] * xi[1] + xi[2] * xi[2]
    inverse = jnp.where(keep, 1.0 / jnp.maximum(length, 1.0), 0.0)
    coupling = (REFERENCE_LAME + REFERENCE_SHEAR) / (
        REFERENCE_SHEAR * (REFERENCE_LAME + 2.0 * REFERENCE_SHEAR)
    )
    xi = [jnp.concatenate([value, value], axis=1) for value in xi]
    inverse = jnp.concatenate([inverse, inverse], axis=1)
    scaled = inverse * (1.0 / (2.0 * REFERENCE_SHEAR))
    traction = [xi[0] * xx + xi[1] * xy + xi[2] * xz, xi[0] * xy + y, xi[0] * xz + z]
    load = xi[0] * traction[0] + xi[1] * traction[1] + xi[2] * traction[2]
    load = load * (inverse * (REFERENCE_SHEAR * coupling))
    field = [scaled * (traction[i] - xi[i] * load) for i in range(3)]
    values = [
        2.0 * (xi[0] * field[0]),
        xi[0] * field[1] + xi[1] * field[0],
        xi[0] * field[2] + xi[2] * field[0],
        field[1],
        field[2],
    ]
    turned = turn(values, back_four)
    for c in range(FIELDS):
        real, imag = turned[c * 64 : (c + 1) * 64, :128], turned[c * 64 : (c + 1) * 64, 128:]
        first, second = real * cosine - imag * sine, real * sine + imag * cosine
        pairs[c] = split(jnp.concatenate([first, second], axis=0))
    result = from_left_values(back_columns, pairs)
    for c in range(FIELDS):
        out_ref[:, c * 8 : (c + 1) * 8, :] = result[:, c * 128 : (c + 1) * 128].reshape(16, 8, 128)


def totals_kernel(in_ref, all_ref):
    line = jnp.sum(in_ref[...].reshape(SLABS, 128), axis=0, keepdims=True)
    all_ref[...] = jnp.broadcast_to(line[None], all_ref.shape)


def own_outputs(line, stress_ref, tangent_ref):
    stress_ref[...] = line[:, :6]
    at = lax.broadcasted_iota(jnp.int32, (1, 128), 1) - OUTER_AT
    a = at // 6
    b = at - 6 * a
    both = (a < 3) & (b < 3)
    shear = jnp.broadcast_to(line[:, 6:7], (1, 128)) * (2.0 * SHEAR_MODULUS)
    fixed = jnp.where(both, BULK_MODULUS - shear * (1.0 / 3.0), 0.0)
    fixed = fixed + jnp.where(a == b, shear, 0.0)
    whole = (fixed - line * jnp.where(b < 3, 1.0, 2.0)) * (1.0 / TANGENT_UNIT)
    for i in range(6):
        tangent_ref[i] = whole[:, OUTER_AT + 6 * i : OUTER_AT + 6 * i + 6]


def assembly_kernel(
    points, basis_ref, turned_ref, in_ref, stress_ref, tangent_ref, stiffness_ref, forces_ref
):
    start = first_of(points)
    own = lax.rem(lax.axis_index("rve") + points - start, points)
    own_outputs(in_ref[own] * (1.0 / VOXELS), stress_ref, tangent_ref)
    shape = (points, 128)
    sums = in_ref[...].reshape(points, 128) * (1.0 / VOXELS)
    sums = jnp.concatenate([sums[points - start :], sums[: points - start]], axis=0)
    basis = [basis_ref[a * points : (a + 1) * points, :] for a in range(6)]
    mean_shear = 2.0 * SHEAR_MODULUS * sums[:, 6:7]

    def column(at):
        return jnp.broadcast_to(sums[:, at : at + 1], shape)

    mean_shear = jnp.broadcast_to(mean_shear, shape)
    on_diagonal = BULK_MODULUS + mean_shear * (2.0 / 3.0)
    off_diagonal = BULK_MODULUS - mean_shear * (1.0 / 3.0)
    answers = []
    force = jnp.zeros(shape, jnp.float32)
    scale = QUADRATURE_WEIGHT / TANGENT_UNIT
    for a in range(6):
        total = jnp.zeros(shape, jnp.float32)
        for b in range(6):
            low, high = min(a, b), max(a, b)
            entry = -PAIR_WEIGHTS[b] * column(OUTER_AT + 6 * low + high)
            if a == b:
                entry = entry + (on_diagonal if a < 3 else mean_shear)
            elif a < 3 and b < 3:
                entry = entry + off_diagonal
            total = total + entry * basis[b]
        answers.append(total * (PAIR_WEIGHTS[a] * scale))
        force = force + basis[a] * (column(a) * (PAIR_WEIGHTS[a] * QUADRATURE_WEIGHT))
    high, low = split(jnp.concatenate(answers, axis=0))
    left_high, left_low = turned_ref[0], turned_ref[1]
    whole = mm(left_high, high) + (mm(left_low, high) + mm(left_high, low))
    stiffness_ref[...] = whole[:60, :60]
    line = jnp.sum(force, axis=0, keepdims=True)
    part8 = lax.broadcasted_iota(jnp.int32, (8, 128), 0)
    lane8 = lax.broadcasted_iota(jnp.int32, (8, 128), 1)
    spread = jnp.where(lane8 % 3 == part8, jnp.broadcast_to(line, (8, 128)), 0.0)
    pick_row = lax.broadcasted_iota(jnp.int32, (128, 128), 0)
    pick_col = lax.broadcasted_iota(jnp.int32, (128, 128), 1)
    pick = (pick_row // 3 == pick_col).astype(jnp.float32)
    forces = jnp.dot(
        spread, pick, precision=lax.Precision.HIGHEST, preferred_element_type=jnp.float32
    )
    forces_ref[...] = forces[:3, :20]


VMEM = pl.BlockSpec(memory_space=pltpu.VMEM)
HBM = pl.BlockSpec(memory_space=pltpu.HBM)
BF16 = jnp.bfloat16
F32 = jnp.float32
LIMIT = 16 * 1024 * 1024


def params():
    return pltpu.CompilerParams(vmem_limit_bytes=LIMIT)


def cost(flops, size):
    return pl.CostEstimate(flops=flops, bytes_accessed=size, transcendentals=0)


def first_of(points):
    return points // 2 + 1 if points > 1 else 0


def exchange(array, turn=0):
    groups = [[(d + turn) % SLABS for d in range(SLABS)]] if turn else None
    return lax.all_to_all(
        array, "slab", split_axis=0, concat_axis=0, tiled=True, axis_index_groups=groups
    )


def on_device(phase_ids, yield_flags, plastic_strain, displacements, connectivity):
    points = lax.axis_size("rve")

    def rows(array):
        lead = math.prod(array.shape[:-2])
        array = array.reshape(lead, PLANES, 32, 128)
        return jnp.transpose(array, (0, 2, 1, 3)).reshape(lead * 128, 128)

    phases = rows(phase_ids)
    flags = rows(yield_flags)
    plastic = rows(plastic_strain)

    there, back = depth_tables()
    depth, back_depth = (
        jnp.asarray(np.stack([right_table(np.roll(t, 32 * l, axis)) for l in range(PLANES)]))
        for t, axis in ((there, 1), (back, 0))
    )
    there, back = row_tables()
    line, back_line = jnp.asarray(left_table(there)), jnp.asarray(left_table(back))
    there, back, twist, four, back_four = column_tables()
    column, back_column = jnp.asarray(left_table(there)), jnp.asarray(left_table(back))
    twist = jnp.asarray(twist)
    four = jnp.asarray(four.astype(ml_dtypes.bfloat16))
    back_four = jnp.asarray(back_four.astype(ml_dtypes.bfloat16))

    block = jax.ShapeDtypeStruct((16, 8 * FIELDS, 128), F32)

    first = pl.pallas_call(
        functools.partial(first_kernel, points),
        out_shape=(
            block, jax.ShapeDtypeStruct((8, 128), F32),
            jax.ShapeDtypeStruct((6 * points, 128), F32),
            jax.ShapeDtypeStruct((2, 128, 6 * points), BF16),
        ),
        in_specs=[HBM] * 7, out_specs=(VMEM,) * 4,
        scratch_shapes=[
            pltpu.SMEM(connectivity.shape, jnp.int32), pltpu.SMEM(displacements.shape[::-1], F32),
            pltpu.VMEM((128, 128), jnp.int32), pltpu.VMEM((128, 128), jnp.int32),
            pltpu.VMEM((768, 128), F32), pltpu.VMEM((PLANES, 256, 256), BF16),
            pltpu.VMEM((256, 256), BF16),
            pltpu.SemaphoreType.DMA((7,)),
        ],
        compiler_params=params(), cost_estimate=cost(400_000_000, 2_000_000), name="first",
    )
    def columns(turn):
        return pl.pallas_call(
            functools.partial(column_kernel, turn), out_shape=block,
            in_specs=[VMEM] * 6, out_specs=VMEM, compiler_params=params(),
            cost_estimate=cost(400_000_000, 2_000_000), name="columns",
        )

    middle = pl.pallas_call(
        middle_kernel, out_shape=(block, jax.ShapeDtypeStruct((768, 128), F32)),
        in_specs=[VMEM] * 9, out_specs=(VMEM, VMEM),
        compiler_params=params(),
        cost_estimate=cost(800_000_000, 4_000_000), name="middle",
    )
    last = pl.pallas_call(
        last_kernel, out_shape=jax.ShapeDtypeStruct((SLABS, 1, 128), F32),
        in_specs=[VMEM] * 6, out_specs=VMEM,
        compiler_params=params(),
        cost_estimate=cost(400_000_000, 2_000_000), name="last",
    )
    totals = pl.pallas_call(
        totals_kernel, out_shape=jax.ShapeDtypeStruct((points, 1, 128), F32),
        in_specs=[VMEM], out_specs=VMEM, compiler_params=params(),
        cost_estimate=cost(10_000, 50_000), name="totals",
    )
    assembly = pl.pallas_call(
        functools.partial(assembly_kernel, points),
        out_shape=(
            jax.ShapeDtypeStruct((1, 6), F32), jax.ShapeDtypeStruct((6, 1, 6), F32),
            jax.ShapeDtypeStruct((60, 60), F32), jax.ShapeDtypeStruct((3, 20), F32),
        ),
        in_specs=[VMEM] * 3, out_specs=(VMEM,) * 4, compiler_params=params(),
        cost_estimate=cost(10_000_000, 200_000), name="assembly",
    )

    def apply_columns(array, turn):
        return exchange(
            columns(turn)(exchange(array, turn), column, back_column, twist, four, back_four)
        )

    operands = (connectivity, displacements.T, phases, flags, plastic, depth, line)
    spectrum, macro, basis, turned_basis = first(
        *(pltpu.with_memory_space_constraint(operand, pltpu.HBM) for operand in operands)
    )
    planes = apply_columns(spectrum, FAR)
    spectrum, elastic = middle(
        macro, phases, flags, plastic, planes, back_depth, back_line, depth, line
    )
    planes = apply_columns(spectrum, FAR)
    partial = last(phases, flags, elastic, planes, back_depth, back_line)
    everyone = totals(exchange(partial, FAR))
    turned = [(g + first_of(points)) % points for g in range(points)]
    everyone = lax.all_to_all(
        everyone, "rve", 0, 0, tiled=True, axis_index_groups=[turned]
    )
    stress, tangent, stiffness, forces = assembly(basis, turned_basis, everyone)
    return (stress, jnp.transpose(tangent, (1, 0, 2)), forces.T, stiffness)


def solution(mesh):
    return jax.shard_map(
        on_device,
        mesh=mesh,
        in_specs=(
            P("slab", None),
            P("rve", None, "slab", None),
            P("rve", None, "slab", None),
            P(),
            P(),
        ),
        out_specs=(P("rve", None), P("rve", None, None), P(), P()),
        check_vma=False,
    )
```

```python
import functools
import math

import jax
import jax.numpy as jnp
import ml_dtypes
import numpy as np
from jax import lax
from jax.experimental import pallas as pl
from jax.experimental.pallas import tpu as pltpu
from jax.sharding import PartitionSpec as P

GRID = 64
ITERS = 2
SLABS = 16
PLANES = GRID // SLABS
KEPT = GRID // 2

SHEAR_MODULUS = 80.0
BULK_MODULUS = 160.0
REFERENCE_SHEAR = 80.0
REFERENCE_LAME = 160.0 - 160.0 / 3.0
TANGENT_UNIT = 100.0
QUADRATURE_WEIGHT = 0.125
PAIR_WEIGHTS = (1.0, 1.0, 1.0, 2.0, 2.0, 2.0)
TENSOR_PAIRS = ((0, 0), (1, 1), (2, 2), (1, 2), (0, 2), (0, 1))
VOXELS = float(GRID**3)
GAUSS_LOW = 0.5 - 0.5 / math.sqrt(3.0)
GAUSS_HIGH = 0.5 + 0.5 / math.sqrt(3.0)
OUTER_AT = 8
FIELDS = 5
FAR = 10


def halves(table):
    high = table.astype(np.float32).astype(ml_dtypes.bfloat16)
    low = (table - high.astype(np.float64)).astype(np.float32).astype(ml_dtypes.bfloat16)
    return high, low


def depth_tables():
    z = np.arange(GRID)
    k = np.arange(KEPT)
    theta = 2.0 * np.pi * np.outer(z, k) / GRID
    forward = np.stack([np.cos(theta), -np.sin(theta)], axis=0)
    weight = np.where(k == 0, 1.0, 2.0) / VOXELS
    inverse = forward * weight[None, None, :]
    pair = np.eye(2)
    there = np.einsum("rR,pzk->rzRpk", pair, forward)
    back = np.einsum("rR,pzk->Rpkrz", pair, inverse)
    return there.reshape(128, 128), back.reshape(128, 128)


def row_tables():
    y = 2 * np.arange(32)[None, :] + np.arange(2)[:, None]
    ky = 4 * np.arange(16)[:, None] + np.arange(4)[None, :]
    theta = 2.0 * np.pi * np.einsum("de,rm->derm", ky, y) / GRID
    c, s = np.cos(theta), np.sin(theta)
    there = np.zeros((16, 2, 4, 2, 2, 32))
    there[:, 0, :, :, 0, :] = c
    there[:, 0, :, :, 1, :] = s
    there[:, 1, :, :, 0, :] = -s
    there[:, 1, :, :, 1, :] = c
    back = np.zeros((2, 2, 32, 16, 2, 4))
    ct, st = np.einsum("derm->rmde", c), np.einsum("derm->rmde", s)
    back[:, 0, :, :, 0, :] = ct
    back[:, 0, :, :, 1, :] = -st
    back[:, 1, :, :, 0, :] = st
    back[:, 1, :, :, 1, :] = ct
    return there.reshape(128, 128), back.reshape(128, 128)


def column_tables():
    d = np.arange(16)
    theta = 2.0 * np.pi * np.outer(d, d) / 16.0
    c, s = np.cos(theta), np.sin(theta)
    same = np.eye(4)
    there = np.zeros((2, 16, 4, 16, 2, 4))
    there[0, :, :, :, 0, :] = np.einsum("bd,ef->bedf", c, same)
    there[0, :, :, :, 1, :] = np.einsum("bd,ef->bedf", s, same)
    there[1, :, :, :, 0, :] = np.einsum("bd,ef->bedf", -s, same)
    there[1, :, :, :, 1, :] = np.einsum("bd,ef->bedf", c, same)
    there = there.reshape(128, 128)
    phi = 2.0 * np.pi * np.outer(np.arange(16), np.arange(4)) / GRID
    twist = np.stack([np.cos(phi), np.sin(phi)])[:, :, None, :, None]
    twist = np.broadcast_to(twist, (2, 16, 4, 4, KEPT)).reshape(2, 64, 128)
    quarter = 2.0 * np.pi * np.outer(np.arange(4), np.arange(4)) / 4.0
    cq, sq = np.rint(np.cos(quarter)), np.rint(np.sin(quarter))
    kept = np.eye(KEPT)
    four = np.zeros((2, 4, KEPT, 2, 4, KEPT))
    four[0, :, :, 0] = np.einsum("la,kK->lkaK", cq, kept)
    four[1, :, :, 0] = np.einsum("la,kK->lkaK", sq, kept)
    four[0, :, :, 1] = np.einsum("la,kK->lkaK", -sq, kept)
    four[1, :, :, 1] = np.einsum("la,kK->lkaK", cq, kept)
    four = four.reshape(256, 256)
    return there, there.T.copy(), twist.astype(np.float32), four, four.T.copy()


def right_table(table):
    high, low = halves(table)
    return np.block([[high, low], [high, np.zeros_like(low)]])


def left_table(table):
    return np.ascontiguousarray(right_table(table.T).T)


def split(x):
    high = x.astype(jnp.bfloat16)
    low = (x - high.astype(jnp.float32)).astype(jnp.bfloat16)
    return high, low


def mm(a, b):
    return jnp.dot(a, b, preferred_element_type=jnp.float32)


def from_left_values(table_ref, pairs):
    both = jnp.concatenate([jnp.concatenate(pair, axis=0) for pair in pairs], axis=1)
    total = mm(table_ref[:128, :], both)
    return total + mm(table_ref[128:, :128], both[:128])


def from_left_halves(table_ref, pairs):
    both = jnp.concatenate([jnp.concatenate(pair, axis=0) for pair in pairs], axis=1)
    both = mm(table_ref[...], both)
    return both[:128] + both[128:]


def from_right(tiles, table_ref):
    results = []
    for l, tile in enumerate(tiles):
        both = mm(jnp.concatenate(split(tile), axis=1), table_ref[l])
        results.append(both[:, :128] + both[:, 128:])
    return results


def gather_chunks(tiles):
    lane = lax.broadcasted_iota(jnp.int32, tiles[0].shape, 1)
    odd = lax.bitwise_and(lane, 32) != 0
    upper = lax.bitwise_and(lane, 64) != 0
    tiles = [jnp.where(odd, tiles[(j + 1) % 4], tiles[j]) for j in range(4)]
    tiles = [jnp.where(upper, tiles[(j + 2) % 4], tiles[j]) for j in range(4)]
    return [tiles[-k % 4] for k in range(4)]


def roll_chunks(tile, count):
    return pltpu.roll(tile, 32 * (count % 4), 1) if count % 4 else tile


def slopes_of(bits, low, high):
    at = [jnp.where(bit == 1, high, low) for bit in bits]
    far = [jnp.where(bit == 1, low, high) for bit in bits]

    def slope(corner, axis):
        value = None
        for other in range(3):
            if other != axis:
                factor = at[other] if corner >> other & 1 else far[other]
                value = factor if value is None else value * factor
        return value if corner >> axis & 1 else -value

    return slope


def point_slopes(point):
    low, high = jnp.float32(GAUSS_LOW), jnp.float32(GAUSS_HIGH)
    bits = [lax.bitwise_and(lax.shift_right_logical(point, d), 1) for d in range(3)]
    slope = slopes_of(bits, low, high)
    return [[slope(corner, d) for d in range(3)] for corner in range(8)]


def macro_strain(point, slopes, conn_ref, disp_ref):
    element = lax.shift_right_logical(point, 3)
    grad = [[jnp.float32(0.0)] * 3 for _ in range(3)]
    for corner in range(8):
        node = conn_ref[element, corner]
        for k in range(3):
            u = disp_ref[k, node]
            for d in range(3):
                grad[k][d] = grad[k][d] + slopes[corner][d] * u
    strain = []
    for i, j in TENSOR_PAIRS:
        strain.append(grad[i][i] if i == j else 0.5 * (grad[i][j] + grad[j][i]))
    return strain


def material(elastic, phases, flags):
    hard = phases == 1
    limit = jnp.where(hard, 1.2, 0.3)
    ratio = jnp.where(
        hard,
        3.0 * SHEAR_MODULUS / (3.0 * SHEAR_MODULUS + 10.0),
        3.0 * SHEAR_MODULUS / (3.0 * SHEAR_MODULUS + 2.0),
    )
    active = flags.astype(jnp.float32)
    volume = elastic[0] + elastic[1] + elastic[2]
    third = volume * (1.0 / 3.0)
    trial = [2.0 * SHEAR_MODULUS * (elastic[a] - third) for a in range(3)]
    trial += [2.0 * SHEAR_MODULUS * elastic[a] for a in range(3, 6)]
    normal = trial[0] * trial[0] + trial[1] * trial[1] + trial[2] * trial[2]
    shear = trial[3] * trial[3] + trial[4] * trial[4] + trial[5] * trial[5]
    equivalent = jnp.sqrt(1.5 * (normal + 2.0 * shear))
    bounded = jnp.maximum(equivalent, limit)
    inverse = 1.0 / bounded
    scaled = ratio * active
    softening = 1.0 - scaled * (equivalent - limit) * inverse
    pressure = BULK_MODULUS * volume
    stress = [trial[a] * softening + pressure for a in range(3)]
    stress += [trial[a] * softening for a in range(3, 6)]
    weight = 3.0 * SHEAR_MODULUS * scaled * limit * (inverse * inverse * inverse)
    return stress, trial, softening, weight


def every_fourth(ref, start, plane):
    return ref[pl.ds(start + plane, 32, stride=4), :]


def plane_waves():
    row = lax.broadcasted_iota(jnp.int32, (8, 128), 0)
    lane = lax.broadcasted_iota(jnp.int32, (8, 128), 1)
    inner = lax.bitwise_and(row, 3).astype(jnp.float32)
    depth = lax.bitwise_and(lane, 31).astype(jnp.float32)
    starts = [4.0 * d if d < 8 else 4.0 * d - GRID for d in range(16)]
    wave_y = jnp.concatenate([inner + start for start in starts], axis=0)
    return wave_y, jnp.concatenate([depth] * 16, axis=0)


def forward_planes(stresses, depth, rows, out_ref, turn=0):
    tiles = gather_chunks(from_right(stresses, depth))
    tiles = [roll_chunks(tile, -s) for s, tile in enumerate(tiles)]
    pairs = [
        split(jnp.concatenate([tile[c * 32 : (c + 1) * 32] for tile in tiles], axis=0))
        for c in range(6)
    ]
    spectrum = from_left_halves(rows, pairs)
    xx, yy, zz, yz, xz, xy = (spectrum[:, c * 128 : (c + 1) * 128] for c in range(6))
    wave_y, wave_z = plane_waves()
    fields = (xx, xy, xz, wave_y * yy + wave_z * yz, wave_y * yz + wave_z * zz)
    for c, field in enumerate(fields):
        block = field.reshape(16, 8, 128)
        out_ref[: 16 - turn, c * 8 : (c + 1) * 8, :] = block[turn:]
        if turn:
            out_ref[16 - turn :, c * 8 : (c + 1) * 8, :] = block[:turn]


def backward_planes(in_ref, depth, rows):
    xx, xy, xz, y, z = (
        in_ref[:, c * 8 : (c + 1) * 8, :].reshape(128, 128) for c in range(FIELDS)
    )
    wave_y, wave_z = plane_waves()
    yy, zz = 2.0 * (wave_y * y), 2.0 * (wave_z * z)
    pairs = [split(value) for value in (xx, yy, zz, wave_y * z + wave_z * y, xz, xy)]
    lines = from_left_values(rows, pairs)
    tiles = [
        jnp.concatenate(
            [lines[s * 32 : (s + 1) * 32, c * 128 : (c + 1) * 128] for c in range(6)], axis=0
        )
        for s in range(4)
    ]
    tiles = [roll_chunks(tile, s) for s, tile in enumerate(tiles)]
    return from_right(gather_chunks(tiles), depth)


def basis_of(points, conn_ref):
    shape = (points, 128)
    lane = lax.broadcasted_iota(jnp.int32, shape, 1)
    point = lax.broadcasted_iota(jnp.int32, shape, 0)
    element = lax.shift_right_logical(point, 3)
    bits = [lax.bitwise_and(lax.shift_right_logical(point, d), 1) for d in range(3)]
    slope = slopes_of(bits, GAUSS_LOW, GAUSS_HIGH)
    node = lane // 3
    part = lane - 3 * node
    elements = conn_ref.shape[0]
    grad = [jnp.zeros(shape, jnp.float32) for _ in range(3)]
    for corner in range(8):
        owner = jnp.full(shape, conn_ref[0, corner], jnp.int32)
        for e in range(1, elements):
            owner = jnp.where(element == e, conn_ref[e, corner], owner)
        here = (owner == node) & (lane < 60)
        for d in range(3):
            grad[d] = grad[d] + jnp.where(here, slope(corner, d), 0.0)
    basis = []
    for i, k in TENSOR_PAIRS:
        if i == k:
            basis.append(jnp.where(part == i, grad[i], 0.0))
        else:
            value = jnp.where(part == i, 0.5 * grad[k], 0.0)
            basis.append(value + jnp.where(part == k, 0.5 * grad[i], 0.0))
    return jnp.concatenate(basis, axis=0)


def first_kernel(
    points, conn_hbm, disp_hbm, phase_hbm, flag_hbm, plastic_hbm, depth_hbm, rows_hbm,
    out_ref, macro_ref, basis_ref, turned_ref,
    conn_ref, disp_ref, phase_ref, flag_ref, plastic_ref, depth, rows, sems,
):
    pairs = (
        (conn_hbm, conn_ref), (disp_hbm, disp_ref), (plastic_hbm, plastic_ref),
        (phase_hbm, phase_ref), (flag_hbm.at[pl.ds(0, 128)], flag_ref),
        (depth_hbm, depth), (rows_hbm, rows),
    )
    copies = [pltpu.make_async_copy(a, b, sems.at[i]) for i, (a, b) in enumerate(pairs)]
    for copy in copies:
        copy.start()
    point = lax.axis_index("rve")
    slopes = point_slopes(point)
    for copy in copies[:2]:
        copy.wait()
    macro = macro_strain(point, slopes, conn_ref, disp_ref)
    row = lax.broadcasted_iota(jnp.int32, (8, 128), 0)
    table = jnp.zeros((8, 128), jnp.float32)
    for c in range(6):
        table = jnp.where(row == c, macro[c], table)
    macro_ref[...] = table
    for copy in copies[2:5]:
        copy.wait()
    stresses = []
    for plane in range(PLANES):
        elastic = [macro[c] - every_fourth(plastic_ref, c * 128, plane) for c in range(6)]
        phases = every_fourth(phase_ref, 0, plane)
        flags = every_fourth(flag_ref, 0, plane)
        stress = material(elastic, phases, flags)[0]
        stresses.append(jnp.concatenate(stress, axis=0))
    for copy in copies[5:]:
        copy.wait()
    basis = basis_of(points, conn_ref)
    basis_ref[...] = basis
    high, low = split(jnp.transpose(basis))
    turned_ref[0] = high
    turned_ref[1] = low
    forward_planes(stresses, depth, rows, out_ref, FAR)


def middle_kernel(
    macro_ref, phase_ref, flag_ref, plastic_ref, in_ref, back_depth, back_rows, depth, rows,
    out_ref, elastic_ref,
):
    macro = [macro_ref[c : c + 1, :] for c in range(6)]
    correction = backward_planes(in_ref, back_depth, back_rows)
    stresses = []
    for plane in range(PLANES):
        elastic = []
        for c in range(6):
            at = plane * 192 + c * 32
            before = macro[c] - every_fourth(plastic_ref, c * 128, plane)
            after = before - correction[plane][c * 32 : (c + 1) * 32]
            elastic_ref[at : at + 32, :] = after
            elastic.append(after)
        phases = every_fourth(phase_ref, 0, plane)
        flags = every_fourth(flag_ref, 128, plane)
        stress = material(elastic, phases, flags)[0]
        stresses.append(jnp.concatenate(stress, axis=0))
    forward_planes(stresses, depth, rows, out_ref)


def last_kernel(
    phase_ref, flag_ref, elastic_ref, in_ref, back_depth, back_rows, out_ref
):
    correction = backward_planes(in_ref, back_depth, back_rows)
    sums = [None] * 28

    def collect(at, value):
        part = value.reshape(4, 8, 128)
        part = (part[0] + part[1]) + (part[2] + part[3])
        sums[at] = part if sums[at] is None else sums[at] + part

    for plane in range(PLANES):
        elastic = [
            elastic_ref[plane * 192 + c * 32 : plane * 192 + (c + 1) * 32, :]
            - correction[plane][c * 32 : (c + 1) * 32]
            for c in range(6)
        ]
        phases = every_fourth(phase_ref, 0, plane)
        flags = every_fourth(flag_ref, 256, plane)
        stress, trial, softening, weight = material(elastic, phases, flags)
        for c in range(6):
            collect(c, stress[c])
        collect(6, softening)
        at = 7
        for a in range(6):
            scaled = weight * trial[a]
            for b in range(a, 6):
                collect(at, scaled * trial[b])
                at += 1
    row = lax.broadcasted_iota(jnp.int32, (8, 128), 0)
    groups = [jnp.zeros((8, 128), jnp.float32)] * 16
    totals = [jnp.sum(value, axis=0, keepdims=True) for value in sums]

    def place(at, value):
        here = jnp.broadcast_to(value, (8, 128))
        groups[at // 8] = jnp.where(row == at % 8, here, groups[at // 8])

    for c in range(7):
        place(c, totals[c])
    at = 7
    for a in range(6):
        for b in range(a, 6):
            place(OUTER_AT + 6 * a + b, totals[at])
            if a != b:
                place(OUTER_AT + 6 * b + a, totals[at])
            at += 1
    lines = jnp.concatenate(groups, axis=0)
    ones = jnp.ones((SLABS, 128), jnp.float32)
    line = lax.dot_general(
        ones, lines, (((1,), (1,)), ((), ())),
        precision=lax.Precision.HIGHEST, preferred_element_type=jnp.float32,
    )
    out_ref[...] = line.reshape(SLABS, 1, 128)


def column_kernel(turn, in_ref, columns, back_columns, twist_ref, four, back_four, out_ref):
    pairs = []
    for c in range(FIELDS):
        block = in_ref[:, c * 8 : (c + 1) * 8, :]
        if turn:
            block = jnp.concatenate([block[16 - turn :], block[: 16 - turn]], axis=0)
        pairs.append(split(block.reshape(128, 128)))
    mixed = from_left_values(columns, pairs)
    cosine, sine = twist_ref[0], twist_ref[1]

    def turn(values, table_ref):
        high, low = split(jnp.concatenate(values, axis=0))
        return mm(high, table_ref[...]) + mm(low, table_ref[...])

    values = []
    for c in range(FIELDS):
        lanes = slice(c * 128, (c + 1) * 128)
        real, imag = mixed[:64, lanes], mixed[64:, lanes]
        turned = (real * cosine + imag * sine, imag * cosine - real * sine)
        values.append(jnp.concatenate(turned, axis=1))
    spectrum = turn(values, four)
    xx, xy, xz, y, z = (spectrum[c * 64 : (c + 1) * 64] for c in range(FIELDS))

    shape = (64, 128)
    row = lax.broadcasted_iota(jnp.int32, shape, 0)
    lane = lax.broadcasted_iota(jnp.int32, shape, 1)
    kx = 16 * lax.shift_right_logical(lane, 5) + lax.shift_right_logical(row, 2)
    ky = 4 * lax.axis_index("slab") + lax.bitwise_and(row, 3)
    kz = lax.bitwise_and(lane, 31)
    half = GRID // 2
    keep = (kx != half) & (ky != half) & (kx + ky + kz > 0)
    xi = [
        jnp.where(kx < half, kx, kx - GRID).astype(jnp.float32),
        jnp.where(ky < half, ky, ky - GRID).astype(jnp.float32),
        kz.astype(jnp.float32),
    ]
    length = xi[0] * xi[0] + xi[1] * xi[1] + xi[2] * xi[2]
    inverse = jnp.where(keep, 1.0 / jnp.maximum(length, 1.0), 0.0)
    coupling = (REFERENCE_LAME + REFERENCE_SHEAR) / (
        REFERENCE_SHEAR * (REFERENCE_LAME + 2.0 * REFERENCE_SHEAR)
    )
    xi = [jnp.concatenate([value, value], axis=1) for value in xi]
    inverse = jnp.concatenate([inverse, inverse], axis=1)
    scaled = inverse * (1.0 / (2.0 * REFERENCE_SHEAR))
    traction = [xi[0] * xx + xi[1] * xy + xi[2] * xz, xi[0] * xy + y, xi[0] * xz + z]
    load = xi[0] * traction[0] + xi[1] * traction[1] + xi[2] * traction[2]
    load = load * (inverse * (REFERENCE_SHEAR * coupling))
    field = [scaled * (traction[i] - xi[i] * load) for i in range(3)]
    values = [
        2.0 * (xi[0] * field[0]),
        xi[0] * field[1] + xi[1] * field[0],
        xi[0] * field[2] + xi[2] * field[0],
        field[1],
        field[2],
    ]
    turned = turn(values, back_four)
    for c in range(FIELDS):
        real, imag = turned[c * 64 : (c + 1) * 64, :128], turned[c * 64 : (c + 1) * 64, 128:]
        first, second = real * cosine - imag * sine, real * sine + imag * cosine
        pairs[c] = split(jnp.concatenate([first, second], axis=0))
    result = from_left_values(back_columns, pairs)
    for c in range(FIELDS):
        out_ref[:, c * 8 : (c + 1) * 8, :] = result[:, c * 128 : (c + 1) * 128].reshape(16, 8, 128)


def totals_kernel(in_ref, all_ref):
    line = jnp.sum(in_ref[...].reshape(SLABS, 128), axis=0, keepdims=True)
    all_ref[...] = jnp.broadcast_to(line[None], all_ref.shape)


def own_outputs(line, stress_ref, tangent_ref):
    stress_ref[...] = line[:, :6]
    at = lax.broadcasted_iota(jnp.int32, (1, 128), 1) - OUTER_AT
    a = at // 6
    b = at - 6 * a
    both = (a < 3) & (b < 3)
    shear = jnp.broadcast_to(line[:, 6:7], (1, 128)) * (2.0 * SHEAR_MODULUS)
    fixed = jnp.where(both, BULK_MODULUS - shear * (1.0 / 3.0), 0.0)
    fixed = fixed + jnp.where(a == b, shear, 0.0)
    whole = (fixed - line * jnp.where(b < 3, 1.0, 2.0)) * (1.0 / TANGENT_UNIT)
    for i in range(6):
        tangent_ref[i] = whole[:, OUTER_AT + 6 * i : OUTER_AT + 6 * i + 6]


def assembly_kernel(
    points, basis_ref, turned_ref, in_ref, stress_ref, tangent_ref, stiffness_ref, forces_ref
):
    start = first_of(points)
    own = lax.rem(lax.axis_index("rve") + points - start, points)
    own_outputs(in_ref[own] * (1.0 / VOXELS), stress_ref, tangent_ref)
    shape = (points, 128)
    sums = in_ref[...].reshape(points, 128) * (1.0 / VOXELS)
    sums = jnp.concatenate([sums[points - start :], sums[: points - start]], axis=0)
    basis = [basis_ref[a * points : (a + 1) * points, :] for a in range(6)]
    mean_shear = 2.0 * SHEAR_MODULUS * sums[:, 6:7]

    def column(at):
        return jnp.broadcast_to(sums[:, at : at + 1], shape)

    mean_shear = jnp.broadcast_to(mean_shear, shape)
    on_diagonal = BULK_MODULUS + mean_shear * (2.0 / 3.0)
    off_diagonal = BULK_MODULUS - mean_shear * (1.0 / 3.0)
    answers = []
    force = jnp.zeros(shape, jnp.float32)
    scale = QUADRATURE_WEIGHT / TANGENT_UNIT
    for a in range(6):
        total = jnp.zeros(shape, jnp.float32)
        for b in range(6):
            low, high = min(a, b), max(a, b)
            entry = -PAIR_WEIGHTS[b] * column(OUTER_AT + 6 * low + high)
            if a == b:
                entry = entry + (on_diagonal if a < 3 else mean_shear)
            elif a < 3 and b < 3:
                entry = entry + off_diagonal
            total = total + entry * basis[b]
        answers.append(total * (PAIR_WEIGHTS[a] * scale))
        force = force + basis[a] * (column(a) * (PAIR_WEIGHTS[a] * QUADRATURE_WEIGHT))
    high, low = split(jnp.concatenate(answers, axis=0))
    left_high, left_low = turned_ref[0], turned_ref[1]
    whole = mm(left_high, high) + (mm(left_low, high) + mm(left_high, low))
    stiffness_ref[...] = whole[:60, :60]
    line = jnp.sum(force, axis=0, keepdims=True)
    part8 = lax.broadcasted_iota(jnp.int32, (8, 128), 0)
    lane8 = lax.broadcasted_iota(jnp.int32, (8, 128), 1)
    spread = jnp.where(lane8 % 3 == part8, jnp.broadcast_to(line, (8, 128)), 0.0)
    pick_row = lax.broadcasted_iota(jnp.int32, (128, 128), 0)
    pick_col = lax.broadcasted_iota(jnp.int32, (128, 128), 1)
    pick = (pick_row // 3 == pick_col).astype(jnp.float32)
    forces = jnp.dot(
        spread, pick, precision=lax.Precision.HIGHEST, preferred_element_type=jnp.float32
    )
    forces_ref[...] = forces[:3, :20]


VMEM = pl.BlockSpec(memory_space=pltpu.VMEM)
HBM = pl.BlockSpec(memory_space=pltpu.HBM)
BF16 = jnp.bfloat16
F32 = jnp.float32
LIMIT = 16 * 1024 * 1024


def params():
    return pltpu.CompilerParams(vmem_limit_bytes=LIMIT)


def cost(flops, size):
    return pl.CostEstimate(flops=flops, bytes_accessed=size, transcendentals=0)


def first_of(points):
    return points // 2 + 3 if points > 4 else 0


def exchange(array, turn=0):
    groups = [[(d + turn) % SLABS for d in range(SLABS)]] if turn else None
    return lax.all_to_all(
        array, "slab", split_axis=0, concat_axis=0, tiled=True, axis_index_groups=groups
    )


def on_device(phase_ids, yield_flags, plastic_strain, displacements, connectivity):
    points = lax.axis_size("rve")

    def rows(array):
        lead = math.prod(array.shape[:-2])
        array = array.reshape(lead, PLANES, 32, 128)
        return jnp.transpose(array, (0, 2, 1, 3)).reshape(lead * 128, 128)

    phases = rows(phase_ids)
    flags = rows(yield_flags)
    plastic = rows(plastic_strain)

    there, back = depth_tables()
    depth, back_depth = (
        jnp.asarray(np.stack([right_table(np.roll(t, 32 * l, axis)) for l in range(PLANES)]))
        for t, axis in ((there, 1), (back, 0))
    )
    there, back = row_tables()
    line, back_line = jnp.asarray(left_table(there)), jnp.asarray(left_table(back))
    there, back, twist, four, back_four = column_tables()
    column, back_column = jnp.asarray(left_table(there)), jnp.asarray(left_table(back))
    twist = jnp.asarray(twist)
    four = jnp.asarray(four.astype(ml_dtypes.bfloat16))
    back_four = jnp.asarray(back_four.astype(ml_dtypes.bfloat16))

    block = jax.ShapeDtypeStruct((16, 8 * FIELDS, 128), F32)

    first = pl.pallas_call(
        functools.partial(first_kernel, points),
        out_shape=(
            block, jax.ShapeDtypeStruct((8, 128), F32),
            jax.ShapeDtypeStruct((6 * points, 128), F32),
            jax.ShapeDtypeStruct((2, 128, 6 * points), BF16),
        ),
        in_specs=[HBM] * 7, out_specs=(VMEM,) * 4,
        scratch_shapes=[
            pltpu.SMEM(connectivity.shape, jnp.int32), pltpu.SMEM(displacements.shape[::-1], F32),
            pltpu.VMEM((128, 128), jnp.int32), pltpu.VMEM((128, 128), jnp.int32),
            pltpu.VMEM((768, 128), F32), pltpu.VMEM((PLANES, 256, 256), BF16),
            pltpu.VMEM((256, 256), BF16),
            pltpu.SemaphoreType.DMA((7,)),
        ],
        compiler_params=params(), cost_estimate=cost(400_000_000, 2_000_000), name="first",
    )
    def columns(turn):
        return pl.pallas_call(
            functools.partial(column_kernel, turn), out_shape=block,
            in_specs=[VMEM] * 6, out_specs=VMEM, compiler_params=params(),
            cost_estimate=cost(400_000_000, 2_000_000), name="columns",
        )

    middle = pl.pallas_call(
        middle_kernel, out_shape=(block, jax.ShapeDtypeStruct((768, 128), F32)),
        in_specs=[VMEM] * 9, out_specs=(VMEM, VMEM),
        compiler_params=params(),
        cost_estimate=cost(800_000_000, 4_000_000), name="middle",
    )
    last = pl.pallas_call(
        last_kernel, out_shape=jax.ShapeDtypeStruct((SLABS, 1, 128), F32),
        in_specs=[VMEM] * 6, out_specs=VMEM,
        compiler_params=params(),
        cost_estimate=cost(400_000_000, 2_000_000), name="last",
    )
    totals = pl.pallas_call(
        totals_kernel, out_shape=jax.ShapeDtypeStruct((points, 1, 128), F32),
        in_specs=[VMEM], out_specs=VMEM, compiler_params=params(),
        cost_estimate=cost(10_000, 50_000), name="totals",
    )
    assembly = pl.pallas_call(
        functools.partial(assembly_kernel, points),
        out_shape=(
            jax.ShapeDtypeStruct((1, 6), F32), jax.ShapeDtypeStruct((6, 1, 6), F32),
            jax.ShapeDtypeStruct((60, 60), F32), jax.ShapeDtypeStruct((3, 20), F32),
        ),
        in_specs=[VMEM] * 3, out_specs=(VMEM,) * 4, compiler_params=params(),
        cost_estimate=cost(10_000_000, 200_000), name="assembly",
    )

    def apply_columns(array, turn):
        return exchange(
            columns(turn)(exchange(array, turn), column, back_column, twist, four, back_four)
        )

    operands = (connectivity, displacements.T, phases, flags, plastic, depth, line)
    spectrum, macro, basis, turned_basis = first(
        *(pltpu.with_memory_space_constraint(operand, pltpu.HBM) for operand in operands)
    )
    planes = apply_columns(spectrum, FAR)
    spectrum, elastic = middle(
        macro, phases, flags, plastic, planes, back_depth, back_line, depth, line
    )
    planes = apply_columns(spectrum, 0)
    partial = last(phases, flags, elastic, planes, back_depth, back_line)
    everyone = totals(exchange(partial, FAR))
    turned = [(g + first_of(points)) % points for g in range(points)]
    everyone = lax.all_to_all(
        everyone, "rve", 0, 0, tiled=True, axis_index_groups=[turned]
    )
    stress, tangent, stiffness, forces = assembly(basis, turned_basis, everyone)
    return (stress, jnp.transpose(tangent, (1, 0, 2)), forces.T, stiffness)


def solution(mesh):
    return jax.shard_map(
        on_device,
        mesh=mesh,
        in_specs=(
            P("slab", None),
            P("rve", None, "slab", None),
            P("rve", None, "slab", None),
            P(),
            P(),
        ),
        out_specs=(P("rve", None), P("rve", None, None), P(), P()),
        check_vma=False,
    )
```
